32 devices in a mesh: fsdp: 32 (over z, y, x, core).
Axes of the slice: x: 2, y: 2, z: 4, core: 2. Of those that a mesh axis runs over, the one named last changes fastest.
Arguments:
- tokens: bfloat16 [4096, 768], P('fsdp'), may hold values from -6 to 6
- attn_weight: bfloat16 [768, 3072], P(None, 'fsdp')
- w_gate: bfloat16 [768, 3072], P(None, 'fsdp'), may hold values from -0.21875 to 0.21875
- w_up: bfloat16 [768, 3072], P(None, 'fsdp'), may hold values from -0.21875 to 0.21875
- w_down: bfloat16 [3072, 768], P('fsdp'), may hold values from -0.109375 to 0.109375
- norm_gains: float32 [2, 768], replicated, may hold values from 0.5 to 1.5
- bias_table: float32 [32, 12], replicated, may hold values from -4 to 4
- router: float32 [768, 64], replicated, may hold values from -0.4375 to 0.4375
- grad_out: bfloat16 [4096, 768], P('fsdp'), may hold values from -6 to 6
- segment: int32 [4096], P('fsdp'), may hold values from -1 to 7, as said below
- expert_ids: int32 [4096, 2], P('fsdp'), may hold values from 0 to 63, as said below
- bucket_of: int32 [64], replicated, may hold values from 0 to 31, as said below
Outputs:
- result: bfloat16 [4096, 768], P('fsdp')
- grad_tokens: bfloat16 [4096, 768], P('fsdp')
- grad_attn: float32 [768, 3072], P(None, 'fsdp')
- grad_gate: float32 [768, 3072], P(None, 'fsdp')
- grad_up: float32 [768, 3072], P(None, 'fsdp')
- grad_down: float32 [3072, 768], P('fsdp')
- grad_gains: float32 [2, 768], replicated
- grad_table: float32 [32, 12], replicated
- grad_router: float32 [768, 64], replicated
The draws below stay inside these ranges and needn't reach their ends.
Inputs may be any that keep to these rules, and one draw needn't show every extreme that they name: `segment`: each block of 64 slots is one micro-batch of one device; sequences take consecutive slots and are numbered 0 to 7 in order within a block; unused slots, marked -1, come at a block's end; the first block has no unused slot and reaches number 7. `expert_ids`: the two experts of a row differ. `bucket_of`: never falls as the distance grows; equal to the distance below 16.
All inputs are finite; a program needn't handle non-finite values.
Results may differ from the reference program's by a relative error of at most 0.012.
The reference program's roundings to bfloat16 on the way count: a program that leaves them out, or rounds other values in their place, can miss the bound.
Values may be sent and summed in bfloat16 or wider, within the bound.
A program may use at most 192 MiB of HBM per device.

```python
import math
import jax
import jax.numpy as jnp
from jax import lax

D = 768
FF = 3072
ROUTED = 64
HEAD_DIM = 64
HEADS = 12
BUCKETS = 32
MICRO = 2
SLOTS = 64
TOKENS = 4096
N_FSDP = 32


def draw_attn_weight(key, part):
    values = jax.random.normal(key, (D, 4 * D), jnp.float32)
    columns = jnp.arange(4 * D)[None, :]
    scaled = values * jnp.where(columns >= 3 * D, float(D // 8) ** (-0.5), float(D) ** (-0.5))
    return jnp.clip(scaled, -0.6, 0.6).astype(jnp.bfloat16)


def draw_segment(key, part):
    spans = TOKENS // SLOTS
    first_key = jax.random.fold_in(key, 11)
    second_key = jax.random.fold_in(key, 23)
    filled = jax.random.randint(first_key, (spans, 1), SLOTS // 2, SLOTS)
    filled = jnp.where(jnp.arange(spans)[:, None] == 0, SLOTS, filled)
    places = jnp.arange(SLOTS)[None, :]
    starts = jax.random.randint(second_key, (spans, SLOTS), 0, max(4, SLOTS // 4)) == 0
    forced = (places % (SLOTS // 8) == 0) & (jnp.arange(spans)[:, None] == 0)
    starts = jnp.where(places == 0, 0, (starts | forced).astype(jnp.int32))
    numbers = jnp.minimum(jnp.cumsum(starts, axis=1), 7).astype(jnp.int32)
    numbers = jnp.where(places < filled, numbers, -1)
    return numbers.reshape(TOKENS).astype(jnp.int32)


def draw_expert_ids(key, part):
    coin = jax.random.randint(jax.random.fold_in(key, 31), (TOKENS,), 0, 2)
    other_first = jax.random.randint(jax.random.fold_in(key, 37), (TOKENS,), 1, ROUTED)
    first = jnp.where(coin == 0, 0, other_first).astype(jnp.int32)
    rest = jax.random.randint(jax.random.fold_in(key, 41), (TOKENS,), 0, ROUTED - 1)
    second = (rest + (rest >= first).astype(jnp.int32)).astype(jnp.int32)
    swap = jax.random.randint(jax.random.fold_in(key, 43), (TOKENS,), 0, 2)
    left = jnp.where(swap == 0, first, second)
    right = jnp.where(swap == 0, second, first)
    return jnp.stack([left, right], axis=1).astype(jnp.int32)


def draw_bucket_of(key, part):
    places = jnp.arange(SLOTS)
    increments = jax.random.randint(jax.random.fold_in(key, 5), (SLOTS,), 0, 2)
    increments = jnp.where(places < BUCKETS // 2, 1, increments)
    increments = jnp.where(places == 0, 0, increments)
    climbed = jnp.minimum(jnp.cumsum(increments), BUCKETS - 1)
    return jnp.where(places == SLOTS - 1, BUCKETS - 1, climbed).astype(jnp.int32)


def shard_levels(rng, dims, pieces, low, largest):
    loudness, own = 1.0, jax.random.fold_in(rng, 6)
    for position, shards_of in pieces:
        heights = jnp.exp(jax.random.uniform(jax.random.fold_in(own, position), (shards_of,), jnp.float32, low / len(pieces), largest / len(pieces)))
        loudness = loudness * jnp.repeat(heights, dims[position] // shards_of).reshape([-1 if axis == position else 1 for axis in range(len(dims))])
    return loudness


def noise(own_key, extent, width, most, pieces=(), dtype=jnp.bfloat16):
    drawn = width * jax.random.normal(own_key, extent, jnp.float32)
    if pieces:
        drawn = drawn * shard_levels(own_key, extent, pieces, -0.22, 0.18)
    return jnp.clip(drawn, -most, most).astype(dtype)


def setup_inputs(seed: int = 0) -> dict:
    seeds = jax.random.split(jax.random.key(seed), 13)
    tokens = noise(seeds[0], (TOKENS, D), 1.0, 6.0, ((0, 32),))
    attn_weight = draw_attn_weight(jax.random.fold_in(seeds[12], 71), 0)
    w_gate = noise(seeds[2], (D, FF), D ** -0.5, 0.21875, ((1, 32),))
    w_up = noise(seeds[3], (D, FF), D ** -0.5, 0.21875, ((1, 32),))
    w_down = noise(seeds[4], (FF, D), FF ** -0.5, 0.109375, ((0, 32),))
    norm_gains = jnp.clip(1.0 + 0.1 * jax.random.normal(seeds[5], (2, D), jnp.float32), 0.5, 1.5)
    bias_table = noise(seeds[6], (BUCKETS, HEADS), 1.0, 4.0, (), jnp.float32)
    router = noise(seeds[7], (D, ROUTED), (D // 4) ** -0.5, 0.4375, (), jnp.float32)
    grad_out = noise(seeds[8], (TOKENS, D), 1.0, 6.0, ((0, 32),))
    segment = draw_segment(jax.random.fold_in(seeds[12], 71), 0)
    expert_ids = draw_expert_ids(jax.random.fold_in(seeds[12], 71), 0)
    bucket_of = draw_bucket_of(jax.random.fold_in(seeds[12], 71), 0)
    return dict(tokens=tokens, attn_weight=attn_weight, w_gate=w_gate, w_up=w_up, w_down=w_down, norm_gains=norm_gains, bias_table=bias_table, router=router, grad_out=grad_out, segment=segment, expert_ids=expert_ids, bucket_of=bucket_of)


EPSILON = 1e-06
HIGHEST = lax.Precision.HIGHEST

@jax.custom_vjp
def low(v):
    return lax.optimization_barrier(v.astype(jnp.bfloat16)).astype(jnp.float32)

@jax.custom_vjp
def low_back(v):
    return v

def low_keep(v):
    return (low(v), None)

def low_pass(kept, grad):
    return (grad,)

def back_keep(v):
    return (v, None)

def back_low(kept, grad):
    return (low(grad),)
low.defvjp(low_keep, low_pass)
low_back.defvjp(back_keep, back_low)

def matmul_high(left, right):
    return jnp.dot(left, right, precision=HIGHEST)

def attend_span(normed, segments, w_attn, table, bucket_grid):
    triple = low(low_back(matmul_high(normed, w_attn[:, :3 * D])))
    query = triple[:, :D].reshape(SLOTS, HEADS, HEAD_DIM)
    keyset = triple[:, D:2 * D].reshape(SLOTS, HEADS, HEAD_DIM)
    valueset = triple[:, 2 * D:].reshape(SLOTS, HEADS, HEAD_DIM)
    places = jnp.arange(SLOTS)
    allowed = (segments[:, None] == segments[None, :]) & (places[None, :] <= places[:, None])
    offsets = jnp.transpose(table[bucket_grid], (2, 0, 1))
    raw = jnp.einsum('ihd,jhd->hij', query, keyset, precision=HIGHEST)
    scores = low_back(raw * HEAD_DIM ** (-0.5) + offsets)
    weights = jax.nn.softmax(jnp.where(allowed[None], scores, -1e+30), axis=-1)
    mixed = jnp.einsum('hij,jhd->ihd', low(weights), valueset, precision=HIGHEST).reshape(SLOTS, D)
    mixed = low(low_back(mixed))
    return low_back(matmul_high(mixed, w_attn[:, 3 * D:].T))

def forward_group(inputs, segments, choices, w_attn, gate_w, up_w, down_w, gains, table, route, bucket_grid):
    scale_one = lax.rsqrt(lax.optimization_barrier(jnp.mean(inputs * inputs, axis=-1, keepdims=True)) + EPSILON)
    normed = low(inputs * scale_one * gains[0])
    branch = jax.vmap(attend_span, in_axes=(0, 0, None, None, None))(normed, segments, w_attn, table, bucket_grid)
    middle = (inputs + branch).reshape(-1, D)
    scale_two = lax.rsqrt(lax.optimization_barrier(jnp.mean(middle * middle, axis=-1, keepdims=True)) + EPSILON)
    second = low(middle * scale_two * gains[1])
    router_probs = jax.nn.softmax(matmul_high(second, route), axis=-1)
    picked = jnp.any(choices[:, :, None] == jnp.arange(ROUTED)[None, None, :], axis=1)
    picked_f = jnp.where(picked, 1.0, 0.0)
    chosen_total = lax.optimization_barrier(jnp.sum(router_probs * picked_f, axis=-1))
    active = jnp.where(segments.reshape(-1) >= 0, 1.0, 0.0)
    combine = router_probs[:, 0] * picked_f[:, 0] * active / chosen_total
    gated = low_back(matmul_high(second, gate_w))
    lifted = low_back(matmul_high(second, up_w))
    hidden = low(jax.nn.gelu(gated, approximate=True) * lifted)
    expert_out = low_back(matmul_high(hidden, down_w))
    total = middle + combine[:, None] * expert_out
    return total.reshape(inputs.shape)

def reference(tokens, attn_weight, w_gate, w_up, w_down, norm_gains, bias_table, router, grad_out, segment, expert_ids, bucket_of):
    spans = N_FSDP * MICRO
    group = math.gcd(spans, max(1, 4096 // SLOTS))
    places = jnp.arange(SLOTS)
    distance = jnp.maximum(places[:, None] - places[None, :], 0)
    bucket_grid = bucket_of[distance]
    seg_groups = segment.reshape(spans // group, group, SLOTS)
    id_groups = expert_ids.reshape(spans // group, group * SLOTS, 2)

    def forward(inputs, w_attn, gate_w, up_w, down_w, gains, table, route):

        def one_group(items):
            block_inputs, block_segments, block_choices = items
            return forward_group(block_inputs, block_segments, block_choices, w_attn, gate_w, up_w, down_w, gains, table, route, bucket_grid)
        grouped = inputs.reshape(spans // group, group, SLOTS, D)
        outputs = lax.map(jax.checkpoint(one_group), (grouped, seg_groups, id_groups))
        return outputs.reshape(TOKENS, D)
    result, backward = jax.vjp(forward, tokens.astype(jnp.float32), attn_weight.astype(jnp.float32), w_gate.astype(jnp.float32), w_up.astype(jnp.float32), w_down.astype(jnp.float32), norm_gains, bias_table, router)
    grads = backward(grad_out.astype(jnp.float32))
    return (result.astype(jnp.bfloat16), grads[0].astype(jnp.bfloat16), grads[1], grads[2], grads[3], grads[4], grads[5], grads[6], grads[7])
```

```python
import functools
import math
import jax
import jax.numpy as jnp
from jax import lax
from jax.experimental import pallas as pl
from jax.experimental.pallas import tpu as pltpu
from jax.sharding import PartitionSpec as P

EPSILON = 1e-06
HIGHEST = lax.Precision.HIGHEST
MESH = pl.DeviceIdType.MESH
TEAM = 4
F32 = jnp.float32
BF16 = jnp.bfloat16
VMEM = pl.BlockSpec(memory_space=pltpu.VMEM)
ANY = pl.BlockSpec(memory_space=pl.ANY)
CONTRACT_ROWS = (((0,), (0,)), ((), ()))
CONTRACT_COLS = (((1,), (1,)), ((), ()))


def place(n):
    sub = n // (TEAM * TEAM)
    me = lax.axis_index("fsdp")
    p = me // (TEAM * sub)
    t = lax.rem(me // sub, TEAM)
    s = lax.rem(me, sub)
    return sub, p, t, s, (lambda p, t, s: (p * (TEAM * sub) + t * sub + s,))


def greet(peers):
    barrier = pltpu.get_barrier_semaphore()
    for peer in peers:
        pl.semaphore_signal(barrier, inc=1, device_id=peer, device_id_type=MESH)
    pl.semaphore_wait(barrier, len(peers))


def remote(src, dst, send, recv, peer):
    return pltpu.make_async_remote_copy(
        src_ref=src, dst_ref=dst, send_sem=send, recv_sem=recv, device_id=peer, device_id_type=MESH
    )


def other(index, step, count):
    return lax.rem(index + step, count)


def spread_peers(sub, p, t, s, dev):
    peers = [dev(other(p, k, TEAM), t, s) for k in range(1, TEAM)]
    return peers + [dev(p, t, other(s, k, sub)) for k in range(1, sub)]


def team_peers(p, t, s, dev):
    return [dev(p, other(t, k, TEAM), s) for k in range(1, TEAM)]


def weights_start(n, w_ref, w_all, sems):
    sub, p, t, s, dev = place(n)
    p_send, p_recv, s_send, s_recv, own_sem = sems
    wide, near, local = [], [], []
    for i in range(w_ref.shape[0]):
        for k in range(1, TEAM):
            c = remote(w_ref.at[i], w_all.at[i, p, s], p_send.at[i, k], p_recv.at[i, k],
                       dev(other(p, k, TEAM), t, s))
            c.start()
            wide.append(c)
    for i in range(w_ref.shape[0]):
        for k in range(1, sub):
            c = remote(w_ref.at[i], w_all.at[i, p, s], s_send.at[i, 0, k], s_recv.at[i, 0, k],
                       dev(p, t, other(s, k, sub)))
            c.start()
            near.append(c)
        c = pltpu.make_async_copy(w_ref.at[i], w_all.at[i, p, s], own_sem.at[i])
        c.start()
        local.append(c)
    return wide, near, local


def weights_finish(n, w_all, sems, state):
    sub, p, t, s, dev = place(n)
    _, _, s_send, s_recv, _ = sems
    wide, near, local = state
    for i in range(w_all.shape[0]):
        for k in range(1, TEAM):
            wide[i * (TEAM - 1) + k - 1].wait_recv()
            q = other(p, TEAM - k, TEAM)
            for j in range(1, sub):
                c = remote(w_all.at[i, q, s], w_all.at[i, q, s], s_send.at[i, k, j], s_recv.at[i, k, j],
                           dev(p, t, other(s, j, sub)))
                c.start()
                near.append(c)
    for c in wide:
        c.wait_send()
    for c in near:
        c.wait()
    for c in local:
        c.wait()


def weights_sems(n, kinds):
    sub = n // (TEAM * TEAM)
    dma = pltpu.SemaphoreType.DMA
    return [dma((kinds, TEAM)), dma((kinds, TEAM)), dma((kinds, TEAM, sub)), dma((kinds, TEAM, sub)), dma((kinds,))]


def weights_shape(n, w):
    return jax.ShapeDtypeStruct((w.shape[0], TEAM, n // (TEAM * TEAM)) + w.shape[1:], w.dtype)


def gather_kernel(n, w_ref, tok_ref, dy_ref, meta_ref, w_all, tok_all, dy_all, meta_all,
                  t_send, t_recv, own_sem, *sems):
    sub, p, t, s, dev = place(n)
    greet(spread_peers(sub, p, t, s, dev) + team_peers(p, t, s, dev))
    state = weights_start(n, w_ref, w_all, sems)
    copies, local = [], []
    for i, (src, dst) in enumerate(((tok_ref, tok_all), (dy_ref, dy_all), (meta_ref, meta_all))):
        for k in range(1, TEAM):
            c = remote(src, dst.at[t], t_send.at[i, k], t_recv.at[i, k], dev(p, other(t, k, TEAM), s))
            c.start()
            copies.append(c)
        c = pltpu.make_async_copy(src, dst.at[t], own_sem.at[i])
        c.start()
        local.append(c)
    weights_finish(n, w_all, sems, state)
    for c in copies:
        c.wait()
    for c in local:
        c.wait()


def gather(n, w, tok, dy, meta):
    dma = pltpu.SemaphoreType.DMA
    shape = jax.ShapeDtypeStruct
    return pl.pallas_call(
        functools.partial(gather_kernel, n),
        out_shape=(
            weights_shape(n, w),
            shape((TEAM,) + tok.shape, BF16),
            shape((TEAM,) + dy.shape, BF16),
            shape((TEAM,) + meta.shape, jnp.int32),
        ),
        in_specs=[VMEM] * 4,
        out_specs=(ANY,) * 4,
        scratch_shapes=[dma((3, TEAM)), dma((3, TEAM)), dma((3,))] + weights_sems(n, w.shape[0]),
        compiler_params=pltpu.CompilerParams(collective_id=0, has_side_effects=True),
        name="gather_all",
    )(w, tok, dy, meta)


def middle_kernel(n, part_ref, x_ref, gain_ref, w_ref, y_ref, h_all, w_all, got, held,
                  a_send, a_recv, b_send, b_recv, own_sem, *sems):
    sub, p, t, s, dev = place(n)
    greet(spread_peers(sub, p, t, s, dev) + team_peers(p, t, s, dev))
    copies = []
    for k in range(1, TEAM):
        u = other(t, k, TEAM)
        c = remote(part_ref.at[u], got.at[k - 1], a_send.at[k], a_recv.at[k], dev(p, u, s))
        c.start()
        copies.append(c)
    state = weights_start(n, w_ref, w_all, sems)
    total = x_ref[...].astype(F32) + part_ref[t].astype(F32)
    for k in range(1, TEAM):
        copies[k - 1].wait_recv()
        total = total + got[k - 1].astype(F32)
    y_ref[...] = total
    scale = lax.rsqrt(jnp.mean(total * total, axis=-1, keepdims=True) + EPSILON)
    held[...] = (total * scale * gain_ref[1:2, :]).astype(BF16)
    local = pltpu.make_async_copy(held, h_all.at[t], own_sem)
    local.start()
    sends = []
    for k in range(1, TEAM):
        c = remote(held, h_all.at[t], b_send.at[k], b_recv.at[k], dev(p, other(t, k, TEAM), s))
        c.start()
        sends.append(c)
    weights_finish(n, w_all, sems, state)
    for c in copies:
        c.wait_send()
    for c in sends:
        c.wait()
    local.wait()


def middle_exchange(n, part, x, gains, w):
    dma = pltpu.SemaphoreType.DMA
    shape = jax.ShapeDtypeStruct
    return pl.pallas_call(
        functools.partial(middle_kernel, n),
        out_shape=(shape(x.shape, F32), shape((TEAM,) + x.shape, BF16), weights_shape(n, w)),
        in_specs=[VMEM] * 4,
        out_specs=(VMEM, ANY, ANY),
        scratch_shapes=[pltpu.VMEM((TEAM - 1,) + x.shape, BF16), pltpu.VMEM(x.shape, BF16),
                        dma((TEAM,)), dma((TEAM,)), dma((TEAM,)), dma((TEAM,)), dma] + weights_sems(n, w.shape[0]),
        compiler_params=pltpu.CompilerParams(collective_id=1, has_side_effects=True),
        name="middle_exchange",
    )(part, x, gains, w)


def reduce_kernel(n, m, h, gain_row, *refs):
    parts, rows, grad_ref = refs[:m], refs[m:m + h], refs[m + h]
    refs = refs[m + h + 1:]
    small = gain_row is not None
    if small:
        unit_ref, small_ref = refs[:2]
        refs = refs[2:]
    outs, rows_all, grad_out = refs[:m], refs[m:m + h], refs[m + h]
    if small:
        small_out = refs[m + h + 1]
        refs = refs[:m + h + 1] + refs[m + h + 2:]
    (got, sib, to_send, far, t_send, t_recv, h_send, h_recv, own_sem,
     s_send, s_recv, p_send, p_recv) = refs[m + h + 1:m + h + 14]
    rest = refs[m + h + 14:]
    sub, p, t, s, dev = place(n)
    greet(spread_peers(sub, p, t, s, dev) + team_peers(p, t, s, dev))
    kinds = grad_ref.shape[0]
    near, tokens, wide, shared, local = [], [], [], [], []
    for kind in range(kinds):
        for k in range(1, sub):
            v = other(s, k, sub)
            c = remote(grad_ref.at[kind, :, v], sib.at[kind, k - 1], s_send.at[kind, k], s_recv.at[kind, k],
                       dev(p, t, v))
            c.start()
            near.append(c)
    for i in range(h):
        for k in range(1, TEAM):
            c = remote(rows[i], rows_all[i].at[t], h_send.at[i, k], h_recv.at[i, k],
                       dev(p, other(t, k, TEAM), s))
            c.start()
            shared.append(c)
        c = pltpu.make_async_copy(rows[i], rows_all[i].at[t], own_sem.at[i])
        c.start()
        local.append(c)
    for i in range(m):
        for k in range(1, TEAM):
            u = other(t, k, TEAM)
            c = remote(parts[i].at[u], got.at[i, k - 1], t_send.at[i, k], t_recv.at[i, k], dev(p, u, s))
            c.start()
            tokens.append(c)
    for kind in range(kinds):
        for c in near[kind * (sub - 1):(kind + 1) * (sub - 1)]:
            c.wait_recv()
        for k in range(1, TEAM):
            q = other(p, k, TEAM)
            total = grad_ref[kind, q, s].astype(F32)
            for j in range(1, sub):
                total = total + sib[kind, j - 1, q].astype(F32)
            to_send[kind, k - 1] = total.astype(BF16)
            c = remote(to_send.at[kind, k - 1], far.at[kind, k - 1], p_send.at[kind, k], p_recv.at[kind, k],
                       dev(q, t, s))
            c.start()
            wide.append(c)
    for i in range(m):
        total = parts[i][t].astype(F32)
        for k in range(1, TEAM):
            tokens[i * (TEAM - 1) + k - 1].wait_recv()
            total = total + got[i, k - 1].astype(F32)
        outs[i][...] = total
    if small:
        buf = rest[0]
        piece, line = divmod(gain_row, small_ref.shape[1])
        gain = jnp.sum(outs[0][...] * unit_ref[...], axis=0, keepdims=True)
        buf[...] = small_ref[...]
        buf[piece, line:line + 1, :] = gain
        small_phases(n, buf, small_out, *rest[1:])
    for kind in range(kinds):
        for c in wide[kind * (TEAM - 1):(kind + 1) * (TEAM - 1)]:
            c.wait_recv()
        total = grad_ref[kind, p, s].astype(F32)
        for j in range(1, sub):
            total = total + sib[kind, j - 1, p].astype(F32)
        for k in range(1, TEAM):
            total = total + far[kind, k - 1].astype(F32)
        grad_out[kind] = total
    for c in near + tokens + wide:
        c.wait_send()
    for c in shared:
        c.wait()
    for c in local:
        c.wait()


def reduce_exchange(n, parts, rows, grads, ident, small=(), gain_row=None):
    sub = n // (TEAM * TEAM)
    m, h = len(parts), len(rows)
    dma = pltpu.SemaphoreType.DMA
    shape = jax.ShapeDtypeStruct
    block = parts[0].shape[1:] if m else (8, 128)
    kinds, tile = grads.shape[0], grads.shape[3:]
    outs = pl.pallas_call(
        functools.partial(reduce_kernel, n, m, h, gain_row),
        out_shape=(shape(block, F32),) * m
        + tuple(shape((TEAM,) + v.shape, v.dtype) for v in rows)
        + (shape((kinds,) + tile, F32),)
        + tuple(shape(v.shape, F32) for v in small[1:]),
        in_specs=[VMEM] * (m + h + 1 + len(small)),
        out_specs=(VMEM,) * m + (ANY,) * h + (VMEM,) * (1 + len(small[1:])),
        scratch_shapes=[
            pltpu.VMEM((max(m, 1), TEAM - 1) + block, BF16),
            pltpu.VMEM((kinds, sub - 1, TEAM) + tile, BF16),
            pltpu.VMEM((kinds, TEAM - 1) + tile, BF16),
            pltpu.VMEM((kinds, TEAM - 1) + tile, BF16),
            dma((max(m, 1), TEAM)), dma((max(m, 1), TEAM)),
            dma((max(h, 1), TEAM)), dma((max(h, 1), TEAM)), dma((max(h, 1),)),
            dma((kinds, sub)), dma((kinds, sub)), dma((kinds, TEAM)), dma((kinds, TEAM)),
        ] + (small_scratch(n, small[1].shape) if small else []),
        compiler_params=pltpu.CompilerParams(collective_id=ident, has_side_effects=True),
        name=f"reduce_{ident}",
    )(*parts, *rows, grads, *small)
    return (outs[:m], outs[m:m + h]) + tuple(outs[m + h:])


def small_phases(n, buf, out_ref, got, mine, sib, held, far,
                 a_send, a_recv, s_send, s_recv, b_send, b_recv, c_send, c_recv):
    sub, p, t, s, dev = place(n)
    first, near, second, third = [], [], [], []
    for k in range(1, TEAM):
        u = other(t, k, TEAM)
        c = remote(buf.at[u], got.at[k - 1], a_send.at[k], a_recv.at[k], dev(p, u, s))
        c.start()
        first.append(c)
    total = buf[t]
    for k in range(1, TEAM):
        first[k - 1].wait_recv()
        total = total + got[k - 1]
    mine[...] = total
    sib[s] = total
    for k in range(1, sub):
        c = remote(mine, sib.at[s], s_send.at[k], s_recv.at[k], dev(p, t, other(s, k, sub)))
        c.start()
        near.append(c)
    for c in near:
        c.wait_recv()
    total = sib[0]
    for k in range(1, sub):
        total = total + sib[k]
    held[...] = total
    far[p] = total
    for k in range(1, TEAM):
        c = remote(held, far.at[p], b_send.at[k], b_recv.at[k], dev(other(p, k, TEAM), t, s))
        c.start()
        second.append(c)
    for c in second:
        c.wait_recv()
    total = far[0]
    for k in range(1, TEAM):
        total = total + far[k]
    out_ref[t] = total
    for k in range(1, TEAM):
        c = remote(out_ref.at[t], out_ref.at[t], c_send.at[k], c_recv.at[k], dev(p, other(t, k, TEAM), s))
        c.start()
        third.append(c)
    for c in first + near + second:
        c.wait_send()
    for c in third:
        c.wait()


def small_scratch(n, shape):
    sub = n // (TEAM * TEAM)
    dma = pltpu.SemaphoreType.DMA
    tile = shape[1:]
    return [pltpu.VMEM(shape, F32), pltpu.VMEM((TEAM - 1,) + tile, F32), pltpu.VMEM(tile, F32),
            pltpu.VMEM((sub,) + tile, F32), pltpu.VMEM(tile, F32), pltpu.VMEM((TEAM,) + tile, F32),
            dma((TEAM,)), dma((TEAM,)), dma((sub,)), dma((sub,))] + [dma((TEAM,))] * 4


def gelu_tanh(inner):
    return jax.nn.gelu(inner, approximate=True)


def norm_back(inputs, scale, gain, upstream):
    weighted = gain * upstream
    return scale * weighted - inputs * scale * scale * scale * jnp.mean(
        weighted * inputs, axis=-1, keepdims=True
    )


def dot_t(a, b):
    return lax.dot_general(a, b, CONTRACT_COLS, preferred_element_type=F32)


def dot_r(a, b):
    return lax.dot_general(a, b, CONTRACT_ROWS, preferred_element_type=F32)


def dot(a, b):
    return jnp.dot(a, b, preferred_element_type=F32)


def body(n, tokens, attn_weight, w_gate, w_up, w_down, norm_gains, bias_table, router,
         grad_out, segment, expert_ids, bucket_of):
    rows, width = tokens.shape
    slots = bucket_of.shape[0]
    routed = router.shape[1]
    buckets, head_count = bias_table.shape
    head_width = width // head_count
    factor = head_width ** (-0.5)
    heads = head_count // TEAM
    part = heads * head_width
    sub, _, t, _, _ = place(n)
    all_rows = TEAM * rows
    spans = all_rows // slots

    early = jnp.stack([attn_weight.T, w_down])
    late = jnp.stack([w_gate.T, w_up.T])
    meta = jnp.concatenate([segment[None], expert_ids.T, jnp.zeros((5, rows), jnp.int32)], axis=0)
    w_all, tok_all, dy_all, meta_all = gather(n, early, tokens, grad_out, meta)
    w_all = w_all.reshape(2, -1, width)
    attn_t, down = w_all[0], w_all[1]
    qkv_t, out_t = attn_t[: 3 * part], attn_t[3 * part :]
    inputs = tok_all.reshape(all_rows, width).astype(F32)
    segments = meta_all[:, 0, :].reshape(all_rows)
    id_a = meta_all[:, 1, :].reshape(all_rows)
    id_b = meta_all[:, 2, :].reshape(all_rows)

    places = jnp.arange(slots)
    gap = places[:, None] - places[None, :]
    causal = gap >= 0
    gap_hit = (gap[:, :, None] == places[None, None, :]).astype(F32)
    bucket_hit = (bucket_of[:, None] == jnp.arange(buckets)[None, :]).astype(F32)
    table_mine = lax.dynamic_slice(bias_table, (0, heads * t), (buckets, heads))
    by_gap = jnp.dot(bucket_hit, table_mine, precision=HIGHEST)
    offsets = jnp.einsum("ijd,dh->hij", gap_hit, by_gap, precision=HIGHEST)

    scale_one = lax.rsqrt(jnp.mean(inputs * inputs, axis=-1, keepdims=True) + EPSILON)
    normed = (inputs * scale_one * norm_gains[0]).astype(BF16)
    triple = dot_t(normed, qkv_t).astype(BF16)
    heads_of = lambda v: v.reshape(spans, slots, heads, head_width)
    query = heads_of(triple[:, :part])
    keyset = heads_of(triple[:, part : 2 * part])
    valueset = heads_of(triple[:, 2 * part :])
    seg = segments.reshape(spans, slots)
    allowed = (seg[:, :, None] == seg[:, None, :]) & causal[None]
    raw = jnp.einsum("bihd,bjhd->bhij", query, keyset, preferred_element_type=F32)
    scores = jnp.where(allowed[:, None], raw * factor + offsets[None], -1e30)
    peak = jnp.max(scores, axis=-1, keepdims=True)
    lifted_scores = jnp.exp(scores - peak)
    weights = lifted_scores / jnp.sum(lifted_scores, axis=-1, keepdims=True)
    weights_low = weights.astype(BF16)
    mixed = jnp.einsum("bhij,bjhd->bihd", weights_low, valueset, preferred_element_type=F32)
    mixed = mixed.reshape(all_rows, part).astype(BF16)
    branch = dot(mixed, out_t).astype(BF16).reshape(TEAM, rows, width)
    middle, second_all, late_all = middle_exchange(n, branch, tokens, norm_gains, late)
    late_all = late_all.reshape(2, -1, width)
    gate_t, up_t = late_all[0], late_all[1]
    second_all = second_all.reshape(all_rows, width)

    second_wide = second_all.astype(F32)
    probs_all = jax.nn.softmax(jnp.dot(second_wide, router, precision=HIGHEST), axis=-1)
    lanes = jnp.arange(routed)[None, :]
    picked_all = jnp.where((id_a[:, None] == lanes) | (id_b[:, None] == lanes), 1.0, 0.0)
    total_all = jnp.sum(probs_all * picked_all, axis=-1)
    live_all = picked_all[:, 0] * jnp.where(segments >= 0, 1.0, 0.0)
    combine_all = probs_all[:, 0] * live_all / total_all
    gated = dot_t(second_all, gate_t)
    lifted = dot_t(second_all, up_t)
    activated, gelu_back = jax.vjp(gelu_tanh, gated)
    hidden = (activated * lifted).astype(BF16)
    out_part = dot(hidden, down).astype(BF16).reshape(TEAM, rows, width)
    d_expert = (combine_all[:, None] * dy_all.reshape(all_rows, width).astype(F32)).astype(BF16)
    d_hidden = dot_t(d_expert, down)
    d_gated = gelu_back(d_hidden * lifted)[0].astype(BF16)
    d_lifted = (d_hidden * activated).astype(BF16)
    back_part = (dot(d_gated, gate_t) + dot(d_lifted, up_t)).astype(BF16).reshape(TEAM, rows, width)
    grad_ffn = jnp.stack(
        [dot_r(d_gated, second_all).astype(BF16), dot_r(d_lifted, second_all).astype(BF16)]
    ).reshape(2, TEAM, sub, -1, width)
    (expert_out, d_second), _, g_ffn = reduce_exchange(n, (out_part, back_part), (), grad_ffn, 2)
    grad_down = dot_r(hidden, d_expert).astype(BF16).reshape(1, TEAM, sub, -1, width)

    mine = lambda v: lax.dynamic_slice_in_dim(v, t * rows, rows, 0)
    second, probs, picked = mine(second_wide), mine(probs_all), mine(picked_all)
    chosen_total, live, combine = mine(total_all), mine(live_all), mine(combine_all)
    upstream = grad_out.astype(F32)
    result = (middle + combine[:, None] * expert_out).astype(BF16)
    d_combine = jnp.sum(expert_out * upstream, axis=-1)
    first_hot = jnp.where(jnp.arange(routed) == 0, 1.0, 0.0)
    ratio = probs[:, 0] / (chosen_total * chosen_total)
    d_probs = (d_combine * live)[:, None] * (
        first_hot[None, :] / chosen_total[:, None] - ratio[:, None] * picked
    )
    d_logits = probs * (d_probs - jnp.sum(d_probs * probs, axis=-1, keepdims=True))
    grad_router_t = lax.dot_general(d_logits, second, CONTRACT_ROWS, precision=HIGHEST)
    d_second = d_second + jnp.dot(d_logits, router.T, precision=HIGHEST)
    scale_two = lax.rsqrt(jnp.mean(middle * middle, axis=-1, keepdims=True) + EPSILON)
    gain_two = jnp.sum(d_second * middle * scale_two, axis=0)
    d_middle = upstream + norm_back(middle, scale_two, norm_gains[1], d_second)
    _, (d_branch,), g_down = reduce_exchange(n, (), (d_middle.astype(BF16),), grad_down, 3)
    d_branch = d_branch.reshape(all_rows, width)

    grad_out_t = dot_r(mixed, d_branch)
    d_mixed = heads_of(dot_t(d_branch, out_t).astype(BF16))
    d_weights = jnp.einsum("bihd,bjhd->bhij", d_mixed, valueset, preferred_element_type=F32)
    d_values = jnp.einsum("bhij,bihd->bjhd", weights_low, d_mixed, preferred_element_type=F32)
    d_scores = weights * (d_weights - jnp.sum(weights * d_weights, axis=-1, keepdims=True))
    d_scores = d_scores.astype(BF16)
    d_query = jnp.einsum("bhij,bjhd->bihd", d_scores, keyset, preferred_element_type=F32) * factor
    d_keys = jnp.einsum("bhij,bihd->bjhd", d_scores, query, preferred_element_type=F32) * factor
    score_sum = jnp.sum(d_scores.astype(F32), axis=0)
    gap_sum = jnp.einsum("hij,ijd->dh", score_sum, gap_hit, precision=HIGHEST)
    table_part = lax.dot_general(bucket_hit, gap_sum, CONTRACT_ROWS, precision=HIGHEST)
    grad_table = lax.dynamic_update_slice(jnp.zeros(bias_table.shape, F32), table_part, (0, heads * t))
    flat = lambda v: v.reshape(all_rows, part).astype(BF16)
    d_triple = jnp.concatenate([flat(d_query), flat(d_keys), flat(d_values)], axis=1)
    grad_in_t = dot_r(d_triple, normed)
    grad_attn = jnp.concatenate([grad_in_t, grad_out_t], axis=0).astype(BF16)
    grad_attn = grad_attn.reshape(1, TEAM, sub, -1, width)
    d_normed_part = dot(d_triple, qkv_t).astype(BF16).reshape(TEAM, rows, width)
    own_inputs = tokens.astype(F32)
    own_scale = mine(scale_one)
    table_flat = grad_table.reshape(-1)
    lines = -(-table_flat.shape[0] // width)
    table_rows = jnp.pad(table_flat, (0, lines * width - table_flat.shape[0])).reshape(lines, width)
    small = jnp.concatenate([grad_router_t, jnp.zeros((1, width), F32), gain_two[None], table_rows], axis=0)
    depth = -(-small.shape[0] // (8 * TEAM)) * 8
    small = jnp.pad(small, ((0, depth * TEAM - small.shape[0]), (0, 0))).reshape(TEAM, depth, width)
    (d_normed,), _, g_attn, small = reduce_exchange(
        n, (d_normed_part,), (), grad_attn, 4, (own_inputs * own_scale, small), routed
    )
    small = small.reshape(TEAM * depth, width)
    input_grad = (d_middle + norm_back(own_inputs, own_scale, norm_gains[0], d_normed)).astype(BF16)
    grad_router = small[:routed].T
    grad_gains = small[routed : routed + 2]
    grad_table = small[routed + 2 : routed + 2 + lines].reshape(-1)[: table_flat.shape[0]].reshape(bias_table.shape)
    return (result, input_grad, g_attn[0].T, g_ffn[0].T, g_ffn[1].T, g_down[0],
            grad_gains, grad_table, grad_router)


LINES = 8
TOK, DY, META, BRANCH, SECOND, OUT, BACK, DBRANCH, DNORM = range(9)
ATTN, GATE, UP, DOWN = range(4)


def split_high(v):
    high = v.astype(BF16)
    return high, (v - high.astype(F32)).astype(BF16)


def eye(size, dtype):
    row = lax.broadcasted_iota(jnp.int32, (size, size), 0)
    col = lax.broadcasted_iota(jnp.int32, (size, size), 1)
    return jnp.where(row == col, 1.0, 0.0).astype(dtype)


def block_kernel(
    n, head_count,
    attn_ref, gate_ref, up_ref, down_ref, tok_ref, dy_ref, seg_ref, ids_ref, gains_ref, router_ref,
    buckets_ref, table_ref, bucket_ref,
    result_ref, dtok_ref, g_ref, small_ref, late_ref,
    w_all, g_part, sib, to_send, far,
    tok_all, dy_all, meta_all, normed, q_all, k_all, v_all, mixed, probs_all, offs,
    row_send, row_got, own_part, middle_s, h_all, dexp_all, coef_s, eprobs_s, rhi, rlo,
    gs, us, hidden, ge_s, dgu_s, dg_s, du_s, dmid_s, db_all, dq_all, dk_all, dv_all, score_s, gap_s,
    sbuf, s_got, s_mine, s_sib, s_held, s_far, l_own, l_got, l_sum, l_sib, l_tot, l_far,
    t_send, t_recv, z_send, z_recv, ws_send, ws_recv, gs_send, gs_recv, gp_send, gp_recv,
    sa_send, sa_recv, sb_send, sb_recv, sc_send, sc_recv, sd_send, sd_recv,
    la_send, la_recv, lb_send, lb_recv, lc_send, lc_recv,
):
    sub, p, t, s, dev = place(n)
    rows, width = tok_ref.shape
    shard = down_ref.shape[0]
    heads = head_count // TEAM
    head_width = width // head_count
    part = heads * head_width
    factor = head_width ** (-0.5)
    slots = buckets_ref.shape[1]
    routed = router_ref.shape[1]
    chunk = 256

    barrier = pltpu.get_barrier_semaphore()
    peers = spread_peers(sub, p, t, s, dev) + team_peers(p, t, s, dev)
    for peer in peers:
        pl.semaphore_signal(barrier, inc=1, device_id=peer, device_id_type=MESH)

    def mate(k):
        return other(t, k, TEAM)

    def seat(u):
        return pl.ds(pl.multiple_of(u * rows, rows), rows)

    def lot(q, v):
        return pl.ds(pl.multiple_of((q * sub + v) * shard, shard), shard)

    pending = []

    def send(src, dst, ssem, rsem, peer):
        c = remote(src, dst, ssem, rsem, peer)
        c.start()
        pending.append(c)
        return c

    def share(kind, src, whole):
        return [send(src, whole.at[seat(t)], t_send.at[kind, k], t_recv.at[kind, k], dev(p, mate(k), s))
                for k in range(1, TEAM)]

    def turned(ref):
        return dot_t(eye(shard, BF16), ref[...]).astype(BF16)

    w_all[ATTN, lot(p, s), :] = turned(attn_ref)
    tok_all[seat(t), :] = tok_ref[...]
    ids = dot_r(ids_ref[...].astype(F32), eye(rows, F32))
    line = lax.broadcasted_iota(jnp.int32, (LINES, rows), 0)
    meta_all[pl.ds(pl.multiple_of(t * LINES, LINES), LINES), :] = jnp.where(
        line == 0, seg_ref[...].astype(F32), jnp.where(line == 1, ids[0:1, :], jnp.where(line == 2, ids[1:2, :], 0.0))
    )
    pl.semaphore_wait(barrier, len(peers))

    wide = {}

    def weights_send(kind):
        mine = w_all.at[kind, lot(p, s), :]
        wide[kind] = [send(mine, mine, z_send.at[kind, k], z_recv.at[kind, k], dev(other(p, k, TEAM), t, s))
                      for k in range(1, TEAM)]
        wide[kind, "near"] = [send(mine, mine, ws_send.at[kind, 0, j], ws_recv.at[kind, 0, j], dev(p, t, other(s, j, sub)))
                              for j in range(1, sub)]

    def weights_forward(kind):
        for k in range(1, TEAM):
            wide[kind][k - 1].wait_recv()
            block = w_all.at[kind, lot(other(p, TEAM - k, TEAM), s), :]
            wide[kind, "near"] += [
                send(block, block, ws_send.at[kind, k, j], ws_recv.at[kind, k, j], dev(p, t, other(s, j, sub)))
                for j in range(1, sub)]

    def weights_wait(kind):
        for c in wide[kind, "near"]:
            c.wait_recv()

    mine_meta = meta_all.at[pl.ds(pl.multiple_of(t * LINES, LINES), LINES), :]
    metas = [send(mine_meta, mine_meta, t_send.at[META, k], t_recv.at[META, k], dev(p, mate(k), s)) for k in range(1, TEAM)]
    toks = share(TOK, tok_ref, tok_all)
    weights_send(ATTN)

    w_all[GATE, lot(p, s), :] = turned(gate_ref)
    w_all[UP, lot(p, s), :] = turned(up_ref)
    w_all[DOWN, lot(p, s), :] = down_ref[...]
    dy_all[seat(t), :] = dy_ref[...]
    rhi[...], rlo[...] = split_high(router_ref[...])

    place_r = lax.broadcasted_iota(jnp.int32, (slots, 2 * slots), 0)
    place_c = lax.rem(lax.broadcasted_iota(jnp.int32, (slots, 2 * slots), 1), slots)
    gap = place_r - place_c
    offs[...] = jnp.zeros(offs.shape, F32)

    def spread_bias(d, carry):
        hit = gap == d
        for h in range(heads):
            offs[h] = jnp.where(hit, table_ref[bucket_ref[d], heads * t + h], offs[h])
        return carry

    lax.fori_loop(0, slots, spread_bias, 0)

    row_i = lax.broadcasted_iota(jnp.int32, (rows, rows), 0)
    col_i = lax.broadcasted_iota(jnp.int32, (rows, rows), 1)
    causal = (row_i >= col_i) & ((row_i // slots) == (col_i // slots))
    lane_head = lax.broadcasted_iota(jnp.int32, (rows, part), 1) // head_width
    gain_one, gain_two = gains_ref[0:1, :], gains_ref[1:2, :]
    zero_low = jnp.zeros((rows, part), BF16)

    def meta_of(u):
        lines = meta_all[pl.ds(pl.multiple_of(u * LINES, LINES), LINES), :]
        return lines, dot_t(eye(rows, F32), lines)

    def unit_of(u):
        x = tok_all[seat(u), :].astype(F32)
        return x * lax.rsqrt(jnp.mean(x * x, axis=-1, keepdims=True) + EPSILON)

    def attend(u):
        rows_u = seat(u)
        h1 = (unit_of(u) * gain_one).astype(BF16)
        normed[rows_u, :] = h1
        q = dot_t(h1, w_all[ATTN, 0:part, :]).astype(BF16)
        key = dot_t(h1, w_all[ATTN, part:2 * part, :]).astype(BF16)
        v = dot_t(h1, w_all[ATTN, 2 * part:3 * part, :]).astype(BF16)
        q_all[rows_u, :], k_all[rows_u, :], v_all[rows_u, :] = q, key, v
        lines, cols = meta_of(u)
        allowed = (cols[:, 0:1] == lines[0:1, :]) & causal
        mix = jnp.zeros((rows, part), F32)
        for h in range(heads):
            raw = dot_t(jnp.where(lane_head == h, q, zero_low), key)
            scores = jnp.where(allowed, raw * factor + jnp.concatenate([offs[h], offs[h]], axis=0), -1e30)
            lifted = jnp.exp(scores - jnp.max(scores, axis=-1, keepdims=True))
            weights = lifted / jnp.sum(lifted, axis=-1, keepdims=True)
            probs_all[h, rows_u, :] = weights
            mix = jnp.where(lane_head == h, dot(weights.astype(BF16), v), mix)
        low = mix.astype(BF16)
        mixed[rows_u, :] = low
        return dot(low, w_all[ATTN, 3 * part:4 * part, :])

    slot = {BRANCH: 0, OUT: 1, BACK: 2, DNORM: 3}

    def scatter(kind, k, value):
        i = slot[kind]
        if k == 0:
            own_part[i] = value
            return []
        row_send[i, k - 1] = value.astype(BF16)
        return [send(row_send.at[i, k - 1], row_got.at[i, k - 1], t_send.at[kind, k], t_recv.at[kind, k],
                     dev(p, mate(k), s))]

    def gathered(kind, copies):
        total = own_part[slot[kind]]
        for c in copies:
            c.wait_recv()
        for k in range(1, TEAM):
            total = total + row_got[slot[kind], k - 1].astype(F32)
        return total

    weights_forward(ATTN)
    weights_send(GATE)
    weights_send(UP)
    dys = share(DY, dy_ref, dy_all)
    weights_wait(ATTN)
    branch = []
    for k in range(TEAM):
        if k:
            metas[k - 1].wait_recv()
            toks[k - 1].wait_recv()
        branch += scatter(BRANCH, (TEAM - k) % TEAM, attend(other(t, TEAM - k, TEAM)))
    weights_send(DOWN)

    middle = tok_ref[...].astype(F32) + gathered(BRANCH, branch)
    middle_s[...] = middle
    scale = lax.rsqrt(jnp.mean(middle * middle, axis=-1, keepdims=True) + EPSILON)
    h_all[seat(t), :] = (middle * scale * gain_two).astype(BF16)
    mine_h = h_all.at[seat(t), :]
    seconds = [send(mine_h, mine_h, t_send.at[SECOND, k], t_recv.at[SECOND, k], dev(p, mate(k), s)) for k in range(1, TEAM)]

    lane_expert = lax.broadcasted_iota(jnp.int32, (rows, routed), 1).astype(F32)

    def route(u):
        h2 = h_all[seat(u), :]
        logits = dot(h2, rhi[...]) + dot(h2, rlo[...])
        lifted = jnp.exp(logits - jnp.max(logits, axis=-1, keepdims=True))
        probs = lifted / jnp.sum(lifted, axis=-1, keepdims=True)
        _, cols = meta_of(u)
        picked = jnp.where((cols[:, 1:2] == lane_expert) | (cols[:, 2:3] == lane_expert), 1.0, 0.0)
        chosen = jnp.sum(probs * picked, axis=-1, keepdims=True)
        live = picked[:, 0:1] * jnp.where(cols[:, 0:1] >= 0.0, 1.0, 0.0)
        combine = probs[:, 0:1] * live / chosen
        dexp_all[seat(u), :] = (combine * dy_all[seat(u), :].astype(F32)).astype(BF16)
        return probs, picked, chosen, live, combine

    eprobs_s[...] = route(t)[0]
    for k in range(1, TEAM):
        dys[k - 1].wait_recv()
        seconds[k - 1].wait_recv()
        route(other(t, TEAM - k, TEAM))

    weights_forward(GATE)
    weights_forward(UP)
    weights_wait(GATE)
    weights_wait(UP)
    k0 = (2.0 / math.pi) ** 0.5
    k1 = 0.044715
    step = 32
    for c in range(width // chunk):
        cols = slice(c * chunk, (c + 1) * chunk)
        gs[...] = dot_t(h_all[...], w_all[GATE, cols, :])
        us[...] = dot_t(h_all[...], w_all[UP, cols, :])

        def lift(r, carry):
            rr = pl.ds(pl.multiple_of(r * step, step), step)
            g, u = gs[rr, :], us[rr, :]
            square = g * g
            bend = jnp.tanh(k0 * g * (1.0 + k1 * square))
            half = 0.5 * (1.0 + bend)
            act = g * half
            slope = half + 0.5 * g * (1.0 - bend * bend) * (k0 * (1.0 + 3.0 * k1 * square))
            hidden[rr, cols] = (act * u).astype(BF16)
            ge_s[rr, cols] = act
            dgu_s[rr, cols] = slope * u
            return carry

        lax.fori_loop(0, TEAM * rows // step, lift, 0)

    near = {}
    reduced = {}

    def grad_near(kind):
        near[kind] = [
            send(g_part.at[kind, lot(q, other(s, j, sub)), :], sib.at[kind, j - 1, q], gs_send.at[kind, q, j],
                 gs_recv.at[kind, q, j], dev(p, t, other(s, j, sub)))
            for q in range(TEAM) for j in range(1, sub)]

    def grad_of(kind, q):
        total = g_part[kind, lot(q, s), :].astype(F32)
        for j in range(1, sub):
            total = total + sib[kind, j - 1, q].astype(F32)
        return total

    def grad_wide(kind):
        for c in near[kind]:
            c.wait_recv()
        reduced[kind] = []
        for k in range(1, TEAM):
            q = other(p, k, TEAM)
            to_send[kind, k - 1] = grad_of(kind, q).astype(BF16)
            reduced[kind].append(send(to_send.at[kind, k - 1], far.at[kind, k - 1], gp_send.at[kind, k],
                                      gp_recv.at[kind, k], dev(q, t, s)))

    def grad_end(kind):
        total = grad_of(kind, p)
        for c in reduced[kind]:
            c.wait_recv()
        for k in range(1, TEAM):
            total = total + far[kind, k - 1].astype(F32)
        g_ref[kind] = total

    g_part[DOWN] = dot_r(hidden[...], dexp_all[...]).astype(BF16)
    grad_near(DOWN)
    weights_forward(DOWN)
    weights_wait(DOWN)
    outs = []
    for k in (1, 2, 3, 0):
        outs += scatter(OUT, k, dot(hidden[seat(mate(k)), :], w_all[DOWN]))
    grad_wide(DOWN)
    for c in range(width // chunk):
        cols = slice(c * chunk, (c + 1) * chunk)
        gs[...] = dot_t(dexp_all[...], w_all[DOWN, cols, :])

        def lower(r, carry):
            rr = pl.ds(pl.multiple_of(r * step, step), step)
            da = gs[rr, :]
            dg_s[rr, cols] = (da * dgu_s[rr, cols]).astype(BF16)
            du_s[rr, cols] = (da * ge_s[rr, cols]).astype(BF16)
            return carry

        lax.fori_loop(0, TEAM * rows // step, lower, 0)
    backs = []
    for k in (1, 2, 3, 0):
        u = seat(mate(k))
        backs += scatter(BACK, k, dot(dg_s[u, :], w_all[GATE]) + dot(du_s[u, :], w_all[UP]))
    g_part[GATE] = dot_r(dg_s[...], h_all[...]).astype(BF16)
    grad_near(GATE)
    g_part[UP] = dot_r(du_s[...], h_all[...]).astype(BF16)
    grad_near(UP)
    grad_wide(GATE)
    grad_wide(UP)

    upstream = dy_ref[...].astype(F32)
    probs = eprobs_s[...]
    _, cols = meta_of(t)
    picked = jnp.where((cols[:, 1:2] == lane_expert) | (cols[:, 2:3] == lane_expert), 1.0, 0.0)
    chosen = jnp.sum(probs * picked, axis=-1, keepdims=True)
    live = picked[:, 0:1] * jnp.where(cols[:, 0:1] >= 0.0, 1.0, 0.0)
    combine = probs[:, 0:1] * live / chosen
    expert = gathered(OUT, outs)
    result_ref[...] = (middle_s[...] + combine * expert).astype(BF16)
    d_combine = jnp.sum(expert * upstream, axis=-1, keepdims=True)
    first_hot = jnp.where(lane_expert == 0.0, 1.0, 0.0)
    ratio = probs[:, 0:1] / (chosen * chosen)
    d_probs = (d_combine * live) * (first_hot / chosen - ratio * picked)
    d_logits = probs * (d_probs - jnp.sum(d_probs * probs, axis=-1, keepdims=True))
    l_hi, l_lo = split_high(d_logits)
    l_lowest = (d_logits - l_hi.astype(F32) - l_lo.astype(F32)).astype(BF16)
    d_route = dot_t(l_hi, rhi[...]) + dot_t(l_hi, rlo[...]) + dot_t(l_lo, rhi[...])
    d_second = gathered(BACK, backs) + d_route
    middle = middle_s[...]
    scale = lax.rsqrt(jnp.mean(middle * middle, axis=-1, keepdims=True) + EPSILON)
    d_middle = upstream + norm_back(middle, scale, gain_two, d_second)
    dmid_s[...] = d_middle
    db_all[seat(t), :] = d_middle.astype(BF16)
    mine_b = db_all.at[seat(t), :]
    dbs = [send(mine_b, mine_b, t_send.at[DBRANCH, k], t_recv.at[DBRANCH, k], dev(p, mate(k), s)) for k in range(1, TEAM)]

    depth = sbuf.shape[0] // TEAM
    h2 = h_all[seat(t), :]
    sbuf[0:routed, :] = dot_r(l_hi, h2) + dot_r(l_lo, h2) + dot_r(l_lowest, h2)
    tail = lax.broadcasted_iota(jnp.int32, (sbuf.shape[0] - routed, width), 0)
    sbuf[routed:, :] = jnp.where(tail == 0, jnp.sum(d_second * middle * scale, axis=0, keepdims=True), 0.0)

    def piece(u):
        return pl.ds(pl.multiple_of(u * depth, depth), depth)

    first = [send(sbuf.at[piece(mate(k)), :], s_got.at[k - 1], sa_send.at[k], sa_recv.at[k], dev(p, mate(k), s))
             for k in range(1, TEAM)]

    score_s[...] = jnp.zeros(score_s.shape, F32)
    for k in range(TEAM):
        if k:
            dbs[k - 1].wait_recv()
        rows_u = seat(other(t, TEAM - k, TEAM))
        d_mix = dot_t(db_all[rows_u, :], w_all[ATTN, 3 * part:4 * part, :]).astype(BF16)
        q, key, v = q_all[rows_u, :], k_all[rows_u, :], v_all[rows_u, :]
        dq = jnp.zeros((rows, part), F32)
        dk = jnp.zeros((rows, part), F32)
        dv = jnp.zeros((rows, part), F32)
        for h in range(heads):
            weights = probs_all[h, rows_u, :]
            d_w = dot_t(jnp.where(lane_head == h, d_mix, zero_low), v)
            ds = (weights * (d_w - jnp.sum(weights * d_w, axis=-1, keepdims=True))).astype(BF16)
            dv = jnp.where(lane_head == h, dot_r(weights.astype(BF16), d_mix), dv)
            dq = jnp.where(lane_head == h, dot(ds, key), dq)
            dk = jnp.where(lane_head == h, dot_r(ds, q), dk)
            wide_ds = ds.astype(F32)
            score_s[h] = score_s[h] + wide_ds[:slots] + wide_ds[slots:]
        dq_all[rows_u, :] = (dq * factor).astype(BF16)
        dk_all[rows_u, :] = (dk * factor).astype(BF16)
        dv_all[rows_u, :] = dv.astype(BF16)

    g_part[ATTN, 3 * part:4 * part, :] = dot_r(mixed[...], db_all[...]).astype(BF16)
    g_part[ATTN, 0:part, :] = dot_r(dq_all[...], normed[...]).astype(BF16)
    g_part[ATTN, part:2 * part, :] = dot_r(dk_all[...], normed[...]).astype(BF16)
    g_part[ATTN, 2 * part:3 * part, :] = dot_r(dv_all[...], normed[...]).astype(BF16)
    grad_near(ATTN)
    norms = []
    gain_sum = jnp.zeros((1, width), F32)
    for k in (1, 2, 3, 0):
        u = mate(k)
        rows_u = seat(u)
        value = (dot(dq_all[rows_u, :], w_all[ATTN, 0:part, :]) + dot(dk_all[rows_u, :], w_all[ATTN, part:2 * part, :])
                 + dot(dv_all[rows_u, :], w_all[ATTN, 2 * part:3 * part, :]))
        norms += scatter(DNORM, k, value)
        gain_sum = gain_sum + jnp.sum(value * unit_of(u), axis=0, keepdims=True)
    grad_wide(ATTN)

    total = sbuf[piece(t), :]
    for c in first:
        c.wait_recv()
    for k in range(1, TEAM):
        total = total + s_got[k - 1]
    s_mine[...] = total
    s_sib[s] = total
    second_near = [send(s_mine, s_sib.at[s], sb_send.at[j], sb_recv.at[j], dev(p, t, other(s, j, sub)))
                   for j in range(1, sub)]

    def gather_gap(d, carry):
        hit = gap == d
        for h in range(heads):
            gap_s[h, pl.ds(d, 1), :] = jnp.sum(jnp.where(hit, score_s[h], 0.0), axis=0, keepdims=True)
        return carry

    lax.fori_loop(0, slots, gather_gap, 0)
    lane = lax.broadcasted_iota(jnp.int32, (slots, 128), 1)
    by_gap = jnp.zeros((slots, 128), F32)
    for h in range(heads):
        by_gap = jnp.where(lane == heads * t + h, jnp.sum(gap_s[h], axis=-1, keepdims=True), by_gap)
    count = table_ref.shape[0]
    bucket_hit = jnp.where(lax.broadcasted_iota(jnp.int32, (count, slots), 0) == buckets_ref[...], 1.0, 0.0)
    l_own[0:count, :] = jnp.dot(bucket_hit, by_gap, precision=HIGHEST, preferred_element_type=F32)
    for i in range(width // 128):
        l_own[count + i:count + i + 1, :] = gain_sum[:, i * 128:(i + 1) * 128]
    used = count + width // 128
    l_own[used:, :] = jnp.zeros((l_own.shape[0] - used, 128), F32)
    late_a = [send(l_own, l_got.at[k - 1], la_send.at[k], la_recv.at[k], dev(p, mate(k), s)) for k in range(1, TEAM)]

    for c in second_near:
        c.wait_recv()
    total = s_sib[0]
    for j in range(1, sub):
        total = total + s_sib[j]
    s_held[...] = total
    s_far[p] = total
    second_far = [send(s_held, s_far.at[p], sc_send.at[k], sc_recv.at[k], dev(other(p, k, TEAM), t, s))
                  for k in range(1, TEAM)]

    grad_end(DOWN)
    for c in late_a:
        c.wait_recv()
    total = l_own[...]
    for k in range(1, TEAM):
        total = total + l_got[k - 1]
    l_sum[...] = total
    l_sib[s] = total
    late_b = [send(l_sum, l_sib.at[s], lb_send.at[j], lb_recv.at[j], dev(p, t, other(s, j, sub))) for j in range(1, sub)]
    grad_end(GATE)
    for c in late_b:
        c.wait_recv()
    total = l_sib[0]
    for j in range(1, sub):
        total = total + l_sib[j]
    l_tot[...] = total
    l_far[p] = total
    late_c = [send(l_tot, l_far.at[p], lc_send.at[k], lc_recv.at[k], dev(other(p, k, TEAM), t, s)) for k in range(1, TEAM)]
    grad_end(UP)

    x = tok_ref[...].astype(F32)
    d_normed = gathered(DNORM, norms)
    scale = lax.rsqrt(jnp.mean(x * x, axis=-1, keepdims=True) + EPSILON)
    dtok_ref[...] = (dmid_s[...] + norm_back(x, scale, gain_one, d_normed)).astype(BF16)

    for c in second_far:
        c.wait_recv()
    total = s_far[0]
    for k in range(1, TEAM):
        total = total + s_far[k]
    small_ref[piece(t), :] = total
    mine_small = small_ref.at[piece(t), :]
    third = [send(mine_small, mine_small, sd_send.at[k], sd_recv.at[k], dev(p, mate(k), s)) for k in range(1, TEAM)]
    for c in late_c:
        c.wait_recv()
    total = l_far[0]
    for k in range(1, TEAM):
        total = total + l_far[k]
    late_ref[...] = total
    grad_end(ATTN)
    for c in third:
        c.wait_recv()
    for c in pending:
        c.wait_send()


def finish_kernel(routed, result_ref, dtok_ref, g_ref, small_ref, late_ref,
                  result_out, dtok_out, attn_out, gate_out, up_out, down_out, gains_out, table_out, router_out):
    result_out[...] = result_ref[...]
    dtok_out[...] = dtok_ref[...]
    attn_out[...] = g_ref[ATTN].T
    gate_out[...] = g_ref[GATE].T
    up_out[...] = g_ref[UP].T
    down_out[...] = g_ref[DOWN]
    router_out[...] = small_ref[0:routed, :].T
    count, heads = table_out.shape
    table_out[...] = late_ref[0:count, 0:heads]
    gains_out[1:2, :] = small_ref[routed:routed + 1, :]
    for i in range(gains_out.shape[1] // 128):
        gains_out[0:1, i * 128:(i + 1) * 128] = late_ref[count + i:count + i + 1, :]


def block(n, tokens, attn_weight, w_gate, w_up, w_down, norm_gains, bias_table, router,
          grad_out, segment, expert_ids, bucket_of):
    rows, width = tokens.shape
    shard = w_down.shape[0]
    sub = n // (TEAM * TEAM)
    head_count = bias_table.shape[1]
    heads = head_count // TEAM
    part = heads * (width // head_count)
    slots = bucket_of.shape[0]
    routed = router.shape[1]
    every = TEAM * rows
    dma = pltpu.SemaphoreType.DMA
    shape = jax.ShapeDtypeStruct
    buf = pltpu.VMEM
    depth = -(-(routed + 1) // (8 * TEAM)) * 8
    lines = -(-(bias_table.shape[0] + width // 128) // 8) * 8
    smem = pl.BlockSpec(memory_space=pltpu.SMEM)
    result, dtok, grads, small, late = pl.pallas_call(
        functools.partial(block_kernel, n, head_count),
        out_shape=(shape(tokens.shape, BF16), shape(tokens.shape, BF16), shape((4, shard, width), F32),
                   shape((depth * TEAM, width), F32), shape((lines, 128), F32)),
        in_specs=[VMEM] * 11 + [smem] * 2,
        out_specs=(VMEM,) * 5,
        scratch_shapes=[
            buf((4, width, width), BF16), buf((4, width, width), BF16), buf((4, sub - 1, TEAM, shard, width), BF16),
            buf((4, TEAM - 1, shard, width), BF16), buf((4, TEAM - 1, shard, width), BF16),
            buf((every, width), BF16), buf((every, width), BF16), buf((TEAM * LINES, rows), F32), buf((every, width), BF16),
            buf((every, part), BF16), buf((every, part), BF16), buf((every, part), BF16), buf((every, part), BF16),
            buf((heads, every, rows), F32), buf((heads, slots, 2 * slots), F32),
            buf((4, TEAM - 1, rows, width), BF16), buf((4, TEAM - 1, rows, width), BF16), buf((4, rows, width), F32),
            buf((rows, width), F32), buf((every, width), BF16), buf((every, width), BF16), buf((rows, 128), F32),
            buf((rows, routed), F32), buf((width, routed), BF16), buf((width, routed), BF16),
            buf((every, 256), F32), buf((every, 256), F32), buf((every, width), BF16), buf((every, width), F32),
            buf((every, width), F32), buf((every, width), BF16), buf((every, width), BF16), buf((rows, width), F32),
            buf((every, width), BF16), buf((every, part), BF16), buf((every, part), BF16), buf((every, part), BF16),
            buf((heads, slots, 2 * slots), F32), buf((heads, slots, 2 * slots), F32),
            buf((depth * TEAM, width), F32), buf((TEAM - 1, depth, width), F32), buf((depth, width), F32),
            buf((sub, depth, width), F32), buf((depth, width), F32), buf((TEAM, depth, width), F32),
            buf((lines, 128), F32), buf((TEAM - 1, lines, 128), F32), buf((lines, 128), F32),
            buf((sub, lines, 128), F32), buf((lines, 128), F32), buf((TEAM, lines, 128), F32),
            dma((9, TEAM)), dma((9, TEAM)), dma((4, TEAM)), dma((4, TEAM)), dma((4, TEAM, sub)), dma((4, TEAM, sub)),
            dma((4, TEAM, sub)), dma((4, TEAM, sub)), dma((4, TEAM)), dma((4, TEAM)),
            dma((TEAM,)), dma((TEAM,)), dma((sub,)), dma((sub,)), dma((TEAM,)), dma((TEAM,)), dma((TEAM,)), dma((TEAM,)),
            dma((TEAM,)), dma((TEAM,)), dma((sub,)), dma((sub,)), dma((TEAM,)), dma((TEAM,)),
        ],
        compiler_params=pltpu.CompilerParams(collective_id=0, has_side_effects=True, vmem_limit_bytes=56 * 2**20),
        name="block",
    )(attn_weight, w_gate, w_up, w_down, tokens, grad_out, segment.reshape(1, rows), expert_ids, norm_gains, router,
      bucket_of.reshape(1, slots), bias_table, bucket_of)
    column = shape((width, shard), F32)
    return pl.pallas_call(
        functools.partial(finish_kernel, routed),
        out_shape=(shape(tokens.shape, BF16), shape(tokens.shape, BF16), column, column, column, shape((shard, width), F32),
                   shape(norm_gains.shape, F32), shape(bias_table.shape, F32), shape(router.shape, F32)),
        in_specs=[VMEM] * 5,
        out_specs=(VMEM,) * 9,
        name="finish",
    )(result, dtok, grads, small, late)


def solution(mesh):
    n = mesh.shape["fsdp"]
    row, col = P("fsdp", None), P(None, "fsdp")
    in_specs = (row, col, col, col, row, P(), P(), P(), row, P("fsdp"), row, P())
    out_specs = (row, row, col, col, col, row, P(), P(), P())

    def run(*args):
        shard, rows = args[4].shape[0] // n, args[0].shape[0] // n
        whole_tiles = shard % 16 == 0 and rows == 2 * args[11].shape[0]
        return jax.shard_map(
            functools.partial(block if whole_tiles else body, n),
            mesh=mesh, in_specs=in_specs, out_specs=out_specs, check_vma=False,
        )(*args)

    return run
```

```python
import functools
import math
import jax
import jax.numpy as jnp
from jax import lax
from jax.experimental import pallas as pl
from jax.experimental.pallas import tpu as pltpu
from jax.sharding import PartitionSpec as P

EPSILON = 1e-06
HIGHEST = lax.Precision.HIGHEST
MESH = pl.DeviceIdType.MESH
TEAM = 4
F32 = jnp.float32
BF16 = jnp.bfloat16
VMEM = pl.BlockSpec(memory_space=pltpu.VMEM)
ANY = pl.BlockSpec(memory_space=pl.ANY)
CONTRACT_ROWS = (((0,), (0,)), ((), ()))
CONTRACT_COLS = (((1,), (1,)), ((), ()))


def place(n):
    sub = n // (TEAM * TEAM)
    me = lax.axis_index("fsdp")
    p = me // (TEAM * sub)
    t = lax.rem(me // sub, TEAM)
    s = lax.rem(me, sub)
    return sub, p, t, s, (lambda p, t, s: (p * (TEAM * sub) + t * sub + s,))


def greet(peers):
    barrier = pltpu.get_barrier_semaphore()
    for peer in peers:
        pl.semaphore_signal(barrier, inc=1, device_id=peer, device_id_type=MESH)
    pl.semaphore_wait(barrier, len(peers))


def remote(src, dst, send, recv, peer):
    return pltpu.make_async_remote_copy(
        src_ref=src, dst_ref=dst, send_sem=send, recv_sem=recv, device_id=peer, device_id_type=MESH
    )


def other(index, step, count):
    return lax.rem(index + step, count)


def spread_peers(sub, p, t, s, dev):
    peers = [dev(other(p, k, TEAM), t, s) for k in range(1, TEAM)]
    return peers + [dev(p, t, other(s, k, sub)) for k in range(1, sub)]


def team_peers(p, t, s, dev):
    return [dev(p, other(t, k, TEAM), s) for k in range(1, TEAM)]


def weights_start(n, w_ref, w_all, sems):
    sub, p, t, s, dev = place(n)
    p_send, p_recv, s_send, s_recv, own_sem = sems
    wide, near, local = [], [], []
    for i in range(w_ref.shape[0]):
        for k in range(1, TEAM):
            c = remote(w_ref.at[i], w_all.at[i, p, s], p_send.at[i, k], p_recv.at[i, k],
                       dev(other(p, k, TEAM), t, s))
            c.start()
            wide.append(c)
    for i in range(w_ref.shape[0]):
        for k in range(1, sub):
            c = remote(w_ref.at[i], w_all.at[i, p, s], s_send.at[i, 0, k], s_recv.at[i, 0, k],
                       dev(p, t, other(s, k, sub)))
            c.start()
            near.append(c)
        c = pltpu.make_async_copy(w_ref.at[i], w_all.at[i, p, s], own_sem.at[i])
        c.start()
        local.append(c)
    return wide, near, local


def weights_finish(n, w_all, sems, state):
    sub, p, t, s, dev = place(n)
    _, _, s_send, s_recv, _ = sems
    wide, near, local = state
    for i in range(w_all.shape[0]):
        for k in range(1, TEAM):
            wide[i * (TEAM - 1) + k - 1].wait_recv()
            q = other(p, TEAM - k, TEAM)
            for j in range(1, sub):
                c = remote(w_all.at[i, q, s], w_all.at[i, q, s], s_send.at[i, k, j], s_recv.at[i, k, j],
                           dev(p, t, other(s, j, sub)))
                c.start()
                near.append(c)
    for c in wide:
        c.wait_send()
    for c in near:
        c.wait()
    for c in local:
        c.wait()


def weights_sems(n, kinds):
    sub = n // (TEAM * TEAM)
    dma = pltpu.SemaphoreType.DMA
    return [dma((kinds, TEAM)), dma((kinds, TEAM)), dma((kinds, TEAM, sub)), dma((kinds, TEAM, sub)), dma((kinds,))]


def weights_shape(n, w):
    return jax.ShapeDtypeStruct((w.shape[0], TEAM, n // (TEAM * TEAM)) + w.shape[1:], w.dtype)


def gather_kernel(n, w_ref, tok_ref, dy_ref, meta_ref, w_all, tok_all, dy_all, meta_all,
                  t_send, t_recv, own_sem, *sems):
    sub, p, t, s, dev = place(n)
    greet(spread_peers(sub, p, t, s, dev) + team_peers(p, t, s, dev))
    state = weights_start(n, w_ref, w_all, sems)
    copies, local = [], []
    for i, (src, dst) in enumerate(((tok_ref, tok_all), (dy_ref, dy_all), (meta_ref, meta_all))):
        for k in range(1, TEAM):
            c = remote(src, dst.at[t], t_send.at[i, k], t_recv.at[i, k], dev(p, other(t, k, TEAM), s))
            c.start()
            copies.append(c)
        c = pltpu.make_async_copy(src, dst.at[t], own_sem.at[i])
        c.start()
        local.append(c)
    weights_finish(n, w_all, sems, state)
    for c in copies:
        c.wait()
    for c in local:
        c.wait()


def gather(n, w, tok, dy, meta):
    dma = pltpu.SemaphoreType.DMA
    shape = jax.ShapeDtypeStruct
    return pl.pallas_call(
        functools.partial(gather_kernel, n),
        out_shape=(
            weights_shape(n, w),
            shape((TEAM,) + tok.shape, BF16),
            shape((TEAM,) + dy.shape, BF16),
            shape((TEAM,) + meta.shape, jnp.int32),
        ),
        in_specs=[VMEM] * 4,
        out_specs=(ANY,) * 4,
        scratch_shapes=[dma((3, TEAM)), dma((3, TEAM)), dma((3,))] + weights_sems(n, w.shape[0]),
        compiler_params=pltpu.CompilerParams(collective_id=0, has_side_effects=True),
        name="gather_all",
    )(w, tok, dy, meta)


def middle_kernel(n, part_ref, x_ref, gain_ref, w_ref, y_ref, h_all, w_all, got, held,
                  a_send, a_recv, b_send, b_recv, own_sem, *sems):
    sub, p, t, s, dev = place(n)
    greet(spread_peers(sub, p, t, s, dev) + team_peers(p, t, s, dev))
    copies = []
    for k in range(1, TEAM):
        u = other(t, k, TEAM)
        c = remote(part_ref.at[u], got.at[k - 1], a_send.at[k], a_recv.at[k], dev(p, u, s))
        c.start()
        copies.append(c)
    state = weights_start(n, w_ref, w_all, sems)
    total = x_ref[...].astype(F32) + part_ref[t].astype(F32)
    for k in range(1, TEAM):
        copies[k - 1].wait_recv()
        total = total + got[k - 1].astype(F32)
    y_ref[...] = total
    scale = lax.rsqrt(jnp.mean(total * total, axis=-1, keepdims=True) + EPSILON)
    held[...] = (total * scale * gain_ref[1:2, :]).astype(BF16)
    local = pltpu.make_async_copy(held, h_all.at[t], own_sem)
    local.start()
    sends = []
    for k in range(1, TEAM):
        c = remote(held, h_all.at[t], b_send.at[k], b_recv.at[k], dev(p, other(t, k, TEAM), s))
        c.start()
        sends.append(c)
    weights_finish(n, w_all, sems, state)
    for c in copies:
        c.wait_send()
    for c in sends:
        c.wait()
    local.wait()


def middle_exchange(n, part, x, gains, w):
    dma = pltpu.SemaphoreType.DMA
    shape = jax.ShapeDtypeStruct
    return pl.pallas_call(
        functools.partial(middle_kernel, n),
        out_shape=(shape(x.shape, F32), shape((TEAM,) + x.shape, BF16), weights_shape(n, w)),
        in_specs=[VMEM] * 4,
        out_specs=(VMEM, ANY, ANY),
        scratch_shapes=[pltpu.VMEM((TEAM - 1,) + x.shape, BF16), pltpu.VMEM(x.shape, BF16),
                        dma((TEAM,)), dma((TEAM,)), dma((TEAM,)), dma((TEAM,)), dma] + weights_sems(n, w.shape[0]),
        compiler_params=pltpu.CompilerParams(collective_id=1, has_side_effects=True),
        name="middle_exchange",
    )(part, x, gains, w)


def reduce_kernel(n, m, h, gain_row, *refs):
    parts, rows, grad_ref = refs[:m], refs[m:m + h], refs[m + h]
    refs = refs[m + h + 1:]
    small = gain_row is not None
    if small:
        unit_ref, small_ref = refs[:2]
        refs = refs[2:]
    outs, rows_all, grad_out = refs[:m], refs[m:m + h], refs[m + h]
    if small:
        small_out = refs[m + h + 1]
        refs = refs[:m + h + 1] + refs[m + h + 2:]
    (got, sib, to_send, far, t_send, t_recv, h_send, h_recv, own_sem,
     s_send, s_recv, p_send, p_recv) = refs[m + h + 1:m + h + 14]
    rest = refs[m + h + 14:]
    sub, p, t, s, dev = place(n)
    greet(spread_peers(sub, p, t, s, dev) + team_peers(p, t, s, dev))
    kinds = grad_ref.shape[0]
    near, tokens, wide, shared, local = [], [], [], [], []
    for kind in range(kinds):
        for k in range(1, sub):
            v = other(s, k, sub)
            c = remote(grad_ref.at[kind, :, v], sib.at[kind, k - 1], s_send.at[kind, k], s_recv.at[kind, k],
                       dev(p, t, v))
            c.start()
            near.append(c)
    for i in range(h):
        for k in range(1, TEAM):
            c = remote(rows[i], rows_all[i].at[t], h_send.at[i, k], h_recv.at[i, k],
                       dev(p, other(t, k, TEAM), s))
            c.start()
            shared.append(c)
        c = pltpu.make_async_copy(rows[i], rows_all[i].at[t], own_sem.at[i])
        c.start()
        local.append(c)
    for i in range(m):
        for k in range(1, TEAM):
            u = other(t, k, TEAM)
            c = remote(parts[i].at[u], got.at[i, k - 1], t_send.at[i, k], t_recv.at[i, k], dev(p, u, s))
            c.start()
            tokens.append(c)
    for kind in range(kinds):
        for c in near[kind * (sub - 1):(kind + 1) * (sub - 1)]:
            c.wait_recv()
        for k in range(1, TEAM):
            q = other(p, k, TEAM)
            total = grad_ref[kind, q, s].astype(F32)
            for j in range(1, sub):
                total = total + sib[kind, j - 1, q].astype(F32)
            to_send[kind, k - 1] = total.astype(BF16)
            c = remote(to_send.at[kind, k - 1], far.at[kind, k - 1], p_send.at[kind, k], p_recv.at[kind, k],
                       dev(q, t, s))
            c.start()
            wide.append(c)
    for i in range(m):
        total = parts[i][t].astype(F32)
        for k in range(1, TEAM):
            tokens[i * (TEAM - 1) + k - 1].wait_recv()
            total = total + got[i, k - 1].astype(F32)
        outs[i][...] = total
    if small:
        buf = rest[0]
        piece, line = divmod(gain_row, small_ref.shape[1])
        gain = jnp.sum(outs[0][...] * unit_ref[...], axis=0, keepdims=True)
        buf[...] = small_ref[...]
        buf[piece, line:line + 1, :] = gain
        small_phases(n, buf, small_out, *rest[1:])
    for kind in range(kinds):
        for c in wide[kind * (TEAM - 1):(kind + 1) * (TEAM - 1)]:
            c.wait_recv()
        total = grad_ref[kind, p, s].astype(F32)
        for j in range(1, sub):
            total = total + sib[kind, j - 1, p].astype(F32)
        for k in range(1, TEAM):
            total = total + far[kind, k - 1].astype(F32)
        grad_out[kind] = total
    for c in near + tokens + wide:
        c.wait_send()
    for c in shared:
        c.wait()
    for c in local:
        c.wait()


def reduce_exchange(n, parts, rows, grads, ident, small=(), gain_row=None):
    sub = n // (TEAM * TEAM)
    m, h = len(parts), len(rows)
    dma = pltpu.SemaphoreType.DMA
    shape = jax.ShapeDtypeStruct
    block = parts[0].shape[1:] if m else (8, 128)
    kinds, tile = grads.shape[0], grads.shape[3:]
    outs = pl.pallas_call(
        functools.partial(reduce_kernel, n, m, h, gain_row),
        out_shape=(shape(block, F32),) * m
        + tuple(shape((TEAM,) + v.shape, v.dtype) for v in rows)
        + (shape((kinds,) + tile, F32),)
        + tuple(shape(v.shape, F32) for v in small[1:]),
        in_specs=[VMEM] * (m + h + 1 + len(small)),
        out_specs=(VMEM,) * m + (ANY,) * h + (VMEM,) * (1 + len(small[1:])),
        scratch_shapes=[
            pltpu.VMEM((max(m, 1), TEAM - 1) + block, BF16),
            pltpu.VMEM((kinds, sub - 1, TEAM) + tile, BF16),
            pltpu.VMEM((kinds, TEAM - 1) + tile, BF16),
            pltpu.VMEM((kinds, TEAM - 1) + tile, BF16),
            dma((max(m, 1), TEAM)), dma((max(m, 1), TEAM)),
            dma((max(h, 1), TEAM)), dma((max(h, 1), TEAM)), dma((max(h, 1),)),
            dma((kinds, sub)), dma((kinds, sub)), dma((kinds, TEAM)), dma((kinds, TEAM)),
        ] + (small_scratch(n, small[1].shape) if small else []),
        compiler_params=pltpu.CompilerParams(collective_id=ident, has_side_effects=True),
        name=f"reduce_{ident}",
    )(*parts, *rows, grads, *small)
    return (outs[:m], outs[m:m + h]) + tuple(outs[m + h:])


def small_phases(n, buf, out_ref, got, mine, sib, held, far,
                 a_send, a_recv, s_send, s_recv, b_send, b_recv, c_send, c_recv):
    sub, p, t, s, dev = place(n)
    first, near, second, third = [], [], [], []
    for k in range(1, TEAM):
        u = other(t, k, TEAM)
        c = remote(buf.at[u], got.at[k - 1], a_send.at[k], a_recv.at[k], dev(p, u, s))
        c.start()
        first.append(c)
    total = buf[t]
    for k in range(1, TEAM):
        first[k - 1].wait_recv()
        total = total + got[k - 1]
    mine[...] = total
    sib[s] = total
    for k in range(1, sub):
        c = remote(mine, sib.at[s], s_send.at[k], s_recv.at[k], dev(p, t, other(s, k, sub)))
        c.start()
        near.append(c)
    for c in near:
        c.wait_recv()
    total = sib[0]
    for k in range(1, sub):
        total = total + sib[k]
    held[...] = total
    far[p] = total
    for k in range(1, TEAM):
        c = remote(held, far.at[p], b_send.at[k], b_recv.at[k], dev(other(p, k, TEAM), t, s))
        c.start()
        second.append(c)
    for c in second:
        c.wait_recv()
    total = far[0]
    for k in range(1, TEAM):
        total = total + far[k]
    out_ref[t] = total
    for k in range(1, TEAM):
        c = remote(out_ref.at[t], out_ref.at[t], c_send.at[k], c_recv.at[k], dev(p, other(t, k, TEAM), s))
        c.start()
        third.append(c)
    for c in first + near + second:
        c.wait_send()
    for c in third:
        c.wait()


def small_scratch(n, shape):
    sub = n // (TEAM * TEAM)
    dma = pltpu.SemaphoreType.DMA
    tile = shape[1:]
    return [pltpu.VMEM(shape, F32), pltpu.VMEM((TEAM - 1,) + tile, F32), pltpu.VMEM(tile, F32),
            pltpu.VMEM((sub,) + tile, F32), pltpu.VMEM(tile, F32), pltpu.VMEM((TEAM,) + tile, F32),
            dma((TEAM,)), dma((TEAM,)), dma((sub,)), dma((sub,))] + [dma((TEAM,))] * 4


def gelu_tanh(inner):
    return jax.nn.gelu(inner, approximate=True)


def norm_back(inputs, scale, gain, upstream):
    weighted = gain * upstream
    return scale * weighted - inputs * scale * scale * scale * jnp.mean(
        weighted * inputs, axis=-1, keepdims=True
    )


def dot_t(a, b):
    return lax.dot_general(a, b, CONTRACT_COLS, preferred_element_type=F32)


def dot_r(a, b):
    return lax.dot_general(a, b, CONTRACT_ROWS, preferred_element_type=F32)


def dot(a, b):
    return jnp.dot(a, b, preferred_element_type=F32)


def body(n, tokens, attn_weight, w_gate, w_up, w_down, norm_gains, bias_table, router,
         grad_out, segment, expert_ids, bucket_of):
    rows, width = tokens.shape
    slots = bucket_of.shape[0]
    routed = router.shape[1]
    buckets, head_count = bias_table.shape
    head_width = width // head_count
    factor = head_width ** (-0.5)
    heads = head_count // TEAM
    part = heads * head_width
    sub, _, t, _, _ = place(n)
    all_rows = TEAM * rows
    spans = all_rows // slots

    early = jnp.stack([attn_weight.T, w_down])
    late = jnp.stack([w_gate.T, w_up.T])
    meta = jnp.concatenate([segment[None], expert_ids.T, jnp.zeros((5, rows), jnp.int32)], axis=0)
    w_all, tok_all, dy_all, meta_all = gather(n, early, tokens, grad_out, meta)
    w_all = w_all.reshape(2, -1, width)
    attn_t, down = w_all[0], w_all[1]
    qkv_t, out_t = attn_t[: 3 * part], attn_t[3 * part :]
    inputs = tok_all.reshape(all_rows, width).astype(F32)
    segments = meta_all[:, 0, :].reshape(all_rows)
    id_a = meta_all[:, 1, :].reshape(all_rows)
    id_b = meta_all[:, 2, :].reshape(all_rows)

    places = jnp.arange(slots)
    gap = places[:, None] - places[None, :]
    causal = gap >= 0
    gap_hit = (gap[:, :, None] == places[None, None, :]).astype(F32)
    bucket_hit = (bucket_of[:, None] == jnp.arange(buckets)[None, :]).astype(F32)
    table_mine = lax.dynamic_slice(bias_table, (0, heads * t), (buckets, heads))
    by_gap = jnp.dot(bucket_hit, table_mine, precision=HIGHEST)
    offsets = jnp.einsum("ijd,dh->hij", gap_hit, by_gap, precision=HIGHEST)

    scale_one = lax.rsqrt(jnp.mean(inputs * inputs, axis=-1, keepdims=True) + EPSILON)
    normed = (inputs * scale_one * norm_gains[0]).astype(BF16)
    triple = dot_t(normed, qkv_t).astype(BF16)
    heads_of = lambda v: v.reshape(spans, slots, heads, head_width)
    query = heads_of(triple[:, :part])
    keyset = heads_of(triple[:, part : 2 * part])
    valueset = heads_of(triple[:, 2 * part :])
    seg = segments.reshape(spans, slots)
    allowed = (seg[:, :, None] == seg[:, None, :]) & causal[None]
    raw = jnp.einsum("bihd,bjhd->bhij", query, keyset, preferred_element_type=F32)
    scores = jnp.where(allowed[:, None], raw * factor + offsets[None], -1e30)
    peak = jnp.max(scores, axis=-1, keepdims=True)
    lifted_scores = jnp.exp(scores - peak)
    weights = lifted_scores / jnp.sum(lifted_scores, axis=-1, keepdims=True)
    weights_low = weights.astype(BF16)
    mixed = jnp.einsum("bhij,bjhd->bihd", weights_low, valueset, preferred_element_type=F32)
    mixed = mixed.reshape(all_rows, part).astype(BF16)
    branch = dot(mixed, out_t).astype(BF16).reshape(TEAM, rows, width)
    middle, second_all, late_all = middle_exchange(n, branch, tokens, norm_gains, late)
    late_all = late_all.reshape(2, -1, width)
    gate_t, up_t = late_all[0], late_all[1]
    second_all = second_all.reshape(all_rows, width)

    second_wide = second_all.astype(F32)
    probs_all = jax.nn.softmax(jnp.dot(second_wide, router, precision=HIGHEST), axis=-1)
    lanes = jnp.arange(routed)[None, :]
    picked_all = jnp.where((id_a[:, None] == lanes) | (id_b[:, None] == lanes), 1.0, 0.0)
    total_all = jnp.sum(probs_all * picked_all, axis=-1)
    live_all = picked_all[:, 0] * jnp.where(segments >= 0, 1.0, 0.0)
    combine_all = probs_all[:, 0] * live_all / total_all
    gated = dot_t(second_all, gate_t)
    lifted = dot_t(second_all, up_t)
    activated, gelu_back = jax.vjp(gelu_tanh, gated)
    hidden = (activated * lifted).astype(BF16)
    out_part = dot(hidden, down).astype(BF16).reshape(TEAM, rows, width)
    d_expert = (combine_all[:, None] * dy_all.reshape(all_rows, width).astype(F32)).astype(BF16)
    d_hidden = dot_t(d_expert, down)
    d_gated = gelu_back(d_hidden * lifted)[0].astype(BF16)
    d_lifted = (d_hidden * activated).astype(BF16)
    back_part = (dot(d_gated, gate_t) + dot(d_lifted, up_t)).astype(BF16).reshape(TEAM, rows, width)
    grad_ffn = jnp.stack(
        [dot_r(d_gated, second_all).astype(BF16), dot_r(d_lifted, second_all).astype(BF16)]
    ).reshape(2, TEAM, sub, -1, width)
    (expert_out, d_second), _, g_ffn = reduce_exchange(n, (out_part, back_part), (), grad_ffn, 2)
    grad_down = dot_r(hidden, d_expert).astype(BF16).reshape(1, TEAM, sub, -1, width)

    mine = lambda v: lax.dynamic_slice_in_dim(v, t * rows, rows, 0)
    second, probs, picked = mine(second_wide), mine(probs_all), mine(picked_all)
    chosen_total, live, combine = mine(total_all), mine(live_all), mine(combine_all)
    upstream = grad_out.astype(F32)
    result = (middle + combine[:, None] * expert_out).astype(BF16)
    d_combine = jnp.sum(expert_out * upstream, axis=-1)
    first_hot = jnp.where(jnp.arange(routed) == 0, 1.0, 0.0)
    ratio = probs[:, 0] / (chosen_total * chosen_total)
    d_probs = (d_combine * live)[:, None] * (
        first_hot[None, :] / chosen_total[:, None] - ratio[:, None] * picked
    )
    d_logits = probs * (d_probs - jnp.sum(d_probs * probs, axis=-1, keepdims=True))
    grad_router_t = lax.dot_general(d_logits, second, CONTRACT_ROWS, precision=HIGHEST)
    d_second = d_second + jnp.dot(d_logits, router.T, precision=HIGHEST)
    scale_two = lax.rsqrt(jnp.mean(middle * middle, axis=-1, keepdims=True) + EPSILON)
    gain_two = jnp.sum(d_second * middle * scale_two, axis=0)
    d_middle = upstream + norm_back(middle, scale_two, norm_gains[1], d_second)
    _, (d_branch,), g_down = reduce_exchange(n, (), (d_middle.astype(BF16),), grad_down, 3)
    d_branch = d_branch.reshape(all_rows, width)

    grad_out_t = dot_r(mixed, d_branch)
    d_mixed = heads_of(dot_t(d_branch, out_t).astype(BF16))
    d_weights = jnp.einsum("bihd,bjhd->bhij", d_mixed, valueset, preferred_element_type=F32)
    d_values = jnp.einsum("bhij,bihd->bjhd", weights_low, d_mixed, preferred_element_type=F32)
    d_scores = weights * (d_weights - jnp.sum(weights * d_weights, axis=-1, keepdims=True))
    d_scores = d_scores.astype(BF16)
    d_query = jnp.einsum("bhij,bjhd->bihd", d_scores, keyset, preferred_element_type=F32) * factor
    d_keys = jnp.einsum("bhij,bihd->bjhd", d_scores, query, preferred_element_type=F32) * factor
    score_sum = jnp.sum(d_scores.astype(F32), axis=0)
    gap_sum = jnp.einsum("hij,ijd->dh", score_sum, gap_hit, precision=HIGHEST)
    table_part = lax.dot_general(bucket_hit, gap_sum, CONTRACT_ROWS, precision=HIGHEST)
    grad_table = lax.dynamic_update_slice(jnp.zeros(bias_table.shape, F32), table_part, (0, heads * t))
    flat = lambda v: v.reshape(all_rows, part).astype(BF16)
    d_triple = jnp.concatenate([flat(d_query), flat(d_keys), flat(d_values)], axis=1)
    grad_in_t = dot_r(d_triple, normed)
    grad_attn = jnp.concatenate([grad_in_t, grad_out_t], axis=0).astype(BF16)
    grad_attn = grad_attn.reshape(1, TEAM, sub, -1, width)
    d_normed_part = dot(d_triple, qkv_t).astype(BF16).reshape(TEAM, rows, width)
    own_inputs = tokens.astype(F32)
    own_scale = mine(scale_one)
    table_flat = grad_table.reshape(-1)
    lines = -(-table_flat.shape[0] // width)
    table_rows = jnp.pad(table_flat, (0, lines * width - table_flat.shape[0])).reshape(lines, width)
    small = jnp.concatenate([grad_router_t, jnp.zeros((1, width), F32), gain_two[None], table_rows], axis=0)
    depth = -(-small.shape[0] // (8 * TEAM)) * 8
    small = jnp.pad(small, ((0, depth * TEAM - small.shape[0]), (0, 0))).reshape(TEAM, depth, width)
    (d_normed,), _, g_attn, small = reduce_exchange(
        n, (d_normed_part,), (), grad_attn, 4, (own_inputs * own_scale, small), routed
    )
    small = small.reshape(TEAM * depth, width)
    input_grad = (d_middle + norm_back(own_inputs, own_scale, norm_gains[0], d_normed)).astype(BF16)
    grad_router = small[:routed].T
    grad_gains = small[routed : routed + 2]
    grad_table = small[routed + 2 : routed + 2 + lines].reshape(-1)[: table_flat.shape[0]].reshape(bias_table.shape)
    return (result, input_grad, g_attn[0].T, g_ffn[0].T, g_ffn[1].T, g_down[0],
            grad_gains, grad_table, grad_router)


LINES = 8
TOK, DY, META, BRANCH, SECOND, OUT, BACK, DBRANCH, DNORM = range(9)
ATTN, GATE, UP, DOWN = range(4)


def split_high(v):
    high = v.astype(BF16)
    return high, (v - high.astype(F32)).astype(BF16)


def eye(size, dtype):
    row = lax.broadcasted_iota(jnp.int32, (size, size), 0)
    col = lax.broadcasted_iota(jnp.int32, (size, size), 1)
    return jnp.where(row == col, 1.0, 0.0).astype(dtype)


def block_kernel(
    n, head_count,
    attn_ref, gate_ref, up_ref, down_ref, tok_ref, dy_ref, seg_ref, ids_ref, gains_ref, router_ref,
    buckets_ref, table_ref, bucket_ref,
    result_ref, dtok_ref, g_ref, small_ref, late_ref,
    w_all, g_part, sib, to_send, far,
    tok_all, dy_all, meta_all, normed, q_all, k_all, v_all, mixed, probs_all, offs,
    row_send, row_got, own_part, middle_s, h_all, dexp_all, coef_s, eprobs_s, rhi, rlo,
    gs, us, hidden, ge_s, dgu_s, dg_s, du_s, dmid_s, db_all, dq_all, dk_all, dv_all, score_s, gap_s,
    sbuf, s_got, s_mine, s_sib, s_held, s_far, l_own, l_got, l_sum, l_sib, l_tot, l_far,
    t_send, t_recv, z_send, z_recv, ws_send, ws_recv, gs_send, gs_recv, gp_send, gp_recv,
    sa_send, sa_recv, sb_send, sb_recv, sc_send, sc_recv, sd_send, sd_recv,
    la_send, la_recv, lb_send, lb_recv, lc_send, lc_recv,
):
    sub, p, t, s, dev = place(n)
    rows, width = tok_ref.shape
    shard = down_ref.shape[0]
    heads = head_count // TEAM
    head_width = width // head_count
    part = heads * head_width
    factor = head_width ** (-0.5)
    slots = buckets_ref.shape[1]
    routed = router_ref.shape[0]
    chunk = 256

    barrier = pltpu.get_barrier_semaphore()
    peers = spread_peers(sub, p, t, s, dev) + team_peers(p, t, s, dev)
    for peer in peers:
        pl.semaphore_signal(barrier, inc=1, device_id=peer, device_id_type=MESH)

    def mate(k):
        return other(t, k, TEAM)

    def seat(u):
        return pl.ds(pl.multiple_of(u * rows, rows), rows)

    def lot(q, v):
        return pl.ds(pl.multiple_of((q * sub + v) * shard, shard), shard)

    pending = []

    def send(src, dst, ssem, rsem, peer):
        c = remote(src, dst, ssem, rsem, peer)
        c.start()
        pending.append(c)
        return c

    def share(kind, src, whole):
        return [send(src, whole.at[seat(t)], t_send.at[kind, k], t_recv.at[kind, k], dev(p, mate(k), s))
                for k in range(1, TEAM)]

    w_all[ATTN, lot(p, s), :] = attn_ref[...]
    tok_all[seat(t), :] = tok_ref[...]
    ids = ids_ref[...].astype(F32)
    line = lax.broadcasted_iota(jnp.int32, (LINES, rows), 0)
    meta_all[pl.ds(pl.multiple_of(t * LINES, LINES), LINES), :] = jnp.where(
        line == 0, seg_ref[...].astype(F32), jnp.where(line == 1, ids[0:1, :], jnp.where(line == 2, ids[1:2, :], 0.0))
    )
    pl.semaphore_wait(barrier, len(peers))

    wide = {}

    def weights_send(kind):
        mine = w_all.at[kind, lot(p, s), :]
        wide[kind] = [send(mine, mine, z_send.at[kind, k], z_recv.at[kind, k], dev(other(p, k, TEAM), t, s))
                      for k in range(1, TEAM)]
        wide[kind, "near"] = [send(mine, mine, ws_send.at[kind, 0, j], ws_recv.at[kind, 0, j], dev(p, t, other(s, j, sub)))
                              for j in range(1, sub)]

    def weights_forward(kind):
        for k in range(1, TEAM):
            wide[kind][k - 1].wait_recv()
            block = w_all.at[kind, lot(other(p, TEAM - k, TEAM), s), :]
            wide[kind, "near"] += [
                send(block, block, ws_send.at[kind, k, j], ws_recv.at[kind, k, j], dev(p, t, other(s, j, sub)))
                for j in range(1, sub)]

    def weights_wait(kind):
        for c in wide[kind, "near"]:
            c.wait_recv()

    mine_meta = meta_all.at[pl.ds(pl.multiple_of(t * LINES, LINES), LINES), :]
    metas = [send(mine_meta, mine_meta, t_send.at[META, k], t_recv.at[META, k], dev(p, mate(k), s)) for k in range(1, TEAM)]
    toks = share(TOK, tok_ref, tok_all)
    weights_send(ATTN)

    w_all[GATE, lot(p, s), :] = gate_ref[...]
    w_all[UP, lot(p, s), :] = up_ref[...]
    w_all[DOWN, lot(p, s), :] = down_ref[...]
    dy_all[seat(t), :] = dy_ref[...]
    rhi[...], rlo[...] = split_high(router_ref[...])

    place_r = lax.broadcasted_iota(jnp.int32, (slots, 2 * slots), 0)
    place_c = lax.rem(lax.broadcasted_iota(jnp.int32, (slots, 2 * slots), 1), slots)
    gap = place_r - place_c
    offs[...] = jnp.zeros(offs.shape, F32)

    def spread_bias(d, carry):
        hit = gap == d
        for h in range(heads):
            offs[h] = jnp.where(hit, table_ref[heads * t + h, bucket_ref[d]], offs[h])
        return carry

    lax.fori_loop(0, slots, spread_bias, 0)

    row_i = lax.broadcasted_iota(jnp.int32, (rows, rows), 0)
    col_i = lax.broadcasted_iota(jnp.int32, (rows, rows), 1)
    causal = (row_i >= col_i) & ((row_i // slots) == (col_i // slots))
    lane_head = lax.broadcasted_iota(jnp.int32, (rows, part), 1) // head_width
    gain_one, gain_two = gains_ref[0:1, :], gains_ref[1:2, :]
    zero_low = jnp.zeros((rows, part), BF16)

    def meta_of(u):
        lines = meta_all[pl.ds(pl.multiple_of(u * LINES, LINES), LINES), :]
        return lines, dot_t(eye(rows, F32), lines)

    def unit_of(u):
        x = tok_all[seat(u), :].astype(F32)
        return x * lax.rsqrt(jnp.mean(x * x, axis=-1, keepdims=True) + EPSILON)

    def attend(u):
        rows_u = seat(u)
        h1 = (unit_of(u) * gain_one).astype(BF16)
        normed[rows_u, :] = h1
        q = dot_t(h1, w_all[ATTN, 0:part, :]).astype(BF16)
        key = dot_t(h1, w_all[ATTN, part:2 * part, :]).astype(BF16)
        v = dot_t(h1, w_all[ATTN, 2 * part:3 * part, :]).astype(BF16)
        q_all[rows_u, :], k_all[rows_u, :], v_all[rows_u, :] = q, key, v
        lines, cols = meta_of(u)
        allowed = (cols[:, 0:1] == lines[0:1, :]) & causal
        mix = jnp.zeros((rows, part), F32)
        for h in range(heads):
            raw = dot_t(jnp.where(lane_head == h, q, zero_low), key)
            scores = jnp.where(allowed, raw * factor + jnp.concatenate([offs[h], offs[h]], axis=0), -1e30)
            lifted = jnp.exp(scores - jnp.max(scores, axis=-1, keepdims=True))
            weights = lifted / jnp.sum(lifted, axis=-1, keepdims=True)
            probs_all[h, rows_u, :] = weights
            mix = jnp.where(lane_head == h, dot(weights.astype(BF16), v), mix)
        low = mix.astype(BF16)
        mixed[rows_u, :] = low
        return dot(low, w_all[ATTN, 3 * part:4 * part, :])

    slot = {BRANCH: 0, OUT: 1, BACK: 2, DNORM: 3}

    def scatter(kind, k, value):
        i = slot[kind]
        if k == 0:
            own_part[i] = value
            return []
        row_send[i, k - 1] = value.astype(BF16)
        return [send(row_send.at[i, k - 1], row_got.at[i, k - 1], t_send.at[kind, k], t_recv.at[kind, k],
                     dev(p, mate(k), s))]

    def gathered(kind, copies):
        total = own_part[slot[kind]]
        for c in copies:
            c.wait_recv()
        for k in range(1, TEAM):
            total = total + row_got[slot[kind], k - 1].astype(F32)
        return total

    weights_forward(ATTN)
    weights_send(GATE)
    weights_send(UP)
    dys = share(DY, dy_ref, dy_all)
    weights_wait(ATTN)
    branch = []
    for k in range(TEAM):
        if k:
            metas[k - 1].wait_recv()
            toks[k - 1].wait_recv()
        branch += scatter(BRANCH, (TEAM - k) % TEAM, attend(other(t, TEAM - k, TEAM)))
    weights_send(DOWN)

    middle = tok_ref[...].astype(F32) + gathered(BRANCH, branch)
    middle_s[...] = middle
    scale = lax.rsqrt(jnp.mean(middle * middle, axis=-1, keepdims=True) + EPSILON)
    h_all[seat(t), :] = (middle * scale * gain_two).astype(BF16)
    mine_h = h_all.at[seat(t), :]
    seconds = [send(mine_h, mine_h, t_send.at[SECOND, k], t_recv.at[SECOND, k], dev(p, mate(k), s)) for k in range(1, TEAM)]

    lane_expert = lax.broadcasted_iota(jnp.int32, (rows, routed), 1).astype(F32)

    def route(u):
        h2 = h_all[seat(u), :]
        logits = dot_t(h2, rhi[...]) + dot_t(h2, rlo[...])
        lifted = jnp.exp(logits - jnp.max(logits, axis=-1, keepdims=True))
        probs = lifted / jnp.sum(lifted, axis=-1, keepdims=True)
        _, cols = meta_of(u)
        picked = jnp.where((cols[:, 1:2] == lane_expert) | (cols[:, 2:3] == lane_expert), 1.0, 0.0)
        chosen = jnp.sum(probs * picked, axis=-1, keepdims=True)
        live = picked[:, 0:1] * jnp.where(cols[:, 0:1] >= 0.0, 1.0, 0.0)
        combine = probs[:, 0:1] * live / chosen
        dexp_all[seat(u), :] = (combine * dy_all[seat(u), :].astype(F32)).astype(BF16)
        return probs, picked, chosen, live, combine

    eprobs_s[...] = route(t)[0]
    for k in range(1, TEAM):
        dys[k - 1].wait_recv()
        seconds[k - 1].wait_recv()
        route(other(t, TEAM - k, TEAM))

    weights_forward(GATE)
    weights_forward(UP)
    weights_wait(GATE)
    weights_wait(UP)
    k0 = (2.0 / math.pi) ** 0.5
    k1 = 0.044715
    step = 32
    for c in range(width // chunk):
        cols = slice(c * chunk, (c + 1) * chunk)
        gs[...] = dot_t(h_all[...], w_all[GATE, cols, :])
        us[...] = dot_t(h_all[...], w_all[UP, cols, :])

        def lift(r, carry):
            rr = pl.ds(pl.multiple_of(r * step, step), step)
            g, u = gs[rr, :], us[rr, :]
            square = g * g
            bend = jnp.tanh(k0 * g * (1.0 + k1 * square))
            half = 0.5 * (1.0 + bend)
            act = g * half
            slope = half + 0.5 * g * (1.0 - bend * bend) * (k0 * (1.0 + 3.0 * k1 * square))
            hidden[rr, cols] = (act * u).astype(BF16)
            ge_s[rr, cols] = act
            dgu_s[rr, cols] = slope * u
            return carry

        lax.fori_loop(0, TEAM * rows // step, lift, 0)

    near = {}
    reduced = {}

    def grad_near(kind):
        near[kind] = [
            send(g_part.at[kind, lot(q, other(s, j, sub)), :], sib.at[kind, j - 1, q], gs_send.at[kind, q, j],
                 gs_recv.at[kind, q, j], dev(p, t, other(s, j, sub)))
            for q in range(TEAM) for j in range(1, sub)]

    def grad_of(kind, q):
        total = g_part[kind, lot(q, s), :].astype(F32)
        for j in range(1, sub):
            total = total + sib[kind, j - 1, q].astype(F32)
        return total

    def grad_wide(kind):
        for c in near[kind]:
            c.wait_recv()
        reduced[kind] = []
        for k in range(1, TEAM):
            q = other(p, k, TEAM)
            to_send[kind, k - 1] = grad_of(kind, q).astype(BF16)
            reduced[kind].append(send(to_send.at[kind, k - 1], far.at[kind, k - 1], gp_send.at[kind, k],
                                      gp_recv.at[kind, k], dev(q, t, s)))

    def grad_end(kind):
        total = grad_of(kind, p)
        for c in reduced[kind]:
            c.wait_recv()
        for k in range(1, TEAM):
            total = total + far[kind, k - 1].astype(F32)
        g_ref[kind] = total

    g_part[DOWN] = dot_r(hidden[...], dexp_all[...]).astype(BF16)
    grad_near(DOWN)
    weights_forward(DOWN)
    weights_wait(DOWN)
    outs = []
    for k in (1, 2, 3, 0):
        outs += scatter(OUT, k, dot(hidden[seat(mate(k)), :], w_all[DOWN]))
    grad_wide(DOWN)
    for c in range(width // chunk):
        cols = slice(c * chunk, (c + 1) * chunk)
        gs[...] = dot_t(dexp_all[...], w_all[DOWN, cols, :])

        def lower(r, carry):
            rr = pl.ds(pl.multiple_of(r * step, step), step)
            da = gs[rr, :]
            dg_s[rr, cols] = (da * dgu_s[rr, cols]).astype(BF16)
            du_s[rr, cols] = (da * ge_s[rr, cols]).astype(BF16)
            return carry

        lax.fori_loop(0, TEAM * rows // step, lower, 0)
    backs = []
    for k in (1, 2, 3, 0):
        u = seat(mate(k))
        backs += scatter(BACK, k, dot(dg_s[u, :], w_all[GATE]) + dot(du_s[u, :], w_all[UP]))
    g_part[GATE] = dot_r(dg_s[...], h_all[...]).astype(BF16)
    grad_near(GATE)
    g_part[UP] = dot_r(du_s[...], h_all[...]).astype(BF16)
    grad_near(UP)
    grad_wide(GATE)
    grad_wide(UP)

    upstream = dy_ref[...].astype(F32)
    probs = eprobs_s[...]
    _, cols = meta_of(t)
    picked = jnp.where((cols[:, 1:2] == lane_expert) | (cols[:, 2:3] == lane_expert), 1.0, 0.0)
    chosen = jnp.sum(probs * picked, axis=-1, keepdims=True)
    live = picked[:, 0:1] * jnp.where(cols[:, 0:1] >= 0.0, 1.0, 0.0)
    combine = probs[:, 0:1] * live / chosen
    expert = gathered(OUT, outs)
    result_ref[...] = (middle_s[...] + combine * expert).astype(BF16)
    d_combine = jnp.sum(expert * upstream, axis=-1, keepdims=True)
    first_hot = jnp.where(lane_expert == 0.0, 1.0, 0.0)
    ratio = probs[:, 0:1] / (chosen * chosen)
    d_probs = (d_combine * live) * (first_hot / chosen - ratio * picked)
    d_logits = probs * (d_probs - jnp.sum(d_probs * probs, axis=-1, keepdims=True))
    l_hi, l_lo = split_high(d_logits)
    l_lowest = (d_logits - l_hi.astype(F32) - l_lo.astype(F32)).astype(BF16)
    d_route = dot(l_hi, rhi[...]) + dot(l_hi, rlo[...]) + dot(l_lo, rhi[...])
    d_second = gathered(BACK, backs) + d_route
    middle = middle_s[...]
    scale = lax.rsqrt(jnp.mean(middle * middle, axis=-1, keepdims=True) + EPSILON)
    d_middle = upstream + norm_back(middle, scale, gain_two, d_second)
    dmid_s[...] = d_middle
    db_all[seat(t), :] = d_middle.astype(BF16)
    mine_b = db_all.at[seat(t), :]
    dbs = [send(mine_b, mine_b, t_send.at[DBRANCH, k], t_recv.at[DBRANCH, k], dev(p, mate(k), s)) for k in range(1, TEAM)]

    depth = sbuf.shape[0] // TEAM
    h2 = h_all[seat(t), :]
    sbuf[0:routed, :] = dot_r(l_hi, h2) + dot_r(l_lo, h2) + dot_r(l_lowest, h2)
    tail = lax.broadcasted_iota(jnp.int32, (sbuf.shape[0] - routed, width), 0)
    sbuf[routed:, :] = jnp.where(tail == 0, jnp.sum(d_second * middle * scale, axis=0, keepdims=True), 0.0)

    def piece(u):
        return pl.ds(pl.multiple_of(u * depth, depth), depth)

    first = [send(sbuf.at[piece(mate(k)), :], s_got.at[k - 1], sa_send.at[k], sa_recv.at[k], dev(p, mate(k), s))
             for k in range(1, TEAM)]

    score_s[...] = jnp.zeros(score_s.shape, F32)
    for k in range(TEAM):
        if k:
            dbs[k - 1].wait_recv()
        rows_u = seat(other(t, TEAM - k, TEAM))
        d_mix = dot_t(db_all[rows_u, :], w_all[ATTN, 3 * part:4 * part, :]).astype(BF16)
        q, key, v = q_all[rows_u, :], k_all[rows_u, :], v_all[rows_u, :]
        dq = jnp.zeros((rows, part), F32)
        dk = jnp.zeros((rows, part), F32)
        dv = jnp.zeros((rows, part), F32)
        for h in range(heads):
            weights = probs_all[h, rows_u, :]
            d_w = dot_t(jnp.where(lane_head == h, d_mix, zero_low), v)
            ds = (weights * (d_w - jnp.sum(weights * d_w, axis=-1, keepdims=True))).astype(BF16)
            dv = jnp.where(lane_head == h, dot_r(weights.astype(BF16), d_mix), dv)
            dq = jnp.where(lane_head == h, dot(ds, key), dq)
            dk = jnp.where(lane_head == h, dot_r(ds, q), dk)
            wide_ds = ds.astype(F32)
            score_s[h] = score_s[h] + wide_ds[:slots] + wide_ds[slots:]
        dq_all[rows_u, :] = (dq * factor).astype(BF16)
        dk_all[rows_u, :] = (dk * factor).astype(BF16)
        dv_all[rows_u, :] = dv.astype(BF16)

    g_part[ATTN, 3 * part:4 * part, :] = dot_r(mixed[...], db_all[...]).astype(BF16)
    g_part[ATTN, 0:part, :] = dot_r(dq_all[...], normed[...]).astype(BF16)
    g_part[ATTN, part:2 * part, :] = dot_r(dk_all[...], normed[...]).astype(BF16)
    g_part[ATTN, 2 * part:3 * part, :] = dot_r(dv_all[...], normed[...]).astype(BF16)
    grad_near(ATTN)
    norms = []
    gain_sum = jnp.zeros((1, width), F32)
    for k in (1, 2, 3, 0):
        u = mate(k)
        rows_u = seat(u)
        value = (dot(dq_all[rows_u, :], w_all[ATTN, 0:part, :]) + dot(dk_all[rows_u, :], w_all[ATTN, part:2 * part, :])
                 + dot(dv_all[rows_u, :], w_all[ATTN, 2 * part:3 * part, :]))
        norms += scatter(DNORM, k, value)
        gain_sum = gain_sum + jnp.sum(value * unit_of(u), axis=0, keepdims=True)
    grad_wide(ATTN)

    total = sbuf[piece(t), :]
    for c in first:
        c.wait_recv()
    for k in range(1, TEAM):
        total = total + s_got[k - 1]
    s_mine[...] = total
    s_sib[s] = total
    second_near = [send(s_mine, s_sib.at[s], sb_send.at[j], sb_recv.at[j], dev(p, t, other(s, j, sub)))
                   for j in range(1, sub)]

    def gather_gap(d, carry):
        hit = gap == d
        for h in range(heads):
            gap_s[h, pl.ds(d, 1), :] = jnp.sum(jnp.where(hit, score_s[h], 0.0), axis=0, keepdims=True)
        return carry

    lax.fori_loop(0, slots, gather_gap, 0)
    lane = lax.broadcasted_iota(jnp.int32, (slots, 128), 1)
    by_gap = jnp.zeros((slots, 128), F32)
    for h in range(heads):
        by_gap = jnp.where(lane == heads * t + h, jnp.sum(gap_s[h], axis=-1, keepdims=True), by_gap)
    count = table_ref.shape[1]
    bucket_hit = jnp.where(lax.broadcasted_iota(jnp.int32, (count, slots), 0) == buckets_ref[...], 1.0, 0.0)
    l_own[0:count, :] = jnp.dot(bucket_hit, by_gap, precision=HIGHEST, preferred_element_type=F32)
    for i in range(width // 128):
        l_own[count + i:count + i + 1, :] = gain_sum[:, i * 128:(i + 1) * 128]
    used = count + width // 128
    l_own[used:, :] = jnp.zeros((l_own.shape[0] - used, 128), F32)
    late_a = [send(l_own, l_got.at[k - 1], la_send.at[k], la_recv.at[k], dev(p, mate(k), s)) for k in range(1, TEAM)]

    for c in second_near:
        c.wait_recv()
    total = s_sib[0]
    for j in range(1, sub):
        total = total + s_sib[j]
    s_held[...] = total
    s_far[p] = total
    second_far = [send(s_held, s_far.at[p], sc_send.at[k], sc_recv.at[k], dev(other(p, k, TEAM), t, s))
                  for k in range(1, TEAM)]

    grad_end(DOWN)
    for c in late_a:
        c.wait_recv()
    total = l_own[...]
    for k in range(1, TEAM):
        total = total + l_got[k - 1]
    l_sum[...] = total
    l_sib[s] = total
    late_b = [send(l_sum, l_sib.at[s], lb_send.at[j], lb_recv.at[j], dev(p, t, other(s, j, sub))) for j in range(1, sub)]
    grad_end(GATE)
    for c in late_b:
        c.wait_recv()
    total = l_sib[0]
    for j in range(1, sub):
        total = total + l_sib[j]
    l_tot[...] = total
    l_far[p] = total
    late_c = [send(l_tot, l_far.at[p], lc_send.at[k], lc_recv.at[k], dev(other(p, k, TEAM), t, s)) for k in range(1, TEAM)]
    grad_end(UP)

    x = tok_ref[...].astype(F32)
    d_normed = gathered(DNORM, norms)
    scale = lax.rsqrt(jnp.mean(x * x, axis=-1, keepdims=True) + EPSILON)
    dtok_ref[...] = (dmid_s[...] + norm_back(x, scale, gain_one, d_normed)).astype(BF16)

    for c in second_far:
        c.wait_recv()
    total = s_far[0]
    for k in range(1, TEAM):
        total = total + s_far[k]
    small_ref[piece(t), :] = total
    mine_small = small_ref.at[piece(t), :]
    third = [send(mine_small, mine_small, sd_send.at[k], sd_recv.at[k], dev(p, mate(k), s)) for k in range(1, TEAM)]
    for c in late_c:
        c.wait_recv()
    total = l_far[0]
    for k in range(1, TEAM):
        total = total + l_far[k]
    late_ref[...] = total
    grad_end(ATTN)
    for c in third:
        c.wait_recv()
    for c in pending:
        c.wait_send()


def finish_kernel(routed, result_ref, dtok_ref, g_ref, small_ref, late_ref,
                  result_out, dtok_out, attn_out, gate_out, up_out, down_out, gains_out, table_out, router_out):
    result_out[...] = result_ref[...]
    dtok_out[...] = dtok_ref[...]
    attn_out[...] = g_ref[ATTN]
    gate_out[...] = g_ref[GATE]
    up_out[...] = g_ref[UP]
    down_out[...] = g_ref[DOWN]
    router_out[...] = small_ref[0:routed, :]
    heads, count = table_out.shape
    table_out[...] = late_ref[0:count, :].T[0:heads, :]
    gains_out[1:2, :] = small_ref[routed:routed + 1, :]
    for i in range(gains_out.shape[1] // 128):
        gains_out[0:1, i * 128:(i + 1) * 128] = late_ref[count + i:count + i + 1, :]


def block(n, tokens, attn_weight, w_gate, w_up, w_down, norm_gains, bias_table, router,
          grad_out, segment, expert_ids, bucket_of):
    rows, width = tokens.shape
    shard = w_down.shape[0]
    sub = n // (TEAM * TEAM)
    head_count = bias_table.shape[1]
    heads = head_count // TEAM
    part = heads * (width // head_count)
    slots = bucket_of.shape[0]
    routed = router.shape[1]
    every = TEAM * rows
    dma = pltpu.SemaphoreType.DMA
    shape = jax.ShapeDtypeStruct
    buf = pltpu.VMEM
    depth = -(-(routed + 1) // (8 * TEAM)) * 8
    lines = -(-(bias_table.shape[0] + width // 128) // 8) * 8
    smem = pl.BlockSpec(memory_space=pltpu.SMEM)
    result, dtok, grads, small, late = pl.pallas_call(
        functools.partial(block_kernel, n, head_count),
        out_shape=(shape(tokens.shape, BF16), shape(tokens.shape, BF16), shape((4, shard, width), F32),
                   shape((depth * TEAM, width), F32), shape((lines, 128), F32)),
        in_specs=[VMEM] * 11 + [smem] * 2,
        out_specs=(VMEM,) * 5,
        scratch_shapes=[
            buf((4, width, width), BF16), buf((4, width, width), BF16), buf((4, sub - 1, TEAM, shard, width), BF16),
            buf((4, TEAM - 1, shard, width), BF16), buf((4, TEAM - 1, shard, width), BF16),
            buf((every, width), BF16), buf((every, width), BF16), buf((TEAM * LINES, rows), F32), buf((every, width), BF16),
            buf((every, part), BF16), buf((every, part), BF16), buf((every, part), BF16), buf((every, part), BF16),
            buf((heads, every, rows), F32), buf((heads, slots, 2 * slots), F32),
            buf((4, TEAM - 1, rows, width), BF16), buf((4, TEAM - 1, rows, width), BF16), buf((4, rows, width), F32),
            buf((rows, width), F32), buf((every, width), BF16), buf((every, width), BF16), buf((rows, 128), F32),
            buf((rows, routed), F32), buf((routed, width), BF16), buf((routed, width), BF16),
            buf((every, 256), F32), buf((every, 256), F32), buf((every, width), BF16), buf((every, width), F32),
            buf((every, width), F32), buf((every, width), BF16), buf((every, width), BF16), buf((rows, width), F32),
            buf((every, width), BF16), buf((every, part), BF16), buf((every, part), BF16), buf((every, part), BF16),
            buf((heads, slots, 2 * slots), F32), buf((heads, slots, 2 * slots), F32),
            buf((depth * TEAM, width), F32), buf((TEAM - 1, depth, width), F32), buf((depth, width), F32),
            buf((sub, depth, width), F32), buf((depth, width), F32), buf((TEAM, depth, width), F32),
            buf((lines, 128), F32), buf((TEAM - 1, lines, 128), F32), buf((lines, 128), F32),
            buf((sub, lines, 128), F32), buf((lines, 128), F32), buf((TEAM, lines, 128), F32),
            dma((9, TEAM)), dma((9, TEAM)), dma((4, TEAM)), dma((4, TEAM)), dma((4, TEAM, sub)), dma((4, TEAM, sub)),
            dma((4, TEAM, sub)), dma((4, TEAM, sub)), dma((4, TEAM)), dma((4, TEAM)),
            dma((TEAM,)), dma((TEAM,)), dma((sub,)), dma((sub,)), dma((TEAM,)), dma((TEAM,)), dma((TEAM,)), dma((TEAM,)),
            dma((TEAM,)), dma((TEAM,)), dma((sub,)), dma((sub,)), dma((TEAM,)), dma((TEAM,)),
        ],
        compiler_params=pltpu.CompilerParams(collective_id=0, has_side_effects=True, vmem_limit_bytes=56 * 2**20),
        name="block",
    )(attn_weight.T, w_gate.T, w_up.T, w_down, tokens, grad_out, segment.reshape(1, rows), expert_ids.T, norm_gains,
      router.T, bucket_of.reshape(1, slots), bias_table.T, bucket_of)
    grad = shape((shard, width), F32)
    result, dtok, g_attn, g_gate, g_up, g_down, gains, table, routes = pl.pallas_call(
        functools.partial(finish_kernel, routed),
        out_shape=(shape(tokens.shape, BF16), shape(tokens.shape, BF16), grad, grad, grad, grad,
                   shape(norm_gains.shape, F32), shape(bias_table.shape[::-1], F32), shape(router.shape[::-1], F32)),
        in_specs=[VMEM] * 5,
        out_specs=(VMEM,) * 9,
        name="finish",
    )(result, dtok, grads, small, late)
    return result, dtok, g_attn.T, g_gate.T, g_up.T, g_down, gains, table.T, routes.T


def solution(mesh):
    n = mesh.shape["fsdp"]
    row, col = P("fsdp", None), P(None, "fsdp")
    in_specs = (row, col, col, col, row, P(), P(), P(), row, P("fsdp"), row, P())
    out_specs = (row, row, col, col, col, row, P(), P(), P())

    def run(*args):
        shard, rows = args[4].shape[0] // n, args[0].shape[0] // n
        whole_tiles = shard % 16 == 0 and rows == 2 * args[11].shape[0]
        return jax.shard_map(
            functools.partial(block if whole_tiles else body, n),
            mesh=mesh, in_specs=in_specs, out_specs=out_specs, check_vma=False,
        )(*args)

    return run
```

```python
import functools
import math
import jax
import jax.numpy as jnp
from jax import lax
from jax.experimental import pallas as pl
from jax.experimental.pallas import tpu as pltpu
from jax.sharding import PartitionSpec as P

EPSILON = 1e-06
HIGHEST = lax.Precision.HIGHEST
MESH = pl.DeviceIdType.MESH
TEAM = 4
F32 = jnp.float32
BF16 = jnp.bfloat16
VMEM = pl.BlockSpec(memory_space=pltpu.VMEM)
ANY = pl.BlockSpec(memory_space=pl.ANY)
CONTRACT_ROWS = (((0,), (0,)), ((), ()))
CONTRACT_COLS = (((1,), (1,)), ((), ()))


def place(n):
    sub = n // (TEAM * TEAM)
    me = lax.axis_index("fsdp")
    p = me // (TEAM * sub)
    t = lax.rem(me // sub, TEAM)
    s = lax.rem(me, sub)
    return sub, p, t, s, (lambda p, t, s: (p * (TEAM * sub) + t * sub + s,))


def greet(peers):
    barrier = pltpu.get_barrier_semaphore()
    for peer in peers:
        pl.semaphore_signal(barrier, inc=1, device_id=peer, device_id_type=MESH)
    pl.semaphore_wait(barrier, len(peers))


def remote(src, dst, send, recv, peer):
    return pltpu.make_async_remote_copy(
        src_ref=src, dst_ref=dst, send_sem=send, recv_sem=recv, device_id=peer, device_id_type=MESH
    )


def other(index, step, count):
    return lax.rem(index + step, count)


def spread_peers(sub, p, t, s, dev):
    peers = [dev(other(p, k, TEAM), t, s) for k in range(1, TEAM)]
    return peers + [dev(p, t, other(s, k, sub)) for k in range(1, sub)]


def team_peers(p, t, s, dev):
    return [dev(p, other(t, k, TEAM), s) for k in range(1, TEAM)]


def weights_start(n, w_ref, w_all, sems):
    sub, p, t, s, dev = place(n)
    p_send, p_recv, s_send, s_recv, own_sem = sems
    wide, near, local = [], [], []
    for i in range(w_ref.shape[0]):
        for k in range(1, TEAM):
            c = remote(w_ref.at[i], w_all.at[i, p, s], p_send.at[i, k], p_recv.at[i, k],
                       dev(other(p, k, TEAM), t, s))
            c.start()
            wide.append(c)
    for i in range(w_ref.shape[0]):
        for k in range(1, sub):
            c = remote(w_ref.at[i], w_all.at[i, p, s], s_send.at[i, 0, k], s_recv.at[i, 0, k],
                       dev(p, t, other(s, k, sub)))
            c.start()
            near.append(c)
        c = pltpu.make_async_copy(w_ref.at[i], w_all.at[i, p, s], own_sem.at[i])
        c.start()
        local.append(c)
    return wide, near, local


def weights_finish(n, w_all, sems, state):
    sub, p, t, s, dev = place(n)
    _, _, s_send, s_recv, _ = sems
    wide, near, local = state
    for i in range(w_all.shape[0]):
        for k in range(1, TEAM):
            wide[i * (TEAM - 1) + k - 1].wait_recv()
            q = other(p, TEAM - k, TEAM)
            for j in range(1, sub):
                c = remote(w_all.at[i, q, s], w_all.at[i, q, s], s_send.at[i, k, j], s_recv.at[i, k, j],
                           dev(p, t, other(s, j, sub)))
                c.start()
                near.append(c)
    for c in wide:
        c.wait_send()
    for c in near:
        c.wait()
    for c in local:
        c.wait()


def weights_sems(n, kinds):
    sub = n // (TEAM * TEAM)
    dma = pltpu.SemaphoreType.DMA
    return [dma((kinds, TEAM)), dma((kinds, TEAM)), dma((kinds, TEAM, sub)), dma((kinds, TEAM, sub)), dma((kinds,))]


def weights_shape(n, w):
    return jax.ShapeDtypeStruct((w.shape[0], TEAM, n // (TEAM * TEAM)) + w.shape[1:], w.dtype)


def gather_kernel(n, w_ref, tok_ref, dy_ref, meta_ref, w_all, tok_all, dy_all, meta_all,
                  t_send, t_recv, own_sem, *sems):
    sub, p, t, s, dev = place(n)
    greet(spread_peers(sub, p, t, s, dev) + team_peers(p, t, s, dev))
    state = weights_start(n, w_ref, w_all, sems)
    copies, local = [], []
    for i, (src, dst) in enumerate(((tok_ref, tok_all), (dy_ref, dy_all), (meta_ref, meta_all))):
        for k in range(1, TEAM):
            c = remote(src, dst.at[t], t_send.at[i, k], t_recv.at[i, k], dev(p, other(t, k, TEAM), s))
            c.start()
            copies.append(c)
        c = pltpu.make_async_copy(src, dst.at[t], own_sem.at[i])
        c.start()
        local.append(c)
    weights_finish(n, w_all, sems, state)
    for c in copies:
        c.wait()
    for c in local:
        c.wait()


def gather(n, w, tok, dy, meta):
    dma = pltpu.SemaphoreType.DMA
    shape = jax.ShapeDtypeStruct
    return pl.pallas_call(
        functools.partial(gather_kernel, n),
        out_shape=(
            weights_shape(n, w),
            shape((TEAM,) + tok.shape, BF16),
            shape((TEAM,) + dy.shape, BF16),
            shape((TEAM,) + meta.shape, jnp.int32),
        ),
        in_specs=[VMEM] * 4,
        out_specs=(ANY,) * 4,
        scratch_shapes=[dma((3, TEAM)), dma((3, TEAM)), dma((3,))] + weights_sems(n, w.shape[0]),
        compiler_params=pltpu.CompilerParams(collective_id=0, has_side_effects=True),
        name="gather_all",
    )(w, tok, dy, meta)


def middle_kernel(n, part_ref, x_ref, gain_ref, w_ref, y_ref, h_all, w_all, got, held,
                  a_send, a_recv, b_send, b_recv, own_sem, *sems):
    sub, p, t, s, dev = place(n)
    greet(spread_peers(sub, p, t, s, dev) + team_peers(p, t, s, dev))
    copies = []
    for k in range(1, TEAM):
        u = other(t, k, TEAM)
        c = remote(part_ref.at[u], got.at[k - 1], a_send.at[k], a_recv.at[k], dev(p, u, s))
        c.start()
        copies.append(c)
    state = weights_start(n, w_ref, w_all, sems)
    total = x_ref[...].astype(F32) + part_ref[t].astype(F32)
    for k in range(1, TEAM):
        copies[k - 1].wait_recv()
        total = total + got[k - 1].astype(F32)
    y_ref[...] = total
    scale = lax.rsqrt(jnp.mean(total * total, axis=-1, keepdims=True) + EPSILON)
    held[...] = (total * scale * gain_ref[1:2, :]).astype(BF16)
    local = pltpu.make_async_copy(held, h_all.at[t], own_sem)
    local.start()
    sends = []
    for k in range(1, TEAM):
        c = remote(held, h_all.at[t], b_send.at[k], b_recv.at[k], dev(p, other(t, k, TEAM), s))
        c.start()
        sends.append(c)
    weights_finish(n, w_all, sems, state)
    for c in copies:
        c.wait_send()
    for c in sends:
        c.wait()
    local.wait()


def middle_exchange(n, part, x, gains, w):
    dma = pltpu.SemaphoreType.DMA
    shape = jax.ShapeDtypeStruct
    return pl.pallas_call(
        functools.partial(middle_kernel, n),
        out_shape=(shape(x.shape, F32), shape((TEAM,) + x.shape, BF16), weights_shape(n, w)),
        in_specs=[VMEM] * 4,
        out_specs=(VMEM, ANY, ANY),
        scratch_shapes=[pltpu.VMEM((TEAM - 1,) + x.shape, BF16), pltpu.VMEM(x.shape, BF16),
                        dma((TEAM,)), dma((TEAM,)), dma((TEAM,)), dma((TEAM,)), dma] + weights_sems(n, w.shape[0]),
        compiler_params=pltpu.CompilerParams(collective_id=1, has_side_effects=True),
        name="middle_exchange",
    )(part, x, gains, w)


def reduce_kernel(n, m, h, gain_row, *refs):
    parts, rows, grad_ref = refs[:m], refs[m:m + h], refs[m + h]
    refs = refs[m + h + 1:]
    small = gain_row is not None
    if small:
        unit_ref, small_ref = refs[:2]
        refs = refs[2:]
    outs, rows_all, grad_out = refs[:m], refs[m:m + h], refs[m + h]
    if small:
        small_out = refs[m + h + 1]
        refs = refs[:m + h + 1] + refs[m + h + 2:]
    (got, sib, to_send, far, t_send, t_recv, h_send, h_recv, own_sem,
     s_send, s_recv, p_send, p_recv) = refs[m + h + 1:m + h + 14]
    rest = refs[m + h + 14:]
    sub, p, t, s, dev = place(n)
    greet(spread_peers(sub, p, t, s, dev) + team_peers(p, t, s, dev))
    kinds = grad_ref.shape[0]
    near, tokens, wide, shared, local = [], [], [], [], []
    for kind in range(kinds):
        for k in range(1, sub):
            v = other(s, k, sub)
            c = remote(grad_ref.at[kind, :, v], sib.at[kind, k - 1], s_send.at[kind, k], s_recv.at[kind, k],
                       dev(p, t, v))
            c.start()
            near.append(c)
    for i in range(h):
        for k in range(1, TEAM):
            c = remote(rows[i], rows_all[i].at[t], h_send.at[i, k], h_recv.at[i, k],
                       dev(p, other(t, k, TEAM), s))
            c.start()
            shared.append(c)
        c = pltpu.make_async_copy(rows[i], rows_all[i].at[t], own_sem.at[i])
        c.start()
        local.append(c)
    for i in range(m):
        for k in range(1, TEAM):
            u = other(t, k, TEAM)
            c = remote(parts[i].at[u], got.at[i, k - 1], t_send.at[i, k], t_recv.at[i, k], dev(p, u, s))
            c.start()
            tokens.append(c)
    for kind in range(kinds):
        for c in near[kind * (sub - 1):(kind + 1) * (sub - 1)]:
            c.wait_recv()
        for k in range(1, TEAM):
            q = other(p, k, TEAM)
            total = grad_ref[kind, q, s].astype(F32)
            for j in range(1, sub):
                total = total + sib[kind, j - 1, q].astype(F32)
            to_send[kind, k - 1] = total.astype(BF16)
            c = remote(to_send.at[kind, k - 1], far.at[kind, k - 1], p_send.at[kind, k], p_recv.at[kind, k],
                       dev(q, t, s))
            c.start()
            wide.append(c)
    for i in range(m):
        total = parts[i][t].astype(F32)
        for k in range(1, TEAM):
            tokens[i * (TEAM - 1) + k - 1].wait_recv()
            total = total + got[i, k - 1].astype(F32)
        outs[i][...] = total
    if small:
        buf = rest[0]
        piece, line = divmod(gain_row, small_ref.shape[1])
        gain = jnp.sum(outs[0][...] * unit_ref[...], axis=0, keepdims=True)
        buf[...] = small_ref[...]
        buf[piece, line:line + 1, :] = gain
        small_phases(n, buf, small_out, *rest[1:])
    for kind in range(kinds):
        for c in wide[kind * (TEAM - 1):(kind + 1) * (TEAM - 1)]:
            c.wait_recv()
        total = grad_ref[kind, p, s].astype(F32)
        for j in range(1, sub):
            total = total + sib[kind, j - 1, p].astype(F32)
        for k in range(1, TEAM):
            total = total + far[kind, k - 1].astype(F32)
        grad_out[kind] = total
    for c in near + tokens + wide:
        c.wait_send()
    for c in shared:
        c.wait()
    for c in local:
        c.wait()


def reduce_exchange(n, parts, rows, grads, ident, small=(), gain_row=None):
    sub = n // (TEAM * TEAM)
    m, h = len(parts), len(rows)
    dma = pltpu.SemaphoreType.DMA
    shape = jax.ShapeDtypeStruct
    block = parts[0].shape[1:] if m else (8, 128)
    kinds, tile = grads.shape[0], grads.shape[3:]
    outs = pl.pallas_call(
        functools.partial(reduce_kernel, n, m, h, gain_row),
        out_shape=(shape(block, F32),) * m
        + tuple(shape((TEAM,) + v.shape, v.dtype) for v in rows)
        + (shape((kinds,) + tile, F32),)
        + tuple(shape(v.shape, F32) for v in small[1:]),
        in_specs=[VMEM] * (m + h + 1 + len(small)),
        out_specs=(VMEM,) * m + (ANY,) * h + (VMEM,) * (1 + len(small[1:])),
        scratch_shapes=[
            pltpu.VMEM((max(m, 1), TEAM - 1) + block, BF16),
            pltpu.VMEM((kinds, sub - 1, TEAM) + tile, BF16),
            pltpu.VMEM((kinds, TEAM - 1) + tile, BF16),
            pltpu.VMEM((kinds, TEAM - 1) + tile, BF16),
            dma((max(m, 1), TEAM)), dma((max(m, 1), TEAM)),
            dma((max(h, 1), TEAM)), dma((max(h, 1), TEAM)), dma((max(h, 1),)),
            dma((kinds, sub)), dma((kinds, sub)), dma((kinds, TEAM)), dma((kinds, TEAM)),
        ] + (small_scratch(n, small[1].shape) if small else []),
        compiler_params=pltpu.CompilerParams(collective_id=ident, has_side_effects=True),
        name=f"reduce_{ident}",
    )(*parts, *rows, grads, *small)
    return (outs[:m], outs[m:m + h]) + tuple(outs[m + h:])


def small_phases(n, buf, out_ref, got, mine, sib, held, far,
                 a_send, a_recv, s_send, s_recv, b_send, b_recv, c_send, c_recv):
    sub, p, t, s, dev = place(n)
    first, near, second, third = [], [], [], []
    for k in range(1, TEAM):
        u = other(t, k, TEAM)
        c = remote(buf.at[u], got.at[k - 1], a_send.at[k], a_recv.at[k], dev(p, u, s))
        c.start()
        first.append(c)
    total = buf[t]
    for k in range(1, TEAM):
        first[k - 1].wait_recv()
        total = total + got[k - 1]
    mine[...] = total
    sib[s] = total
    for k in range(1, sub):
        c = remote(mine, sib.at[s], s_send.at[k], s_recv.at[k], dev(p, t, other(s, k, sub)))
        c.start()
        near.append(c)
    for c in near:
        c.wait_recv()
    total = sib[0]
    for k in range(1, sub):
        total = total + sib[k]
    held[...] = total
    far[p] = total
    for k in range(1, TEAM):
        c = remote(held, far.at[p], b_send.at[k], b_recv.at[k], dev(other(p, k, TEAM), t, s))
        c.start()
        second.append(c)
    for c in second:
        c.wait_recv()
    total = far[0]
    for k in range(1, TEAM):
        total = total + far[k]
    out_ref[t] = total
    for k in range(1, TEAM):
        c = remote(out_ref.at[t], out_ref.at[t], c_send.at[k], c_recv.at[k], dev(p, other(t, k, TEAM), s))
        c.start()
        third.append(c)
    for c in first + near + second:
        c.wait_send()
    for c in third:
        c.wait()


def small_scratch(n, shape):
    sub = n // (TEAM * TEAM)
    dma = pltpu.SemaphoreType.DMA
    tile = shape[1:]
    return [pltpu.VMEM(shape, F32), pltpu.VMEM((TEAM - 1,) + tile, F32), pltpu.VMEM(tile, F32),
            pltpu.VMEM((sub,) + tile, F32), pltpu.VMEM(tile, F32), pltpu.VMEM((TEAM,) + tile, F32),
            dma((TEAM,)), dma((TEAM,)), dma((sub,)), dma((sub,))] + [dma((TEAM,))] * 4


def gelu_tanh(inner):
    return jax.nn.gelu(inner, approximate=True)


def norm_back(inputs, scale, gain, upstream):
    weighted = gain * upstream
    return scale * weighted - inputs * scale * scale * scale * jnp.mean(
        weighted * inputs, axis=-1, keepdims=True
    )


def dot_t(a, b):
    return lax.dot_general(a, b, CONTRACT_COLS, preferred_element_type=F32)


def dot_r(a, b):
    return lax.dot_general(a, b, CONTRACT_ROWS, preferred_element_type=F32)


def dot(a, b):
    return jnp.dot(a, b, preferred_element_type=F32)


def body(n, tokens, attn_weight, w_gate, w_up, w_down, norm_gains, bias_table, router,
         grad_out, segment, expert_ids, bucket_of):
    rows, width = tokens.shape
    slots = bucket_of.shape[0]
    routed = router.shape[1]
    buckets, head_count = bias_table.shape
    head_width = width // head_count
    factor = head_width ** (-0.5)
    heads = head_count // TEAM
    part = heads * head_width
    sub, _, t, _, _ = place(n)
    all_rows = TEAM * rows
    spans = all_rows // slots

    early = jnp.stack([attn_weight.T, w_down])
    late = jnp.stack([w_gate.T, w_up.T])
    meta = jnp.concatenate([segment[None], expert_ids.T, jnp.zeros((5, rows), jnp.int32)], axis=0)
    w_all, tok_all, dy_all, meta_all = gather(n, early, tokens, grad_out, meta)
    w_all = w_all.reshape(2, -1, width)
    attn_t, down = w_all[0], w_all[1]
    qkv_t, out_t = attn_t[: 3 * part], attn_t[3 * part :]
    inputs = tok_all.reshape(all_rows, width).astype(F32)
    segments = meta_all[:, 0, :].reshape(all_rows)
    id_a = meta_all[:, 1, :].reshape(all_rows)
    id_b = meta_all[:, 2, :].reshape(all_rows)

    places = jnp.arange(slots)
    gap = places[:, None] - places[None, :]
    causal = gap >= 0
    gap_hit = (gap[:, :, None] == places[None, None, :]).astype(F32)
    bucket_hit = (bucket_of[:, None] == jnp.arange(buckets)[None, :]).astype(F32)
    table_mine = lax.dynamic_slice(bias_table, (0, heads * t), (buckets, heads))
    by_gap = jnp.dot(bucket_hit, table_mine, precision=HIGHEST)
    offsets = jnp.einsum("ijd,dh->hij", gap_hit, by_gap, precision=HIGHEST)

    scale_one = lax.rsqrt(jnp.mean(inputs * inputs, axis=-1, keepdims=True) + EPSILON)
    normed = (inputs * scale_one * norm_gains[0]).astype(BF16)
    triple = dot_t(normed, qkv_t).astype(BF16)
    heads_of = lambda v: v.reshape(spans, slots, heads, head_width)
    query = heads_of(triple[:, :part])
    keyset = heads_of(triple[:, part : 2 * part])
    valueset = heads_of(triple[:, 2 * part :])
    seg = segments.reshape(spans, slots)
    allowed = (seg[:, :, None] == seg[:, None, :]) & causal[None]
    raw = jnp.einsum("bihd,bjhd->bhij", query, keyset, preferred_element_type=F32)
    scores = jnp.where(allowed[:, None], raw * factor + offsets[None], -1e30)
    peak = jnp.max(scores, axis=-1, keepdims=True)
    lifted_scores = jnp.exp(scores - peak)
    weights = lifted_scores / jnp.sum(lifted_scores, axis=-1, keepdims=True)
    weights_low = weights.astype(BF16)
    mixed = jnp.einsum("bhij,bjhd->bihd", weights_low, valueset, preferred_element_type=F32)
    mixed = mixed.reshape(all_rows, part).astype(BF16)
    branch = dot(mixed, out_t).astype(BF16).reshape(TEAM, rows, width)
    middle, second_all, late_all = middle_exchange(n, branch, tokens, norm_gains, late)
    late_all = late_all.reshape(2, -1, width)
    gate_t, up_t = late_all[0], late_all[1]
    second_all = second_all.reshape(all_rows, width)

    second_wide = second_all.astype(F32)
    probs_all = jax.nn.softmax(jnp.dot(second_wide, router, precision=HIGHEST), axis=-1)
    lanes = jnp.arange(routed)[None, :]
    picked_all = jnp.where((id_a[:, None] == lanes) | (id_b[:, None] == lanes), 1.0, 0.0)
    total_all = jnp.sum(probs_all * picked_all, axis=-1)
    live_all = picked_all[:, 0] * jnp.where(segments >= 0, 1.0, 0.0)
    combine_all = probs_all[:, 0] * live_all / total_all
    gated = dot_t(second_all, gate_t)
    lifted = dot_t(second_all, up_t)
    activated, gelu_back = jax.vjp(gelu_tanh, gated)
    hidden = (activated * lifted).astype(BF16)
    out_part = dot(hidden, down).astype(BF16).reshape(TEAM, rows, width)
    d_expert = (combine_all[:, None] * dy_all.reshape(all_rows, width).astype(F32)).astype(BF16)
    d_hidden = dot_t(d_expert, down)
    d_gated = gelu_back(d_hidden * lifted)[0].astype(BF16)
    d_lifted = (d_hidden * activated).astype(BF16)
    back_part = (dot(d_gated, gate_t) + dot(d_lifted, up_t)).astype(BF16).reshape(TEAM, rows, width)
    grad_ffn = jnp.stack(
        [dot_r(d_gated, second_all).astype(BF16), dot_r(d_lifted, second_all).astype(BF16)]
    ).reshape(2, TEAM, sub, -1, width)
    (expert_out, d_second), _, g_ffn = reduce_exchange(n, (out_part, back_part), (), grad_ffn, 2)
    grad_down = dot_r(hidden, d_expert).astype(BF16).reshape(1, TEAM, sub, -1, width)

    mine = lambda v: lax.dynamic_slice_in_dim(v, t * rows, rows, 0)
    second, probs, picked = mine(second_wide), mine(probs_all), mine(picked_all)
    chosen_total, live, combine = mine(total_all), mine(live_all), mine(combine_all)
    upstream = grad_out.astype(F32)
    result = (middle + combine[:, None] * expert_out).astype(BF16)
    d_combine = jnp.sum(expert_out * upstream, axis=-1)
    first_hot = jnp.where(jnp.arange(routed) == 0, 1.0, 0.0)
    ratio = probs[:, 0] / (chosen_total * chosen_total)
    d_probs = (d_combine * live)[:, None] * (
        first_hot[None, :] / chosen_total[:, None] - ratio[:, None] * picked
    )
    d_logits = probs * (d_probs - jnp.sum(d_probs * probs, axis=-1, keepdims=True))
    grad_router_t = lax.dot_general(d_logits, second, CONTRACT_ROWS, precision=HIGHEST)
    d_second = d_second + jnp.dot(d_logits, router.T, precision=HIGHEST)
    scale_two = lax.rsqrt(jnp.mean(middle * middle, axis=-1, keepdims=True) + EPSILON)
    gain_two = jnp.sum(d_second * middle * scale_two, axis=0)
    d_middle = upstream + norm_back(middle, scale_two, norm_gains[1], d_second)
    _, (d_branch,), g_down = reduce_exchange(n, (), (d_middle.astype(BF16),), grad_down, 3)
    d_branch = d_branch.reshape(all_rows, width)

    grad_out_t = dot_r(mixed, d_branch)
    d_mixed = heads_of(dot_t(d_branch, out_t).astype(BF16))
    d_weights = jnp.einsum("bihd,bjhd->bhij", d_mixed, valueset, preferred_element_type=F32)
    d_values = jnp.einsum("bhij,bihd->bjhd", weights_low, d_mixed, preferred_element_type=F32)
    d_scores = weights * (d_weights - jnp.sum(weights * d_weights, axis=-1, keepdims=True))
    d_scores = d_scores.astype(BF16)
    d_query = jnp.einsum("bhij,bjhd->bihd", d_scores, keyset, preferred_element_type=F32) * factor
    d_keys = jnp.einsum("bhij,bihd->bjhd", d_scores, query, preferred_element_type=F32) * factor
    score_sum = jnp.sum(d_scores.astype(F32), axis=0)
    gap_sum = jnp.einsum("hij,ijd->dh", score_sum, gap_hit, precision=HIGHEST)
    table_part = lax.dot_general(bucket_hit, gap_sum, CONTRACT_ROWS, precision=HIGHEST)
    grad_table = lax.dynamic_update_slice(jnp.zeros(bias_table.shape, F32), table_part, (0, heads * t))
    flat = lambda v: v.reshape(all_rows, part).astype(BF16)
    d_triple = jnp.concatenate([flat(d_query), flat(d_keys), flat(d_values)], axis=1)
    grad_in_t = dot_r(d_triple, normed)
    grad_attn = jnp.concatenate([grad_in_t, grad_out_t], axis=0).astype(BF16)
    grad_attn = grad_attn.reshape(1, TEAM, sub, -1, width)
    d_normed_part = dot(d_triple, qkv_t).astype(BF16).reshape(TEAM, rows, width)
    own_inputs = tokens.astype(F32)
    own_scale = mine(scale_one)
    table_flat = grad_table.reshape(-1)
    lines = -(-table_flat.shape[0] // width)
    table_rows = jnp.pad(table_flat, (0, lines * width - table_flat.shape[0])).reshape(lines, width)
    small = jnp.concatenate([grad_router_t, jnp.zeros((1, width), F32), gain_two[None], table_rows], axis=0)
    depth = -(-small.shape[0] // (8 * TEAM)) * 8
    small = jnp.pad(small, ((0, depth * TEAM - small.shape[0]), (0, 0))).reshape(TEAM, depth, width)
    (d_normed,), _, g_attn, small = reduce_exchange(
        n, (d_normed_part,), (), grad_attn, 4, (own_inputs * own_scale, small), routed
    )
    small = small.reshape(TEAM * depth, width)
    input_grad = (d_middle + norm_back(own_inputs, own_scale, norm_gains[0], d_normed)).astype(BF16)
    grad_router = small[:routed].T
    grad_gains = small[routed : routed + 2]
    grad_table = small[routed + 2 : routed + 2 + lines].reshape(-1)[: table_flat.shape[0]].reshape(bias_table.shape)
    return (result, input_grad, g_attn[0].T, g_ffn[0].T, g_ffn[1].T, g_down[0],
            grad_gains, grad_table, grad_router)


LINES = 8
TOK, DY, META, BRANCH, SECOND, OUT, BACK, DBRANCH, DNORM = range(9)
ATTN, GATE, UP, DOWN = range(4)


def split_high(v):
    high = v.astype(BF16)
    return high, (v - high.astype(F32)).astype(BF16)


def eye(size, dtype):
    row = lax.broadcasted_iota(jnp.int32, (size, size), 0)
    col = lax.broadcasted_iota(jnp.int32, (size, size), 1)
    return jnp.where(row == col, 1.0, 0.0).astype(dtype)


def block_kernel(
    n, head_count,
    attn_ref, gate_ref, up_ref, down_ref, tok_ref, dy_ref, seg_ref, ids_ref, gains_ref, router_ref,
    buckets_ref, table_ref, bucket_ref,
    result_ref, dtok_ref, g_ref, small_ref, late_ref,
    w_all, g_part, sib, to_send, far, hop,
    tok_all, dy_all, meta_all, normed, q_all, k_all, v_all, mixed, probs_all, offs,
    row_send, row_got, own_part, middle_s, h_all, dexp_all, coef_s, eprobs_s, rhi, rlo,
    gs, us, hidden, ge_s, dgu_s, dg_s, du_s, dmid_s, db_all, dq_all, dk_all, dv_all, score_s, gap_s,
    sbuf, s_got, s_held, s_far, l_own, l_got, l_sum, l_sib, l_tot, l_far,
    t_send, t_recv, z_send, z_recv, ws_send, ws_recv, gs_send, gs_recv, gp_send, gp_recv, hp_send, hp_recv,
    sa_send, sa_recv, sc_send, sc_recv, sd_send, sd_recv,
    la_send, la_recv, lb_send, lb_recv, lc_send, lc_recv,
):
    sub, p, t, s, dev = place(n)
    rows, width = tok_ref.shape
    shard = down_ref.shape[0]
    heads = head_count // TEAM
    head_width = width // head_count
    part = heads * head_width
    factor = head_width ** (-0.5)
    slots = buckets_ref.shape[1]
    routed = router_ref.shape[0]
    chunk = 256

    barrier = pltpu.get_barrier_semaphore()
    ring = [(a, b) for a in range(TEAM) for b in range(sub)][1:]
    plane = [dev(p, other(t, a, TEAM), other(s, b, sub)) for a, b in ring]
    peers = plane + [dev(other(p, k, TEAM), t, s) for k in range(1, TEAM)]
    for peer in peers:
        pl.semaphore_signal(barrier, inc=1, device_id=peer, device_id_type=MESH)

    def mate(k):
        return other(t, k, TEAM)

    def seat(u):
        return pl.ds(pl.multiple_of(u * rows, rows), rows)

    def lot(q, v):
        return pl.ds(pl.multiple_of((q * sub + v) * shard, shard), shard)

    pending = []
    waited = [0]

    def drain(upto):
        for where, c in pending[waited[0]:upto]:
            if where is None:
                c.wait_send()
            else:
                pl.when(where)(c.wait_send)
        waited[0] = upto

    def send(src, dst, ssem, rsem, peer, where=None):
        c = remote(src, dst, ssem, rsem, peer)
        if where is None:
            c.start()
        else:
            pl.when(where)(c.start)
        pending.append((where, c))
        return c

    def share(kind, src, whole):
        return [send(src, whole.at[seat(t)], t_send.at[kind, k], t_recv.at[kind, k], dev(p, mate(k), s))
                for k in range(1, TEAM)]

    w_all[ATTN, lot(p, s), :] = attn_ref[...]
    tok_all[seat(t), :] = tok_ref[...]
    dy_all[seat(t), :] = dy_ref[...]
    ids = ids_ref[...].astype(F32)
    line = lax.broadcasted_iota(jnp.int32, (LINES, rows), 0)
    meta_all[pl.ds(pl.multiple_of(t * LINES, LINES), LINES), :] = jnp.where(
        line == 0, seg_ref[...].astype(F32), jnp.where(line == 1, ids[0:1, :], jnp.where(line == 2, ids[1:2, :], 0.0))
    )
    pl.semaphore_wait(barrier, len(peers))

    wide = {}

    inner = (p == 1) | (p == 2)

    def weights_send(kind):
        mine = w_all.at[kind, lot(p, s), :]
        wide[kind] = {k: send(mine, mine, z_send.at[kind, k], z_recv.at[kind, k], dev(other(p, k, TEAM), t, s), where)
                      for k, where in ((2, None), (1, p < TEAM - 1), (3, p > 0))}
        wide[kind, "near"] = [send(mine, mine, ws_send.at[kind, 0, j], ws_recv.at[kind, 0, j], dev(p, t, other(s, j, sub)))
                              for j in range(1, sub)]

    def weights_arrive(kind, k):
        wide[kind][k].wait_recv()
        block = w_all.at[kind, lot(other(p, TEAM - k, TEAM), s), :]
        if k == 2:
            edge = p // 2
            send(block, block, z_send.at[kind, 0], z_recv.at[kind, 1 + 2 * edge], dev(3 * edge, t, s), inner)
        wide[kind, "near"] += [
            send(block, block, ws_send.at[kind, k, j], ws_recv.at[kind, k, j], dev(p, t, other(s, j, sub)))
            for j in range(1, sub)]

    def weights_forward(kind):
        weights_arrive(kind, 1)
        weights_arrive(kind, 3)

    def weights_wait(kind):
        for c in wide[kind, "near"]:
            c.wait_recv()

    mine_meta = meta_all.at[pl.ds(pl.multiple_of(t * LINES, LINES), LINES), :]
    metas = [send(mine_meta, mine_meta, t_send.at[META, k], t_recv.at[META, k], dev(p, mate(k), s)) for k in range(1, TEAM)]
    toks = share(TOK, tok_ref, tok_all)
    weights_send(ATTN)
    dys = share(DY, dy_ref, dy_all)

    w_all[GATE, lot(p, s), :] = gate_ref[...]
    w_all[UP, lot(p, s), :] = up_ref[...]
    w_all[DOWN, lot(p, s), :] = down_ref[...]
    rhi[...], rlo[...] = split_high(router_ref[...])

    place_r = lax.broadcasted_iota(jnp.int32, (slots, 2 * slots), 0)
    place_c = lax.rem(lax.broadcasted_iota(jnp.int32, (slots, 2 * slots), 1), slots)
    gap = place_r - place_c
    offs[...] = jnp.zeros(offs.shape, F32)

    def spread_bias(d, carry):
        hit = gap == d
        for h in range(heads):
            offs[h] = jnp.where(hit, table_ref[heads * t + h, bucket_ref[d]], offs[h])
        return carry

    lax.fori_loop(0, slots, spread_bias, 0)

    row_i = lax.broadcasted_iota(jnp.int32, (rows, rows), 0)
    col_i = lax.broadcasted_iota(jnp.int32, (rows, rows), 1)
    causal = (row_i >= col_i) & ((row_i // slots) == (col_i // slots))
    lane_head = lax.broadcasted_iota(jnp.int32, (rows, part), 1) // head_width
    gain_one, gain_two = gains_ref[0:1, :], gains_ref[1:2, :]
    zero_low = jnp.zeros((rows, part), BF16)

    def meta_of(u):
        lines = meta_all[pl.ds(pl.multiple_of(u * LINES, LINES), LINES), :]
        return lines, dot_t(eye(rows, F32), lines)

    def unit_of(u):
        x = tok_all[seat(u), :].astype(F32)
        return x * lax.rsqrt(jnp.mean(x * x, axis=-1, keepdims=True) + EPSILON)

    def attend(u):
        rows_u = seat(u)
        h1 = (unit_of(u) * gain_one).astype(BF16)
        normed[rows_u, :] = h1
        q = dot_t(h1, w_all[ATTN, 0:part, :]).astype(BF16)
        key = dot_t(h1, w_all[ATTN, part:2 * part, :]).astype(BF16)
        v = dot_t(h1, w_all[ATTN, 2 * part:3 * part, :]).astype(BF16)
        q_all[rows_u, :], k_all[rows_u, :], v_all[rows_u, :] = q, key, v
        lines, cols = meta_of(u)
        allowed = (cols[:, 0:1] == lines[0:1, :]) & causal
        mix = jnp.zeros((rows, part), F32)
        for h in range(heads):
            raw = dot_t(jnp.where(lane_head == h, q, zero_low), key)
            scores = jnp.where(allowed, raw * factor + jnp.concatenate([offs[h], offs[h]], axis=0), -1e30)
            lifted = jnp.exp(scores - jnp.max(scores, axis=-1, keepdims=True))
            weights = lifted / jnp.sum(lifted, axis=-1, keepdims=True)
            probs_all[h, rows_u, :] = weights
            mix = jnp.where(lane_head == h, dot(weights.astype(BF16), v), mix)
        low = mix.astype(BF16)
        mixed[rows_u, :] = low
        return dot(low, w_all[ATTN, 3 * part:4 * part, :])

    slot = {BRANCH: 0, OUT: 1, BACK: 2, DNORM: 3}

    def scatter(kind, k, value):
        i = slot[kind]
        if k == 0:
            own_part[i] = value
            return []
        row_send[i, k - 1] = value.astype(BF16)
        return [send(row_send.at[i, k - 1], row_got.at[i, k - 1], t_send.at[kind, k], t_recv.at[kind, k],
                     dev(p, mate(k), s))]

    def gathered(kind, copies):
        total = own_part[slot[kind]]
        for c in copies:
            c.wait_recv()
        for k in range(1, TEAM):
            total = total + row_got[slot[kind], k - 1].astype(F32)
        return total

    weights_arrive(ATTN, 2)
    weights_send(GATE)
    weights_forward(ATTN)
    weights_send(UP)
    weights_wait(ATTN)
    branch = []
    for k in range(TEAM):
        if k:
            metas[k - 1].wait_recv()
            toks[k - 1].wait_recv()
        branch += scatter(BRANCH, (TEAM - k) % TEAM, attend(other(t, TEAM - k, TEAM)))
    weights_arrive(GATE, 2)
    weights_send(DOWN)

    middle = tok_ref[...].astype(F32) + gathered(BRANCH, branch)
    middle_s[...] = middle
    scale = lax.rsqrt(jnp.mean(middle * middle, axis=-1, keepdims=True) + EPSILON)
    h_all[seat(t), :] = (middle * scale * gain_two).astype(BF16)
    mine_h = h_all.at[seat(t), :]
    seconds = [send(mine_h, mine_h, t_send.at[SECOND, k], t_recv.at[SECOND, k], dev(p, mate(k), s)) for k in range(1, TEAM)]

    lane_expert = lax.broadcasted_iota(jnp.int32, (rows, routed), 1).astype(F32)

    def route(u):
        h2 = h_all[seat(u), :]
        logits = dot_t(h2, rhi[...]) + dot_t(h2, rlo[...])
        lifted = jnp.exp(logits - jnp.max(logits, axis=-1, keepdims=True))
        probs = lifted / jnp.sum(lifted, axis=-1, keepdims=True)
        _, cols = meta_of(u)
        picked = jnp.where((cols[:, 1:2] == lane_expert) | (cols[:, 2:3] == lane_expert), 1.0, 0.0)
        chosen = jnp.sum(probs * picked, axis=-1, keepdims=True)
        live = picked[:, 0:1] * jnp.where(cols[:, 0:1] >= 0.0, 1.0, 0.0)
        combine = probs[:, 0:1] * live / chosen
        dexp_all[seat(u), :] = (combine * dy_all[seat(u), :].astype(F32)).astype(BF16)
        return probs, picked, chosen, live, combine

    weights_forward(GATE)
    weights_arrive(UP, 2)
    eprobs_s[...] = route(t)[0]
    for k in range(1, TEAM):
        dys[k - 1].wait_recv()
        seconds[k - 1].wait_recv()
        route(other(t, TEAM - k, TEAM))

    weights_forward(UP)
    weights_wait(GATE)
    weights_wait(UP)
    k0 = (2.0 / math.pi) ** 0.5
    k1 = 0.044715
    step = 32
    for c in range(width // chunk):
        cols = slice(c * chunk, (c + 1) * chunk)
        gs[...] = dot_t(h_all[...], w_all[GATE, cols, :])
        us[...] = dot_t(h_all[...], w_all[UP, cols, :])

        def lift(r, carry):
            rr = pl.ds(pl.multiple_of(r * step, step), step)
            g, u = gs[rr, :], us[rr, :]
            square = g * g
            bend = jnp.tanh(k0 * g * (1.0 + k1 * square))
            half = 0.5 * (1.0 + bend)
            act = g * half
            slope = half + 0.5 * g * (1.0 - bend * bend) * (k0 * (1.0 + 3.0 * k1 * square))
            hidden[rr, cols] = (act * u).astype(BF16)
            ge_s[rr, cols] = act
            dgu_s[rr, cols] = slope * u
            return carry

        lax.fori_loop(0, TEAM * rows // step, lift, 0)

    near = {}

    def grad_near(kind, q):
        near[kind, q] = [
            send(g_part.at[kind, lot(q, other(s, j, sub)), :], sib.at[kind, j - 1, q], gs_send.at[kind, q, j],
                 gs_recv.at[kind, q, j], dev(p, t, other(s, j, sub)))
            for j in range(1, sub)]

    def grad_of(kind, q):
        total = g_part[kind, lot(q, s), :].astype(F32)
        for j in range(1, sub):
            total = total + sib[kind, j - 1, q].astype(F32)
        return total

    def to_owner(kind, q, where):
        send(to_send.at[kind, q], far.at[kind, p], gp_send.at[kind, q], gp_recv.at[kind, p], dev(q, t, s), where)

    def hop_of(kind, q):
        return remote(to_send.at[kind, q], hop.at[kind], hp_send.at[kind], hp_recv.at[kind], dev(2 - q // 2, t, s))

    def grad_push(kind, q):
        for c in near[kind, q]:
            c.wait_recv()

        @pl.when(p != q)
        def _():
            to_send[kind, q] = grad_of(kind, q).astype(BF16)

        if q in (0, 3):
            next_to, end = (1, 3) if q == 0 else (2, 0)
            c = hop_of(kind, q)
            pl.when(p == end)(c.start)
            pending.append((p == end, c))
            to_owner(kind, q, p == next_to)
        else:
            to_owner(kind, q, p != q)

    def grad_relay(kind, q):
        through = 2 if q == 0 else 1

        @pl.when(p == through)
        def _():
            hop_of(kind, q).wait_recv()
            to_send[kind, q] = (grad_of(kind, q) + hop[kind].astype(F32)).astype(BF16)

        to_owner(kind, q, p == through)

    def grad_relays(kind):
        grad_relay(kind, 0)
        grad_relay(kind, 3)

    def grad_all_near(kind):
        for q in range(TEAM):
            grad_near(kind, q)

    def grad_wide(kind):
        for q in (0, 3, 1, 2):
            grad_push(kind, q)

    def grad_end(kind):
        g_ref[kind] = grad_of(kind, p)
        for q in range(TEAM):
            @pl.when((p != q) & (p + q != 3 if q in (0, 3) else p != q))
            def _():
                remote(to_send.at[kind, q], far.at[kind, q], gp_send.at[kind, q], gp_recv.at[kind, q], dev(q, t, s)).wait_recv()
                g_ref[kind] += far[kind, q].astype(F32)

    weights_arrive(DOWN, 2)
    g_part[DOWN] = dot_r(hidden[...], dexp_all[...]).astype(BF16)
    grad_all_near(DOWN)
    weights_forward(DOWN)
    weights_wait(DOWN)
    mark_down = len(pending)
    outs = []
    for k in (1, 2, 3, 0):
        outs += scatter(OUT, k, dot(hidden[seat(mate(k)), :], w_all[DOWN]))
    grad_wide(DOWN)
    for c in range(width // chunk):
        cols = slice(c * chunk, (c + 1) * chunk)
        gs[...] = dot_t(dexp_all[...], w_all[DOWN, cols, :])

        def lower(r, carry):
            rr = pl.ds(pl.multiple_of(r * step, step), step)
            da = gs[rr, :]
            dg_s[rr, cols] = (da * dgu_s[rr, cols]).astype(BF16)
            du_s[rr, cols] = (da * ge_s[rr, cols]).astype(BF16)
            return carry

        lax.fori_loop(0, TEAM * rows // step, lower, 0)
    backs = []
    for k in (1, 2, 3, 0):
        u = seat(mate(k))
        backs += scatter(BACK, k, dot(dg_s[u, :], w_all[GATE]) + dot(du_s[u, :], w_all[UP]))
    g_part[GATE] = dot_r(dg_s[...], h_all[...]).astype(BF16)
    grad_all_near(GATE)
    g_part[UP] = dot_r(du_s[...], h_all[...]).astype(BF16)
    grad_all_near(UP)
    grad_wide(GATE)
    grad_wide(UP)
    grad_relays(DOWN)

    upstream = dy_ref[...].astype(F32)
    probs = eprobs_s[...]
    _, cols = meta_of(t)
    picked = jnp.where((cols[:, 1:2] == lane_expert) | (cols[:, 2:3] == lane_expert), 1.0, 0.0)
    chosen = jnp.sum(probs * picked, axis=-1, keepdims=True)
    live = picked[:, 0:1] * jnp.where(cols[:, 0:1] >= 0.0, 1.0, 0.0)
    combine = probs[:, 0:1] * live / chosen
    mark_out = len(pending)
    expert = gathered(OUT, outs)
    result_ref[...] = (middle_s[...] + combine * expert).astype(BF16)
    d_combine = jnp.sum(expert * upstream, axis=-1, keepdims=True)
    first_hot = jnp.where(lane_expert == 0.0, 1.0, 0.0)
    ratio = probs[:, 0:1] / (chosen * chosen)
    d_probs = (d_combine * live) * (first_hot / chosen - ratio * picked)
    d_logits = probs * (d_probs - jnp.sum(d_probs * probs, axis=-1, keepdims=True))
    l_hi, l_lo = split_high(d_logits)
    l_lowest = (d_logits - l_hi.astype(F32) - l_lo.astype(F32)).astype(BF16)
    d_route = dot(l_hi, rhi[...]) + dot(l_hi, rlo[...]) + dot(l_lo, rhi[...])
    depth = sbuf.shape[0] // (TEAM * sub)
    h2 = h_all[seat(t), :]
    sbuf[...] = dot_r(l_hi, h2) + dot_r(l_lo, h2) + dot_r(l_lowest, h2)

    def piece(a, b):
        return pl.ds(pl.multiple_of((other(t, a, TEAM) * sub + other(s, b, sub)) * depth, depth), depth)

    first = [send(sbuf.at[piece(a, b), :], s_got.at[i], sa_send.at[i], sa_recv.at[i], plane[i]) for i, (a, b) in enumerate(ring)]
    drain(mark_down)
    grad_relays(GATE)
    d_second = gathered(BACK, backs) + d_route
    middle = middle_s[...]
    scale = lax.rsqrt(jnp.mean(middle * middle, axis=-1, keepdims=True) + EPSILON)
    d_middle = upstream + norm_back(middle, scale, gain_two, d_second)
    dmid_s[...] = d_middle
    db_all[seat(t), :] = d_middle.astype(BF16)
    mine_b = db_all.at[seat(t), :]
    dbs = [send(mine_b, mine_b, t_send.at[DBRANCH, k], t_recv.at[DBRANCH, k], dev(p, mate(k), s)) for k in range(1, TEAM)]

    total = sbuf[piece(0, 0), :]
    for i, c in enumerate(first):
        c.wait_recv()
        total = total + s_got[i]
    s_held[...] = total
    s_far[p] = total
    second = [send(s_held, s_far.at[p], sc_send.at[k], sc_recv.at[k], dev(other(p, k, TEAM), t, s)) for k in range(1, TEAM)]
    gain_two_sum = jnp.sum(d_second * middle * scale, axis=0, keepdims=True)
    grad_relays(UP)
    score_s[...] = jnp.zeros(score_s.shape, F32)

    def attend_back(u):
        rows_u = seat(u)
        d_mix = dot_t(db_all[rows_u, :], w_all[ATTN, 3 * part:4 * part, :]).astype(BF16)
        q, key, v = q_all[rows_u, :], k_all[rows_u, :], v_all[rows_u, :]
        dq = jnp.zeros((rows, part), F32)
        dk = jnp.zeros((rows, part), F32)
        dv = jnp.zeros((rows, part), F32)
        for h in range(heads):
            weights = probs_all[h, rows_u, :]
            d_w = dot_t(jnp.where(lane_head == h, d_mix, zero_low), v)
            ds = (weights * (d_w - jnp.sum(weights * d_w, axis=-1, keepdims=True))).astype(BF16)
            dv = jnp.where(lane_head == h, dot_r(weights.astype(BF16), d_mix), dv)
            dq = jnp.where(lane_head == h, dot(ds, key), dq)
            dk = jnp.where(lane_head == h, dot_r(ds, q), dk)
            wide_ds = ds.astype(F32)
            score_s[h] = score_s[h] + wide_ds[:slots] + wide_ds[slots:]
        dq_all[rows_u, :] = (dq * factor).astype(BF16)
        dk_all[rows_u, :] = (dk * factor).astype(BF16)
        dv_all[rows_u, :] = dv.astype(BF16)

    norms = []
    gain_sum = jnp.zeros((1, width), F32)

    def norm_rows(k):
        u = mate(k)
        rows_u = seat(u)
        value = (dot(dq_all[rows_u, :], w_all[ATTN, 0:part, :]) + dot(dk_all[rows_u, :], w_all[ATTN, part:2 * part, :])
                 + dot(dv_all[rows_u, :], w_all[ATTN, 2 * part:3 * part, :]))
        norms.extend(scatter(DNORM, k, value))
        return jnp.sum(value * unit_of(u), axis=0, keepdims=True)

    attend_back(t)
    gain_sum = gain_sum + norm_rows(0)
    drain(mark_out)
    for k in (3, 2, 1):
        dbs[TEAM - k - 1].wait_recv()
        attend_back(mate(k))
        gain_sum = gain_sum + norm_rows(k)

    for q, left, right in ((3, mixed, db_all), (0, dq_all, normed), (2, dv_all, normed), (1, dk_all, normed)):
        g_part[ATTN, q * part:(q + 1) * part, :] = dot_r(left[...], right[...]).astype(BF16)
        grad_near(ATTN, q)
    for q in (3, 0, 2, 1):
        grad_push(ATTN, q)
    for c in second:
        c.wait_recv()
    total = s_far[0]
    for k in range(1, TEAM):
        total = total + s_far[k]
    small_ref[piece(0, 0), :] = total
    mine_small = small_ref.at[piece(0, 0), :]
    third = [send(mine_small, mine_small, sd_send.at[i], sd_recv.at[i], plane[i]) for i in range(len(plane))]
    def gather_gap(d, carry):
        hit = gap == d
        for h in range(heads):
            gap_s[h, pl.ds(d, 1), :] = jnp.sum(jnp.where(hit, score_s[h], 0.0), axis=0, keepdims=True)
        return carry

    lax.fori_loop(0, slots, gather_gap, 0)
    lane = lax.broadcasted_iota(jnp.int32, (slots, 128), 1)
    by_gap = jnp.zeros((slots, 128), F32)
    for h in range(heads):
        by_gap = jnp.where(lane == heads * t + h, jnp.sum(gap_s[h], axis=-1, keepdims=True), by_gap)
    count = table_ref.shape[1]
    bucket_hit = jnp.where(lax.broadcasted_iota(jnp.int32, (count, slots), 0) == buckets_ref[...], 1.0, 0.0)
    l_own[0:count, :] = jnp.dot(bucket_hit, by_gap, precision=HIGHEST, preferred_element_type=F32)
    for i in range(width // 128):
        l_own[count + i:count + i + 1, :] = gain_sum[:, i * 128:(i + 1) * 128]
        j = count + width // 128 + i
        l_own[j:j + 1, :] = gain_two_sum[:, i * 128:(i + 1) * 128]
    used = count + 2 * (width // 128)
    l_own[used:, :] = jnp.zeros((l_own.shape[0] - used, 128), F32)
    late_a = [send(l_own, l_got.at[k - 1], la_send.at[k], la_recv.at[k], dev(p, mate(k), s)) for k in range(1, TEAM)]

    grad_relays(ATTN)
    grad_end(DOWN)
    for c in late_a:
        c.wait_recv()
    total = l_own[...]
    for k in range(1, TEAM):
        total = total + l_got[k - 1]
    l_sum[...] = total
    l_sib[s] = total
    late_b = [send(l_sum, l_sib.at[s], lb_send.at[j], lb_recv.at[j], dev(p, t, other(s, j, sub))) for j in range(1, sub)]
    grad_end(GATE)
    for c in late_b:
        c.wait_recv()
    total = l_sib[0]
    for j in range(1, sub):
        total = total + l_sib[j]
    l_tot[...] = total
    l_far[p] = total
    late_c = [send(l_tot, l_far.at[p], lc_send.at[k], lc_recv.at[k], dev(other(p, k, TEAM), t, s)) for k in range(1, TEAM)]
    grad_end(UP)

    x = tok_ref[...].astype(F32)
    d_normed = gathered(DNORM, norms)
    scale = lax.rsqrt(jnp.mean(x * x, axis=-1, keepdims=True) + EPSILON)
    dtok_ref[...] = (dmid_s[...] + norm_back(x, scale, gain_one, d_normed)).astype(BF16)

    for c in late_c:
        c.wait_recv()
    total = l_far[0]
    for k in range(1, TEAM):
        total = total + l_far[k]
    late_ref[...] = total
    grad_end(ATTN)
    for c in third:
        c.wait_recv()
    drain(len(pending))


def finish_kernel(routed, result_ref, dtok_ref, g_ref, small_ref, late_ref,
                  result_out, dtok_out, attn_out, gate_out, up_out, down_out, gains_out, table_out, router_out):
    result_out[...] = result_ref[...]
    dtok_out[...] = dtok_ref[...]
    attn_out[...] = g_ref[ATTN]
    gate_out[...] = g_ref[GATE]
    up_out[...] = g_ref[UP]
    down_out[...] = g_ref[DOWN]
    router_out[...] = small_ref[0:routed, :]
    heads, count = table_out.shape
    table_out[...] = late_ref[0:count, :].T[0:heads, :]
    parts = gains_out.shape[1] // 128
    for i in range(2 * parts):
        gains_out[i // parts:i // parts + 1, (i % parts) * 128:(i % parts + 1) * 128] = late_ref[count + i:count + i + 1, :]


def block(n, tokens, attn_weight, w_gate, w_up, w_down, norm_gains, bias_table, router,
          grad_out, segment, expert_ids, bucket_of):
    rows, width = tokens.shape
    shard = w_down.shape[0]
    sub = n // (TEAM * TEAM)
    head_count = bias_table.shape[1]
    heads = head_count // TEAM
    part = heads * (width // head_count)
    slots = bucket_of.shape[0]
    routed = router.shape[1]
    every = TEAM * rows
    dma = pltpu.SemaphoreType.DMA
    shape = jax.ShapeDtypeStruct
    buf = pltpu.VMEM
    depth = routed // (TEAM * sub)
    lines = -(-(bias_table.shape[0] + 2 * (width // 128)) // 8) * 8
    smem = pl.BlockSpec(memory_space=pltpu.SMEM)
    result, dtok, grads, small, late = pl.pallas_call(
        functools.partial(block_kernel, n, head_count),
        out_shape=(shape(tokens.shape, BF16), shape(tokens.shape, BF16), shape((4, shard, width), F32),
                   shape((routed, width), F32), shape((lines, 128), F32)),
        in_specs=[VMEM] * 11 + [smem] * 2,
        out_specs=(VMEM,) * 5,
        scratch_shapes=[
            buf((4, width, width), BF16), buf((4, width, width), BF16), buf((4, sub - 1, TEAM, shard, width), BF16),
            buf((4, TEAM, shard, width), BF16), buf((4, TEAM, shard, width), BF16), buf((4, shard, width), BF16),
            buf((every, width), BF16), buf((every, width), BF16), buf((TEAM * LINES, rows), F32), buf((every, width), BF16),
            buf((every, part), BF16), buf((every, part), BF16), buf((every, part), BF16), buf((every, part), BF16),
            buf((heads, every, rows), F32), buf((heads, slots, 2 * slots), F32),
            buf((4, TEAM - 1, rows, width), BF16), buf((4, TEAM - 1, rows, width), BF16), buf((4, rows, width), F32),
            buf((rows, width), F32), buf((every, width), BF16), buf((every, width), BF16), buf((rows, 128), F32),
            buf((rows, routed), F32), buf((routed, width), BF16), buf((routed, width), BF16),
            buf((every, 256), F32), buf((every, 256), F32), buf((every, width), BF16), buf((every, width), F32),
            buf((every, width), F32), buf((every, width), BF16), buf((every, width), BF16), buf((rows, width), F32),
            buf((every, width), BF16), buf((every, part), BF16), buf((every, part), BF16), buf((every, part), BF16),
            buf((heads, slots, 2 * slots), F32), buf((heads, slots, 2 * slots), F32),
            buf((routed, width), F32), buf((TEAM * sub - 1, depth, width), F32),
            buf((depth, width), F32), buf((TEAM, depth, width), F32),
            buf((lines, 128), F32), buf((TEAM - 1, lines, 128), F32), buf((lines, 128), F32),
            buf((sub, lines, 128), F32), buf((lines, 128), F32), buf((TEAM, lines, 128), F32),
            dma((9, TEAM)), dma((9, TEAM)), dma((4, TEAM)), dma((4, TEAM)), dma((4, TEAM, sub)), dma((4, TEAM, sub)),
            dma((4, TEAM, sub)), dma((4, TEAM, sub)), dma((4, TEAM)), dma((4, TEAM)), dma((4,)), dma((4,)),
            dma((TEAM * sub,)), dma((TEAM * sub,)), dma((TEAM,)), dma((TEAM,)), dma((TEAM * sub,)), dma((TEAM * sub,)),
            dma((TEAM,)), dma((TEAM,)), dma((sub,)), dma((sub,)), dma((TEAM,)), dma((TEAM,)),
        ],
        compiler_params=pltpu.CompilerParams(collective_id=0, has_side_effects=True, vmem_limit_bytes=56 * 2**20),
        name="block",
    )(attn_weight.T, w_gate.T, w_up.T, w_down, tokens, grad_out, segment.reshape(1, rows), expert_ids.T, norm_gains,
      router.T, bucket_of.reshape(1, slots), bias_table.T, bucket_of)
    grad = shape((shard, width), F32)
    result, dtok, g_attn, g_gate, g_up, g_down, gains, table, routes = pl.pallas_call(
        functools.partial(finish_kernel, routed),
        out_shape=(shape(tokens.shape, BF16), shape(tokens.shape, BF16), grad, grad, grad, grad,
                   shape(norm_gains.shape, F32), shape(bias_table.shape[::-1], F32), shape(router.shape[::-1], F32)),
        in_specs=[VMEM] * 5,
        out_specs=(VMEM,) * 9,
        name="finish",
    )(result, dtok, grads, small, late)
    return result, dtok, g_attn.T, g_gate.T, g_up.T, g_down, gains, table.T, routes.T


def solution(mesh):
    n = mesh.shape["fsdp"]
    row, col = P("fsdp", None), P(None, "fsdp")
    in_specs = (row, col, col, col, row, P(), P(), P(), row, P("fsdp"), row, P())
    out_specs = (row, row, col, col, col, row, P(), P(), P())

    def run(*args):
        shard, rows = args[4].shape[0] // n, args[0].shape[0] // n
        whole_tiles = shard % 16 == 0 and rows == 2 * args[11].shape[0] and args[7].shape[1] % (n // 2) == 0
        return jax.shard_map(
            functools.partial(block if whole_tiles else body, n),
            mesh=mesh, in_specs=in_specs, out_specs=out_specs, check_vma=False,
        )(*args)

    return run
```

```python
import functools
import math
import jax
import jax.numpy as jnp
from jax import lax
from jax.experimental import pallas as pl
from jax.experimental.pallas import tpu as pltpu
from jax.sharding import PartitionSpec as P

EPSILON = 1e-06
HIGHEST = lax.Precision.HIGHEST
MESH = pl.DeviceIdType.MESH
TEAM = 4
F32 = jnp.float32
BF16 = jnp.bfloat16
VMEM = pl.BlockSpec(memory_space=pltpu.VMEM)
ANY = pl.BlockSpec(memory_space=pl.ANY)
HBM = pl.BlockSpec(memory_space=pltpu.HBM)
CONTRACT_ROWS = (((0,), (0,)), ((), ()))
CONTRACT_COLS = (((1,), (1,)), ((), ()))


def place(n):
    sub = n // (TEAM * TEAM)
    me = lax.axis_index("fsdp")
    p = me // (TEAM * sub)
    t = lax.rem(me // sub, TEAM)
    s = lax.rem(me, sub)
    return sub, p, t, s, (lambda p, t, s: (p * (TEAM * sub) + t * sub + s,))


def greet(peers):
    barrier = pltpu.get_barrier_semaphore()
    for peer in peers:
        pl.semaphore_signal(barrier, inc=1, device_id=peer, device_id_type=MESH)
    pl.semaphore_wait(barrier, len(peers))


def remote(src, dst, send, recv, peer):
    return pltpu.make_async_remote_copy(
        src_ref=src, dst_ref=dst, send_sem=send, recv_sem=recv, device_id=peer, device_id_type=MESH
    )


def other(index, step, count):
    return lax.rem(index + step, count)


def spread_peers(sub, p, t, s, dev):
    peers = [dev(other(p, k, TEAM), t, s) for k in range(1, TEAM)]
    return peers + [dev(p, t, other(s, k, sub)) for k in range(1, sub)]


def team_peers(p, t, s, dev):
    return [dev(p, other(t, k, TEAM), s) for k in range(1, TEAM)]


def weights_start(n, w_ref, w_all, sems):
    sub, p, t, s, dev = place(n)
    p_send, p_recv, s_send, s_recv, own_sem = sems
    wide, near, local = [], [], []
    for i in range(w_ref.shape[0]):
        for k in range(1, TEAM):
            c = remote(w_ref.at[i], w_all.at[i, p, s], p_send.at[i, k], p_recv.at[i, k],
                       dev(other(p, k, TEAM), t, s))
            c.start()
            wide.append(c)
    for i in range(w_ref.shape[0]):
        for k in range(1, sub):
            c = remote(w_ref.at[i], w_all.at[i, p, s], s_send.at[i, 0, k], s_recv.at[i, 0, k],
                       dev(p, t, other(s, k, sub)))
            c.start()
            near.append(c)
        c = pltpu.make_async_copy(w_ref.at[i], w_all.at[i, p, s], own_sem.at[i])
        c.start()
        local.append(c)
    return wide, near, local


def weights_finish(n, w_all, sems, state):
    sub, p, t, s, dev = place(n)
    _, _, s_send, s_recv, _ = sems
    wide, near, local = state
    for i in range(w_all.shape[0]):
        for k in range(1, TEAM):
            wide[i * (TEAM - 1) + k - 1].wait_recv()
            q = other(p, TEAM - k, TEAM)
            for j in range(1, sub):
                c = remote(w_all.at[i, q, s], w_all.at[i, q, s], s_send.at[i, k, j], s_recv.at[i, k, j],
                           dev(p, t, other(s, j, sub)))
                c.start()
                near.append(c)
    for c in wide:
        c.wait_send()
    for c in near:
        c.wait()
    for c in local:
        c.wait()


def weights_sems(n, kinds):
    sub = n // (TEAM * TEAM)
    dma = pltpu.SemaphoreType.DMA
    return [dma((kinds, TEAM)), dma((kinds, TEAM)), dma((kinds, TEAM, sub)), dma((kinds, TEAM, sub)), dma((kinds,))]


def weights_shape(n, w):
    return jax.ShapeDtypeStruct((w.shape[0], TEAM, n // (TEAM * TEAM)) + w.shape[1:], w.dtype)


def gather_kernel(n, w_ref, tok_ref, dy_ref, meta_ref, w_all, tok_all, dy_all, meta_all,
                  t_send, t_recv, own_sem, *sems):
    sub, p, t, s, dev = place(n)
    greet(spread_peers(sub, p, t, s, dev) + team_peers(p, t, s, dev))
    state = weights_start(n, w_ref, w_all, sems)
    copies, local = [], []
    for i, (src, dst) in enumerate(((tok_ref, tok_all), (dy_ref, dy_all), (meta_ref, meta_all))):
        for k in range(1, TEAM):
            c = remote(src, dst.at[t], t_send.at[i, k], t_recv.at[i, k], dev(p, other(t, k, TEAM), s))
            c.start()
            copies.append(c)
        c = pltpu.make_async_copy(src, dst.at[t], own_sem.at[i])
        c.start()
        local.append(c)
    weights_finish(n, w_all, sems, state)
    for c in copies:
        c.wait()
    for c in local:
        c.wait()


def gather(n, w, tok, dy, meta):
    dma = pltpu.SemaphoreType.DMA
    shape = jax.ShapeDtypeStruct
    return pl.pallas_call(
        functools.partial(gather_kernel, n),
        out_shape=(
            weights_shape(n, w),
            shape((TEAM,) + tok.shape, BF16),
            shape((TEAM,) + dy.shape, BF16),
            shape((TEAM,) + meta.shape, jnp.int32),
        ),
        in_specs=[VMEM] * 4,
        out_specs=(ANY,) * 4,
        scratch_shapes=[dma((3, TEAM)), dma((3, TEAM)), dma((3,))] + weights_sems(n, w.shape[0]),
        compiler_params=pltpu.CompilerParams(collective_id=0, has_side_effects=True),
        name="gather_all",
    )(w, tok, dy, meta)


def middle_kernel(n, part_ref, x_ref, gain_ref, w_ref, y_ref, h_all, w_all, got, held,
                  a_send, a_recv, b_send, b_recv, own_sem, *sems):
    sub, p, t, s, dev = place(n)
    greet(spread_peers(sub, p, t, s, dev) + team_peers(p, t, s, dev))
    copies = []
    for k in range(1, TEAM):
        u = other(t, k, TEAM)
        c = remote(part_ref.at[u], got.at[k - 1], a_send.at[k], a_recv.at[k], dev(p, u, s))
        c.start()
        copies.append(c)
    state = weights_start(n, w_ref, w_all, sems)
    total = x_ref[...].astype(F32) + part_ref[t].astype(F32)
    for k in range(1, TEAM):
        copies[k - 1].wait_recv()
        total = total + got[k - 1].astype(F32)
    y_ref[...] = total
    scale = lax.rsqrt(jnp.mean(total * total, axis=-1, keepdims=True) + EPSILON)
    held[...] = (total * scale * gain_ref[1:2, :]).astype(BF16)
    local = pltpu.make_async_copy(held, h_all.at[t], own_sem)
    local.start()
    sends = []
    for k in range(1, TEAM):
        c = remote(held, h_all.at[t], b_send.at[k], b_recv.at[k], dev(p, other(t, k, TEAM), s))
        c.start()
        sends.append(c)
    weights_finish(n, w_all, sems, state)
    for c in copies:
        c.wait_send()
    for c in sends:
        c.wait()
    local.wait()


def middle_exchange(n, part, x, gains, w):
    dma = pltpu.SemaphoreType.DMA
    shape = jax.ShapeDtypeStruct
    return pl.pallas_call(
        functools.partial(middle_kernel, n),
        out_shape=(shape(x.shape, F32), shape((TEAM,) + x.shape, BF16), weights_shape(n, w)),
        in_specs=[VMEM] * 4,
        out_specs=(VMEM, ANY, ANY),
        scratch_shapes=[pltpu.VMEM((TEAM - 1,) + x.shape, BF16), pltpu.VMEM(x.shape, BF16),
                        dma((TEAM,)), dma((TEAM,)), dma((TEAM,)), dma((TEAM,)), dma] + weights_sems(n, w.shape[0]),
        compiler_params=pltpu.CompilerParams(collective_id=1, has_side_effects=True),
        name="middle_exchange",
    )(part, x, gains, w)


def reduce_kernel(n, m, h, gain_row, *refs):
    parts, rows, grad_ref = refs[:m], refs[m:m + h], refs[m + h]
    refs = refs[m + h + 1:]
    small = gain_row is not None
    if small:
        unit_ref, small_ref = refs[:2]
        refs = refs[2:]
    outs, rows_all, grad_out = refs[:m], refs[m:m + h], refs[m + h]
    if small:
        small_out = refs[m + h + 1]
        refs = refs[:m + h + 1] + refs[m + h + 2:]
    (got, sib, to_send, far, t_send, t_recv, h_send, h_recv, own_sem,
     s_send, s_recv, p_send, p_recv) = refs[m + h + 1:m + h + 14]
    rest = refs[m + h + 14:]
    sub, p, t, s, dev = place(n)
    greet(spread_peers(sub, p, t, s, dev) + team_peers(p, t, s, dev))
    kinds = grad_ref.shape[0]
    near, tokens, wide, shared, local = [], [], [], [], []
    for kind in range(kinds):
        for k in range(1, sub):
            v = other(s, k, sub)
            c = remote(grad_ref.at[kind, :, v], sib.at[kind, k - 1], s_send.at[kind, k], s_recv.at[kind, k],
                       dev(p, t, v))
            c.start()
            near.append(c)
    for i in range(h):
        for k in range(1, TEAM):
            c = remote(rows[i], rows_all[i].at[t], h_send.at[i, k], h_recv.at[i, k],
                       dev(p, other(t, k, TEAM), s))
            c.start()
            shared.append(c)
        c = pltpu.make_async_copy(rows[i], rows_all[i].at[t], own_sem.at[i])
        c.start()
        local.append(c)
    for i in range(m):
        for k in range(1, TEAM):
            u = other(t, k, TEAM)
            c = remote(parts[i].at[u], got.at[i, k - 1], t_send.at[i, k], t_recv.at[i, k], dev(p, u, s))
            c.start()
            tokens.append(c)
    for kind in range(kinds):
        for c in near[kind * (sub - 1):(kind + 1) * (sub - 1)]:
            c.wait_recv()
        for k in range(1, TEAM):
            q = other(p, k, TEAM)
            total = grad_ref[kind, q, s].astype(F32)
            for j in range(1, sub):
                total = total + sib[kind, j - 1, q].astype(F32)
            to_send[kind, k - 1] = total.astype(BF16)
            c = remote(to_send.at[kind, k - 1], far.at[kind, k - 1], p_send.at[kind, k], p_recv.at[kind, k],
                       dev(q, t, s))
            c.start()
            wide.append(c)
    for i in range(m):
        total = parts[i][t].astype(F32)
        for k in range(1, TEAM):
            tokens[i * (TEAM - 1) + k - 1].wait_recv()
            total = total + got[i, k - 1].astype(F32)
        outs[i][...] = total
    if small:
        buf = rest[0]
        piece, line = divmod(gain_row, small_ref.shape[1])
        gain = jnp.sum(outs[0][...] * unit_ref[...], axis=0, keepdims=True)
        buf[...] = small_ref[...]
        buf[piece, line:line + 1, :] = gain
        small_phases(n, buf, small_out, *rest[1:])
    for kind in range(kinds):
        for c in wide[kind * (TEAM - 1):(kind + 1) * (TEAM - 1)]:
            c.wait_recv()
        total = grad_ref[kind, p, s].astype(F32)
        for j in range(1, sub):
            total = total + sib[kind, j - 1, p].astype(F32)
        for k in range(1, TEAM):
            total = total + far[kind, k - 1].astype(F32)
        grad_out[kind] = total
    for c in near + tokens + wide:
        c.wait_send()
    for c in shared:
        c.wait()
    for c in local:
        c.wait()


def reduce_exchange(n, parts, rows, grads, ident, small=(), gain_row=None):
    sub = n // (TEAM * TEAM)
    m, h = len(parts), len(rows)
    dma = pltpu.SemaphoreType.DMA
    shape = jax.ShapeDtypeStruct
    block = parts[0].shape[1:] if m else (8, 128)
    kinds, tile = grads.shape[0], grads.shape[3:]
    outs = pl.pallas_call(
        functools.partial(reduce_kernel, n, m, h, gain_row),
        out_shape=(shape(block, F32),) * m
        + tuple(shape((TEAM,) + v.shape, v.dtype) for v in rows)
        + (shape((kinds,) + tile, F32),)
        + tuple(shape(v.shape, F32) for v in small[1:]),
        in_specs=[VMEM] * (m + h + 1 + len(small)),
        out_specs=(VMEM,) * m + (ANY,) * h + (VMEM,) * (1 + len(small[1:])),
        scratch_shapes=[
            pltpu.VMEM((max(m, 1), TEAM - 1) + block, BF16),
            pltpu.VMEM((kinds, sub - 1, TEAM) + tile, BF16),
            pltpu.VMEM((kinds, TEAM - 1) + tile, BF16),
            pltpu.VMEM((kinds, TEAM - 1) + tile, BF16),
            dma((max(m, 1), TEAM)), dma((max(m, 1), TEAM)),
            dma((max(h, 1), TEAM)), dma((max(h, 1), TEAM)), dma((max(h, 1),)),
            dma((kinds, sub)), dma((kinds, sub)), dma((kinds, TEAM)), dma((kinds, TEAM)),
        ] + (small_scratch(n, small[1].shape) if small else []),
        compiler_params=pltpu.CompilerParams(collective_id=ident, has_side_effects=True),
        name=f"reduce_{ident}",
    )(*parts, *rows, grads, *small)
    return (outs[:m], outs[m:m + h]) + tuple(outs[m + h:])


def small_phases(n, buf, out_ref, got, mine, sib, held, far,
                 a_send, a_recv, s_send, s_recv, b_send, b_recv, c_send, c_recv):
    sub, p, t, s, dev = place(n)
    first, near, second, third = [], [], [], []
    for k in range(1, TEAM):
        u = other(t, k, TEAM)
        c = remote(buf.at[u], got.at[k - 1], a_send.at[k], a_recv.at[k], dev(p, u, s))
        c.start()
        first.append(c)
    total = buf[t]
    for k in range(1, TEAM):
        first[k - 1].wait_recv()
        total = total + got[k - 1]
    mine[...] = total
    sib[s] = total
    for k in range(1, sub):
        c = remote(mine, sib.at[s], s_send.at[k], s_recv.at[k], dev(p, t, other(s, k, sub)))
        c.start()
        near.append(c)
    for c in near:
        c.wait_recv()
    total = sib[0]
    for k in range(1, sub):
        total = total + sib[k]
    held[...] = total
    far[p] = total
    for k in range(1, TEAM):
        c = remote(held, far.at[p], b_send.at[k], b_recv.at[k], dev(other(p, k, TEAM), t, s))
        c.start()
        second.append(c)
    for c in second:
        c.wait_recv()
    total = far[0]
    for k in range(1, TEAM):
        total = total + far[k]
    out_ref[t] = total
    for k in range(1, TEAM):
        c = remote(out_ref.at[t], out_ref.at[t], c_send.at[k], c_recv.at[k], dev(p, other(t, k, TEAM), s))
        c.start()
        third.append(c)
    for c in first + near + second:
        c.wait_send()
    for c in third:
        c.wait()


def small_scratch(n, shape):
    sub = n // (TEAM * TEAM)
    dma = pltpu.SemaphoreType.DMA
    tile = shape[1:]
    return [pltpu.VMEM(shape, F32), pltpu.VMEM((TEAM - 1,) + tile, F32), pltpu.VMEM(tile, F32),
            pltpu.VMEM((sub,) + tile, F32), pltpu.VMEM(tile, F32), pltpu.VMEM((TEAM,) + tile, F32),
            dma((TEAM,)), dma((TEAM,)), dma((sub,)), dma((sub,))] + [dma((TEAM,))] * 4


def gelu_tanh(inner):
    return jax.nn.gelu(inner, approximate=True)


def norm_back(inputs, scale, gain, upstream):
    weighted = gain * upstream
    return scale * weighted - inputs * scale * scale * scale * jnp.mean(
        weighted * inputs, axis=-1, keepdims=True
    )


def dot_t(a, b):
    return lax.dot_general(a, b, CONTRACT_COLS, preferred_element_type=F32)


def dot_r(a, b):
    return lax.dot_general(a, b, CONTRACT_ROWS, preferred_element_type=F32)


def dot(a, b):
    return jnp.dot(a, b, preferred_element_type=F32)


def body(n, tokens, attn_weight, w_gate, w_up, w_down, norm_gains, bias_table, router,
         grad_out, segment, expert_ids, bucket_of):
    rows, width = tokens.shape
    slots = bucket_of.shape[0]
    routed = router.shape[1]
    buckets, head_count = bias_table.shape
    head_width = width // head_count
    factor = head_width ** (-0.5)
    heads = head_count // TEAM
    part = heads * head_width
    sub, _, t, _, _ = place(n)
    all_rows = TEAM * rows
    spans = all_rows // slots

    early = jnp.stack([attn_weight.T, w_down])
    late = jnp.stack([w_gate.T, w_up.T])
    meta = jnp.concatenate([segment[None], expert_ids.T, jnp.zeros((5, rows), jnp.int32)], axis=0)
    w_all, tok_all, dy_all, meta_all = gather(n, early, tokens, grad_out, meta)
    w_all = w_all.reshape(2, -1, width)
    attn_t, down = w_all[0], w_all[1]
    qkv_t, out_t = attn_t[: 3 * part], attn_t[3 * part :]
    inputs = tok_all.reshape(all_rows, width).astype(F32)
    segments = meta_all[:, 0, :].reshape(all_rows)
    id_a = meta_all[:, 1, :].reshape(all_rows)
    id_b = meta_all[:, 2, :].reshape(all_rows)

    places = jnp.arange(slots)
    gap = places[:, None] - places[None, :]
    causal = gap >= 0
    gap_hit = (gap[:, :, None] == places[None, None, :]).astype(F32)
    bucket_hit = (bucket_of[:, None] == jnp.arange(buckets)[None, :]).astype(F32)
    table_mine = lax.dynamic_slice(bias_table, (0, heads * t), (buckets, heads))
    by_gap = jnp.dot(bucket_hit, table_mine, precision=HIGHEST)
    offsets = jnp.einsum("ijd,dh->hij", gap_hit, by_gap, precision=HIGHEST)

    scale_one = lax.rsqrt(jnp.mean(inputs * inputs, axis=-1, keepdims=True) + EPSILON)
    normed = (inputs * scale_one * norm_gains[0]).astype(BF16)
    triple = dot_t(normed, qkv_t).astype(BF16)
    heads_of = lambda v: v.reshape(spans, slots, heads, head_width)
    query = heads_of(triple[:, :part])
    keyset = heads_of(triple[:, part : 2 * part])
    valueset = heads_of(triple[:, 2 * part :])
    seg = segments.reshape(spans, slots)
    allowed = (seg[:, :, None] == seg[:, None, :]) & causal[None]
    raw = jnp.einsum("bihd,bjhd->bhij", query, keyset, preferred_element_type=F32)
    scores = jnp.where(allowed[:, None], raw * factor + offsets[None], -1e30)
    peak = jnp.max(scores, axis=-1, keepdims=True)
    lifted_scores = jnp.exp(scores - peak)
    weights = lifted_scores / jnp.sum(lifted_scores, axis=-1, keepdims=True)
    weights_low = weights.astype(BF16)
    mixed = jnp.einsum("bhij,bjhd->bihd", weights_low, valueset, preferred_element_type=F32)
    mixed = mixed.reshape(all_rows, part).astype(BF16)
    branch = dot(mixed, out_t).astype(BF16).reshape(TEAM, rows, width)
    middle, second_all, late_all = middle_exchange(n, branch, tokens, norm_gains, late)
    late_all = late_all.reshape(2, -1, width)
    gate_t, up_t = late_all[0], late_all[1]
    second_all = second_all.reshape(all_rows, width)

    second_wide = second_all.astype(F32)
    probs_all = jax.nn.softmax(jnp.dot(second_wide, router, precision=HIGHEST), axis=-1)
    lanes = jnp.arange(routed)[None, :]
    picked_all = jnp.where((id_a[:, None] == lanes) | (id_b[:, None] == lanes), 1.0, 0.0)
    total_all = jnp.sum(probs_all * picked_all, axis=-1)
    live_all = picked_all[:, 0] * jnp.where(segments >= 0, 1.0, 0.0)
    combine_all = probs_all[:, 0] * live_all / total_all
    gated = dot_t(second_all, gate_t)
    lifted = dot_t(second_all, up_t)
    activated, gelu_back = jax.vjp(gelu_tanh, gated)
    hidden = (activated * lifted).astype(BF16)
    out_part = dot(hidden, down).astype(BF16).reshape(TEAM, rows, width)
    d_expert = (combine_all[:, None] * dy_all.reshape(all_rows, width).astype(F32)).astype(BF16)
    d_hidden = dot_t(d_expert, down)
    d_gated = gelu_back(d_hidden * lifted)[0].astype(BF16)
    d_lifted = (d_hidden * activated).astype(BF16)
    back_part = (dot(d_gated, gate_t) + dot(d_lifted, up_t)).astype(BF16).reshape(TEAM, rows, width)
    grad_ffn = jnp.stack(
        [dot_r(d_gated, second_all).astype(BF16), dot_r(d_lifted, second_all).astype(BF16)]
    ).reshape(2, TEAM, sub, -1, width)
    (expert_out, d_second), _, g_ffn = reduce_exchange(n, (out_part, back_part), (), grad_ffn, 2)
    grad_down = dot_r(hidden, d_expert).astype(BF16).reshape(1, TEAM, sub, -1, width)

    mine = lambda v: lax.dynamic_slice_in_dim(v, t * rows, rows, 0)
    second, probs, picked = mine(second_wide), mine(probs_all), mine(picked_all)
    chosen_total, live, combine = mine(total_all), mine(live_all), mine(combine_all)
    upstream = grad_out.astype(F32)
    result = (middle + combine[:, None] * expert_out).astype(BF16)
    d_combine = jnp.sum(expert_out * upstream, axis=-1)
    first_hot = jnp.where(jnp.arange(routed) == 0, 1.0, 0.0)
    ratio = probs[:, 0] / (chosen_total * chosen_total)
    d_probs = (d_combine * live)[:, None] * (
        first_hot[None, :] / chosen_total[:, None] - ratio[:, None] * picked
    )
    d_logits = probs * (d_probs - jnp.sum(d_probs * probs, axis=-1, keepdims=True))
    grad_router_t = lax.dot_general(d_logits, second, CONTRACT_ROWS, precision=HIGHEST)
    d_second = d_second + jnp.dot(d_logits, router.T, precision=HIGHEST)
    scale_two = lax.rsqrt(jnp.mean(middle * middle, axis=-1, keepdims=True) + EPSILON)
    gain_two = jnp.sum(d_second * middle * scale_two, axis=0)
    d_middle = upstream + norm_back(middle, scale_two, norm_gains[1], d_second)
    _, (d_branch,), g_down = reduce_exchange(n, (), (d_middle.astype(BF16),), grad_down, 3)
    d_branch = d_branch.reshape(all_rows, width)

    grad_out_t = dot_r(mixed, d_branch)
    d_mixed = heads_of(dot_t(d_branch, out_t).astype(BF16))
    d_weights = jnp.einsum("bihd,bjhd->bhij", d_mixed, valueset, preferred_element_type=F32)
    d_values = jnp.einsum("bhij,bihd->bjhd", weights_low, d_mixed, preferred_element_type=F32)
    d_scores = weights * (d_weights - jnp.sum(weights * d_weights, axis=-1, keepdims=True))
    d_scores = d_scores.astype(BF16)
    d_query = jnp.einsum("bhij,bjhd->bihd", d_scores, keyset, preferred_element_type=F32) * factor
    d_keys = jnp.einsum("bhij,bihd->bjhd", d_scores, query, preferred_element_type=F32) * factor
    score_sum = jnp.sum(d_scores.astype(F32), axis=0)
    gap_sum = jnp.einsum("hij,ijd->dh", score_sum, gap_hit, precision=HIGHEST)
    table_part = lax.dot_general(bucket_hit, gap_sum, CONTRACT_ROWS, precision=HIGHEST)
    grad_table = lax.dynamic_update_slice(jnp.zeros(bias_table.shape, F32), table_part, (0, heads * t))
    flat = lambda v: v.reshape(all_rows, part).astype(BF16)
    d_triple = jnp.concatenate([flat(d_query), flat(d_keys), flat(d_values)], axis=1)
    grad_in_t = dot_r(d_triple, normed)
    grad_attn = jnp.concatenate([grad_in_t, grad_out_t], axis=0).astype(BF16)
    grad_attn = grad_attn.reshape(1, TEAM, sub, -1, width)
    d_normed_part = dot(d_triple, qkv_t).astype(BF16).reshape(TEAM, rows, width)
    own_inputs = tokens.astype(F32)
    own_scale = mine(scale_one)
    table_flat = grad_table.reshape(-1)
    lines = -(-table_flat.shape[0] // width)
    table_rows = jnp.pad(table_flat, (0, lines * width - table_flat.shape[0])).reshape(lines, width)
    small = jnp.concatenate([grad_router_t, jnp.zeros((1, width), F32), gain_two[None], table_rows], axis=0)
    depth = -(-small.shape[0] // (8 * TEAM)) * 8
    small = jnp.pad(small, ((0, depth * TEAM - small.shape[0]), (0, 0))).reshape(TEAM, depth, width)
    (d_normed,), _, g_attn, small = reduce_exchange(
        n, (d_normed_part,), (), grad_attn, 4, (own_inputs * own_scale, small), routed
    )
    small = small.reshape(TEAM * depth, width)
    input_grad = (d_middle + norm_back(own_inputs, own_scale, norm_gains[0], d_normed)).astype(BF16)
    grad_router = small[:routed].T
    grad_gains = small[routed : routed + 2]
    grad_table = small[routed + 2 : routed + 2 + lines].reshape(-1)[: table_flat.shape[0]].reshape(bias_table.shape)
    return (result, input_grad, g_attn[0].T, g_ffn[0].T, g_ffn[1].T, g_down[0],
            grad_gains, grad_table, grad_router)


LINES = 8
TOK, DY, META, BRANCH, SECOND, OUT, BACK, DBRANCH, DNORM = range(9)
ATTN, GATE, UP, DOWN = range(4)


def split_high(v):
    high = v.astype(BF16)
    return high, (v - high.astype(F32)).astype(BF16)


def eye(size, dtype):
    row = lax.broadcasted_iota(jnp.int32, (size, size), 0)
    col = lax.broadcasted_iota(jnp.int32, (size, size), 1)
    return jnp.where(row == col, 1.0, 0.0).astype(dtype)


def block_kernel(
    n, head_count,
    attn_in, gate_in, up_in, down_in, tok_in, dy_in, seg_in, ids_in, gains_in, router_in, buckets_in, table_ref, bucket_ref,
    result_out, dtok_out, attn_out, gate_out, up_out, down_out, gains_out, table_out, router_out,
    seg_ref, ids_ref, gains_ref, router_ref, buckets_ref, result_ref, dtok_ref, g_ref, small_ref, gains_s, table_s, in_sem, out_sem,
    w_all, g_part, sib, to_send, far, hop,
    tok_all, dy_all, meta_all, normed, q_all, k_all, v_all, mixed, probs_all, offs,
    row_send, row_got, passed, kept, own_part, middle_s, h_all, dexp_all, coef_s, eprobs_s, rhi, rlo,
    gs, us, hidden, ge_s, dgu_s, dg_s, du_s, dmid_s, db_all, dq_all, dk_all, dv_all, score_s, gap_s,
    sbuf, s_got, s_held, s_far, l_own, l_got, l_sum, l_sib, l_tot, l_far,
    t_send, t_recv, z_send, z_recv, ws_send, ws_recv, gs_send, gs_recv, gp_send, gp_recv, hp_send, hp_recv,
    sa_send, sa_recv, sc_send, sc_recv, sd_send, sd_recv,
    la_send, la_recv, lb_send, lb_recv, lc_send, lc_recv,
):
    sub, p, t, s, dev = place(n)
    rows, width = tok_in.shape
    shard = down_in.shape[0]
    heads = head_count // TEAM
    head_width = width // head_count
    part = heads * head_width
    factor = head_width ** (-0.5)
    slots = buckets_ref.shape[1]
    routed = router_ref.shape[0]
    chunk = 256

    barrier = pltpu.get_barrier_semaphore()
    ring = [(a, b) for a in range(TEAM) for b in range(sub)][1:]
    plane = [dev(p, other(t, a, TEAM), other(s, b, sub)) for a, b in ring]
    peers = plane + [dev(other(p, k, TEAM), t, s) for k in range(1, TEAM)]
    for peer in peers:
        pl.semaphore_signal(barrier, inc=1, device_id=peer, device_id_type=MESH)

    def mate(k):
        return other(t, k, TEAM)

    def seat(u):
        return pl.ds(pl.multiple_of(u * rows, rows), rows)

    def lot(q, v):
        return pl.ds(pl.multiple_of((q * sub + v) * shard, shard), shard)

    pending = []
    waited = [0]

    def drain(upto):
        for where, c in pending[waited[0]:upto]:
            if where is None:
                c.wait_send()
            else:
                pl.when(where)(c.wait_send)
        waited[0] = upto

    def send(src, dst, ssem, rsem, peer, where=None):
        c = remote(src, dst, ssem, rsem, peer)
        if where is None:
            c.start()
        else:
            pl.when(where)(c.start)
        pending.append((where, c))
        return c

    slot = {BRANCH: 0, OUT: 1, BACK: 2, DNORM: 3}
    beside = t + 1 - 2 * lax.rem(t, 2)
    across = other(t, 2, TEAM)
    corner = TEAM - 1 - t
    half = rows // 2

    def half_seat(u, i):
        return pl.ds(pl.multiple_of(u * rows + i * half, half), half)

    def team(kind, slot, src, dst, u):
        return send(src, dst, t_send.at[kind, slot], t_recv.at[kind, slot], dev(p, u, s))

    def spread(kind, whole):
        first, last = whole.at[half_seat(t, 0), :], whole.at[half_seat(t, 1), :]
        return {1: team(kind, 1, first, first, beside), 3: team(kind, 3, last, last, across),
                2: team(kind, 2, last, last, beside), 4: team(kind, 4, first, first, across)}

    def spread_on(kind, whole, copies):
        copies[1].wait_recv()
        block = whole.at[half_seat(beside, 0), :]
        copies[5] = team(kind, 5, block, block, across)
        copies[3].wait_recv()
        block = whole.at[half_seat(across, 1), :]
        copies[6] = team(kind, 6, block, block, beside)

    spread_order = ((beside, (2,)), (across, (4,)), (corner, (5, 6)))

    def fold(kind, u, value, copies):
        i = slot[kind]
        first, last = slice(0, half), slice(half, rows)
        if u is corner:
            row_send[i, 0] = value.astype(BF16)
            copies[1] = team(kind, 1, row_send.at[i, 0, first], passed.at[i, 0], beside)
            copies[2] = team(kind, 2, row_send.at[i, 0, last], passed.at[i, 1], across)
        elif u is beside:
            row_send[i, 1, first] = value[first].astype(BF16)
            copies[3] = team(kind, 3, row_send.at[i, 1, first], row_got.at[i, 0, first], beside)
            kept[i, 1] = value[last]
        elif u is across:
            row_send[i, 2, last] = value[last].astype(BF16)
            copies[5] = team(kind, 5, row_send.at[i, 2, last], row_got.at[i, 1, last], across)
            kept[i, 0] = value[first]
        else:
            own_part[i] = value

    def fold_on(kind, copies):
        i = slot[kind]
        copies[1].wait_recv()
        row_send[i, 2, 0:half] = (kept[i, 0] + passed[i, 0].astype(F32)).astype(BF16)
        copies[6] = team(kind, 6, row_send.at[i, 2, 0:half], row_got.at[i, 1, 0:half], across)
        copies[2].wait_recv()
        row_send[i, 1, half:rows] = (kept[i, 1] + passed[i, 1].astype(F32)).astype(BF16)
        copies[4] = team(kind, 4, row_send.at[i, 1, half:rows], row_got.at[i, 0, half:rows], beside)

    def folded(kind, copies):
        for k in (3, 5, 6, 4):
            copies[k].wait_recv()
        i = slot[kind]
        return own_part[i] + row_got[i, 0].astype(F32) + row_got[i, 1].astype(F32)

    fold_order = (corner, beside, across, t)

    def share(kind, src, whole):
        return [send(src, whole.at[seat(t)], t_send.at[kind, k], t_recv.at[kind, k], dev(p, mate(k), s))
                for k in range(1, TEAM)]

    weight_in = (attn_in, gate_in, up_in, down_in)
    loads = []
    for i, (src, dst) in enumerate((
        (seg_in, seg_ref), (ids_in, ids_ref), (tok_in, tok_all.at[seat(t)]), (attn_in, w_all.at[ATTN, lot(p, s), :]),
        (gains_in, gains_ref), (router_in, router_ref), (buckets_in, buckets_ref), (dy_in, dy_all.at[seat(t)]),
        (gate_in, w_all.at[GATE, lot(p, s), :]), (up_in, w_all.at[UP, lot(p, s), :]), (down_in, w_all.at[DOWN, lot(p, s), :]),
    )):
        loads.append(pltpu.make_async_copy(src, dst, in_sem.at[i]))
        loads[i].start()
    stores = []

    def store(src, dst):
        stores.append(pltpu.make_async_copy(src, dst, out_sem.at[len(stores)]))
        stores[-1].start()

    loads[0].wait()
    loads[1].wait()
    ids = ids_ref[...].astype(F32)
    line = lax.broadcasted_iota(jnp.int32, (LINES, rows), 0)
    meta_all[pl.ds(pl.multiple_of(t * LINES, LINES), LINES), :] = jnp.where(
        line == 0, seg_ref[...].astype(F32), jnp.where(line == 1, ids[0:1, :], jnp.where(line == 2, ids[1:2, :], 0.0))
    )
    pl.semaphore_wait(barrier, len(peers))

    wide = {}

    inner = (p == 1) | (p == 2)

    def weights_send(kind):
        mine = w_all.at[kind, lot(p, s), :]
        own = weight_in[kind]
        wide[kind] = {k: send(own, mine, z_send.at[kind, k], z_recv.at[kind, k], dev(other(p, k, TEAM), t, s), where)
                      for k, where in ((2, None), (1, p < TEAM - 1), (3, p > 0))}
        wide[kind, "near"] = [send(own, mine, ws_send.at[kind, 0, j], ws_recv.at[kind, 0, j], dev(p, t, other(s, j, sub)))
                              for j in range(1, sub)]

    def weights_arrive(kind, k):
        wide[kind][k].wait_recv()
        block = w_all.at[kind, lot(other(p, TEAM - k, TEAM), s), :]
        if k == 2:
            edge = p // 2
            send(block, block, z_send.at[kind, 0], z_recv.at[kind, 1 + 2 * edge], dev(3 * edge, t, s), inner)
        wide[kind, "near"] += [
            send(block, block, ws_send.at[kind, k, j], ws_recv.at[kind, k, j], dev(p, t, other(s, j, sub)))
            for j in range(1, sub)]

    def weights_forward(kind):
        weights_arrive(kind, 1)
        weights_arrive(kind, 3)

    def weights_wait(kind):
        for c in wide[kind, "near"]:
            c.wait_recv()

    mine_meta = meta_all.at[pl.ds(pl.multiple_of(t * LINES, LINES), LINES), :]
    metas = [send(mine_meta, mine_meta, t_send.at[META, k], t_recv.at[META, k], dev(p, mate(k), s)) for k in range(1, TEAM)]
    toks = share(TOK, tok_in, tok_all)
    weights_send(ATTN)
    weights_send(GATE)
    dys = share(DY, dy_in, dy_all)

    for c in loads[2:]:
        c.wait()
    rhi[...], rlo[...] = split_high(router_ref[...])

    place_r = lax.broadcasted_iota(jnp.int32, (slots, 2 * slots), 0)
    place_c = lax.rem(lax.broadcasted_iota(jnp.int32, (slots, 2 * slots), 1), slots)
    gap = place_r - place_c
    offs[...] = jnp.zeros(offs.shape, F32)

    def spread_bias(d, carry):
        hit = gap == d
        for h in range(heads):
            offs[h] = jnp.where(hit, table_ref[heads * t + h, bucket_ref[d]], offs[h])
        return carry

    lax.fori_loop(0, slots, spread_bias, 0)

    row_i = lax.broadcasted_iota(jnp.int32, (rows, rows), 0)
    col_i = lax.broadcasted_iota(jnp.int32, (rows, rows), 1)
    causal = (row_i >= col_i) & ((row_i // slots) == (col_i // slots))
    lane_head = lax.broadcasted_iota(jnp.int32, (rows, part), 1) // head_width
    gain_one, gain_two = gains_ref[0:1, :], gains_ref[1:2, :]
    zero_low = jnp.zeros((rows, part), BF16)

    def meta_of(u):
        lines = meta_all[pl.ds(pl.multiple_of(u * LINES, LINES), LINES), :]
        return lines, dot_t(eye(rows, F32), lines)

    def unit_of(u):
        x = tok_all[seat(u), :].astype(F32)
        return x * lax.rsqrt(jnp.mean(x * x, axis=-1, keepdims=True) + EPSILON)

    def attend(u):
        rows_u = seat(u)
        h1 = (unit_of(u) * gain_one).astype(BF16)
        normed[rows_u, :] = h1
        q = dot_t(h1, w_all[ATTN, 0:part, :]).astype(BF16)
        key = dot_t(h1, w_all[ATTN, part:2 * part, :]).astype(BF16)
        v = dot_t(h1, w_all[ATTN, 2 * part:3 * part, :]).astype(BF16)
        q_all[rows_u, :], k_all[rows_u, :], v_all[rows_u, :] = q, key, v
        lines, cols = meta_of(u)
        allowed = (cols[:, 0:1] == lines[0:1, :]) & causal
        mix = jnp.zeros((rows, part), F32)
        for h in range(heads):
            raw = dot_t(jnp.where(lane_head == h, q, zero_low), key)
            scores = jnp.where(allowed, raw * factor + jnp.concatenate([offs[h], offs[h]], axis=0), -1e30)
            lifted = jnp.exp(scores - jnp.max(scores, axis=-1, keepdims=True))
            weights = lifted / jnp.sum(lifted, axis=-1, keepdims=True)
            probs_all[h, rows_u, :] = weights
            mix = jnp.where(lane_head == h, dot(weights.astype(BF16), v), mix)
        low = mix.astype(BF16)
        mixed[rows_u, :] = low
        return dot(low, w_all[ATTN, 3 * part:4 * part, :])


    def scatter(kind, k, value, u):
        i = slot[kind]
        if k == 0:
            own_part[i] = value
            return []
        row_send[i, k - 1] = value.astype(BF16)
        return [send(row_send.at[i, k - 1], row_got.at[i, k - 1], t_send.at[kind, k], t_recv.at[kind, k],
                     dev(p, u, s))]

    def gathered(kind, copies):
        total = own_part[slot[kind]]
        for c in copies:
            c.wait_recv()
        for k in range(1, TEAM):
            total = total + row_got[slot[kind], k - 1].astype(F32)
        return total

    weights_arrive(ATTN, 2)
    weights_forward(ATTN)
    weights_send(UP)
    weights_wait(ATTN)
    for c in metas + toks:
        c.wait_recv()
    branch = {}
    for u in fold_order:
        fold(BRANCH, u, attend(u), branch)
    fold_on(BRANCH, branch)
    weights_arrive(GATE, 2)
    weights_send(DOWN)

    middle = tok_all[seat(t), :].astype(F32) + folded(BRANCH, branch)
    middle_s[...] = middle
    scale = lax.rsqrt(jnp.mean(middle * middle, axis=-1, keepdims=True) + EPSILON)
    h_all[seat(t), :] = (middle * scale * gain_two).astype(BF16)
    seconds = spread(SECOND, h_all)

    lane_expert = lax.broadcasted_iota(jnp.int32, (rows, routed), 1).astype(F32)

    def route(u):
        h2 = h_all[seat(u), :]
        logits = dot_t(h2, rhi[...]) + dot_t(h2, rlo[...])
        lifted = jnp.exp(logits - jnp.max(logits, axis=-1, keepdims=True))
        probs = lifted / jnp.sum(lifted, axis=-1, keepdims=True)
        _, cols = meta_of(u)
        picked = jnp.where((cols[:, 1:2] == lane_expert) | (cols[:, 2:3] == lane_expert), 1.0, 0.0)
        chosen = jnp.sum(probs * picked, axis=-1, keepdims=True)
        live = picked[:, 0:1] * jnp.where(cols[:, 0:1] >= 0.0, 1.0, 0.0)
        combine = probs[:, 0:1] * live / chosen
        dexp_all[seat(u), :] = (combine * dy_all[seat(u), :].astype(F32)).astype(BF16)
        return probs, picked, chosen, live, combine

    eprobs_s[...] = route(t)[0]
    spread_on(SECOND, h_all, seconds)
    weights_forward(GATE)
    weights_arrive(UP, 2)
    for c in dys:
        c.wait_recv()
    for u, parts in spread_order:
        for i in parts:
            seconds[i].wait_recv()
        route(u)

    weights_forward(UP)
    weights_wait(GATE)
    weights_wait(UP)
    k0 = (2.0 / math.pi) ** 0.5
    k1 = 0.044715
    step = 32
    for c in range(width // chunk):
        cols = slice(c * chunk, (c + 1) * chunk)
        gs[...] = dot_t(h_all[...], w_all[GATE, cols, :])
        us[...] = dot_t(h_all[...], w_all[UP, cols, :])

        def lift(r, carry):
            rr = pl.ds(pl.multiple_of(r * step, step), step)
            g, u = gs[rr, :], us[rr, :]
            square = g * g
            bend = jnp.tanh(k0 * g * (1.0 + k1 * square))
            half = 0.5 * (1.0 + bend)
            act = g * half
            slope = half + 0.5 * g * (1.0 - bend * bend) * (k0 * (1.0 + 3.0 * k1 * square))
            hidden[rr, cols] = (act * u).astype(BF16)
            ge_s[rr, cols] = act
            dgu_s[rr, cols] = slope * u
            return carry

        lax.fori_loop(0, TEAM * rows // step, lift, 0)

    near = {}

    def grad_near(kind, q):
        near[kind, q] = [
            send(g_part.at[kind, lot(q, other(s, j, sub)), :], sib.at[kind, j - 1, q], gs_send.at[kind, q, j],
                 gs_recv.at[kind, q, j], dev(p, t, other(s, j, sub)))
            for j in range(1, sub)]

    def grad_of(kind, q):
        total = g_part[kind, lot(q, s), :].astype(F32)
        for j in range(1, sub):
            total = total + sib[kind, j - 1, q].astype(F32)
        return total

    def to_owner(kind, q, where):
        send(to_send.at[kind, q], far.at[kind, p], gp_send.at[kind, q], gp_recv.at[kind, p], dev(q, t, s), where)

    def hop_of(kind, q):
        return remote(to_send.at[kind, q], hop.at[kind], hp_send.at[kind], hp_recv.at[kind], dev(2 - q // 2, t, s))

    def grad_push(kind, q):
        for c in near[kind, q]:
            c.wait_recv()

        @pl.when(p != q)
        def _():
            to_send[kind, q] = grad_of(kind, q).astype(BF16)

        if q in (0, 3):
            next_to, end = (1, 3) if q == 0 else (2, 0)
            c = hop_of(kind, q)
            pl.when(p == end)(c.start)
            pending.append((p == end, c))
            to_owner(kind, q, p == next_to)
        else:
            to_owner(kind, q, p != q)

    def grad_relay(kind, q):
        through = 2 if q == 0 else 1

        @pl.when(p == through)
        def _():
            hop_of(kind, q).wait_recv()
            to_send[kind, q] = (grad_of(kind, q) + hop[kind].astype(F32)).astype(BF16)

        to_owner(kind, q, p == through)

    def grad_relays(kind):
        grad_relay(kind, 0)
        grad_relay(kind, 3)

    def grad_all_near(kind):
        for q in range(TEAM):
            grad_near(kind, q)

    def grad_wide(kind):
        for q in (0, 3, 1, 2):
            grad_push(kind, q)

    def grad_end(kind):
        g_ref[kind] = grad_of(kind, p)
        for q in range(TEAM):
            @pl.when((p != q) & (p + q != 3 if q in (0, 3) else p != q))
            def _():
                remote(to_send.at[kind, q], far.at[kind, q], gp_send.at[kind, q], gp_recv.at[kind, q], dev(q, t, s)).wait_recv()
                g_ref[kind] += far[kind, q].astype(F32)

        store(g_ref.at[kind], (attn_out, gate_out, up_out, down_out)[kind])

    weights_arrive(DOWN, 2)
    g_part[DOWN] = dot_r(hidden[...], dexp_all[...]).astype(BF16)
    grad_all_near(DOWN)
    weights_forward(DOWN)
    weights_wait(DOWN)
    mark_down = len(pending)
    outs = {}
    for u in fold_order:
        fold(OUT, u, dot(hidden[seat(u), :], w_all[DOWN]), outs)
    grad_wide(DOWN)
    for c in range(width // chunk):
        cols = slice(c * chunk, (c + 1) * chunk)
        gs[...] = dot_t(dexp_all[...], w_all[DOWN, cols, :])

        def lower(r, carry):
            rr = pl.ds(pl.multiple_of(r * step, step), step)
            da = gs[rr, :]
            dg_s[rr, cols] = (da * dgu_s[rr, cols]).astype(BF16)
            du_s[rr, cols] = (da * ge_s[rr, cols]).astype(BF16)
            return carry

        lax.fori_loop(0, TEAM * rows // step, lower, 0)
    fold_on(OUT, outs)
    backs = {}
    for u in fold_order:
        fold(BACK, u, dot(dg_s[seat(u), :], w_all[GATE]) + dot(du_s[seat(u), :], w_all[UP]), backs)
    g_part[GATE] = dot_r(dg_s[...], h_all[...]).astype(BF16)
    grad_all_near(GATE)
    g_part[UP] = dot_r(du_s[...], h_all[...]).astype(BF16)
    grad_all_near(UP)
    grad_wide(GATE)
    grad_wide(UP)
    grad_relays(DOWN)
    fold_on(BACK, backs)

    upstream = dy_all[seat(t), :].astype(F32)
    probs = eprobs_s[...]
    _, cols = meta_of(t)
    picked = jnp.where((cols[:, 1:2] == lane_expert) | (cols[:, 2:3] == lane_expert), 1.0, 0.0)
    chosen = jnp.sum(probs * picked, axis=-1, keepdims=True)
    live = picked[:, 0:1] * jnp.where(cols[:, 0:1] >= 0.0, 1.0, 0.0)
    combine = probs[:, 0:1] * live / chosen
    mark_out = len(pending)
    expert = folded(OUT, outs)
    result_ref[...] = (middle_s[...] + combine * expert).astype(BF16)
    store(result_ref, result_out)
    d_combine = jnp.sum(expert * upstream, axis=-1, keepdims=True)
    first_hot = jnp.where(lane_expert == 0.0, 1.0, 0.0)
    ratio = probs[:, 0:1] / (chosen * chosen)
    d_probs = (d_combine * live) * (first_hot / chosen - ratio * picked)
    d_logits = probs * (d_probs - jnp.sum(d_probs * probs, axis=-1, keepdims=True))
    l_hi, l_lo = split_high(d_logits)
    l_lowest = (d_logits - l_hi.astype(F32) - l_lo.astype(F32)).astype(BF16)
    d_route = dot(l_hi, rhi[...]) + dot(l_hi, rlo[...]) + dot(l_lo, rhi[...])
    depth = sbuf.shape[0] // (TEAM * sub)
    h2 = h_all[seat(t), :]
    sbuf[...] = dot_r(l_hi, h2) + dot_r(l_lo, h2) + dot_r(l_lowest, h2)

    def piece(a, b):
        return pl.ds(pl.multiple_of((other(t, a, TEAM) * sub + other(s, b, sub)) * depth, depth), depth)

    first = [send(sbuf.at[piece(a, b), :], s_got.at[i], sa_send.at[i], sa_recv.at[i], plane[i]) for i, (a, b) in enumerate(ring)]
    drain(mark_down)
    grad_relays(GATE)
    d_second = folded(BACK, backs) + d_route
    middle = middle_s[...]
    scale = lax.rsqrt(jnp.mean(middle * middle, axis=-1, keepdims=True) + EPSILON)
    d_middle = upstream + norm_back(middle, scale, gain_two, d_second)
    dmid_s[...] = d_middle
    db_all[seat(t), :] = d_middle.astype(BF16)
    dbs = spread(DBRANCH, db_all)
    gain_two_sum = jnp.sum(d_second * middle * scale, axis=0, keepdims=True)
    score_s[...] = jnp.zeros(score_s.shape, F32)

    def attend_back(u):
        rows_u = seat(u)
        d_mix = dot_t(db_all[rows_u, :], w_all[ATTN, 3 * part:4 * part, :]).astype(BF16)
        q, key, v = q_all[rows_u, :], k_all[rows_u, :], v_all[rows_u, :]
        dq = jnp.zeros((rows, part), F32)
        dk = jnp.zeros((rows, part), F32)
        dv = jnp.zeros((rows, part), F32)
        for h in range(heads):
            weights = probs_all[h, rows_u, :]
            d_w = dot_t(jnp.where(lane_head == h, d_mix, zero_low), v)
            ds = (weights * (d_w - jnp.sum(weights * d_w, axis=-1, keepdims=True))).astype(BF16)
            dv = jnp.where(lane_head == h, dot_r(weights.astype(BF16), d_mix), dv)
            dq = jnp.where(lane_head == h, dot(ds, key), dq)
            dk = jnp.where(lane_head == h, dot_r(ds, q), dk)
            wide_ds = ds.astype(F32)
            score_s[h] = score_s[h] + wide_ds[:slots] + wide_ds[slots:]
        dq_all[rows_u, :] = (dq * factor).astype(BF16)
        dk_all[rows_u, :] = (dk * factor).astype(BF16)
        dv_all[rows_u, :] = dv.astype(BF16)

    norms = []
    gain_sum = jnp.zeros((1, width), F32)

    def norm_rows(k, u):
        rows_u = seat(u)
        value = (dot(dq_all[rows_u, :], w_all[ATTN, 0:part, :]) + dot(dk_all[rows_u, :], w_all[ATTN, part:2 * part, :])
                 + dot(dv_all[rows_u, :], w_all[ATTN, 2 * part:3 * part, :]))
        norms.extend(scatter(DNORM, k, value, u))
        return jnp.sum(value * unit_of(u), axis=0, keepdims=True)

    attend_back(t)
    gain_sum = gain_sum + norm_rows(0, t)
    spread_on(DBRANCH, db_all, dbs)
    total = sbuf[piece(0, 0), :]
    for i, c in enumerate(first):
        c.wait_recv()
        total = total + s_got[i]
    s_held[...] = total
    s_far[p] = total
    second = [send(s_held, s_far.at[p], sc_send.at[k], sc_recv.at[k], dev(other(p, k, TEAM), t, s)) for k in range(1, TEAM)]
    grad_relays(UP)
    drain(mark_out)
    for slot_u, (u, parts) in enumerate(spread_order):
        for i in parts:
            dbs[i].wait_recv()
        attend_back(u)
        gain_sum = gain_sum + norm_rows(slot_u + 1, u)

    for q, left, right in ((3, mixed, db_all), (0, dq_all, normed), (2, dv_all, normed), (1, dk_all, normed)):
        g_part[ATTN, q * part:(q + 1) * part, :] = dot_r(left[...], right[...]).astype(BF16)
        grad_near(ATTN, q)
    for q in (3, 0, 2, 1):
        grad_push(ATTN, q)
    for c in second:
        c.wait_recv()
    total = s_far[0]
    for k in range(1, TEAM):
        total = total + s_far[k]
    small_ref[piece(0, 0), :] = total
    mine_small = small_ref.at[piece(0, 0), :]
    third = [send(mine_small, mine_small, sd_send.at[i], sd_recv.at[i], plane[i]) for i in range(len(plane))]
    def gather_gap(d, carry):
        hit = gap == d
        for h in range(heads):
            gap_s[h, pl.ds(d, 1), :] = jnp.sum(jnp.where(hit, score_s[h], 0.0), axis=0, keepdims=True)
        return carry

    lax.fori_loop(0, slots, gather_gap, 0)
    lane = lax.broadcasted_iota(jnp.int32, (slots, 128), 1)
    by_gap = jnp.zeros((slots, 128), F32)
    for h in range(heads):
        by_gap = jnp.where(lane == heads * t + h, jnp.sum(gap_s[h], axis=-1, keepdims=True), by_gap)
    count = table_ref.shape[1]
    bucket_hit = jnp.where(lax.broadcasted_iota(jnp.int32, (count, slots), 0) == buckets_ref[...], 1.0, 0.0)
    l_own[0:count, :] = jnp.dot(bucket_hit, by_gap, precision=HIGHEST, preferred_element_type=F32)
    for i in range(width // 128):
        l_own[count + i:count + i + 1, :] = gain_sum[:, i * 128:(i + 1) * 128]
        j = count + width // 128 + i
        l_own[j:j + 1, :] = gain_two_sum[:, i * 128:(i + 1) * 128]
    used = count + 2 * (width // 128)
    l_own[used:, :] = jnp.zeros((l_own.shape[0] - used, 128), F32)
    late_a = [send(l_own, l_got.at[k - 1], la_send.at[k], la_recv.at[k], dev(p, mate(k), s)) for k in range(1, TEAM)]

    grad_relays(ATTN)
    grad_end(DOWN)
    for c in late_a:
        c.wait_recv()
    total = l_own[...]
    for k in range(1, TEAM):
        total = total + l_got[k - 1]
    l_sum[...] = total
    l_sib[s] = total
    late_b = [send(l_sum, l_sib.at[s], lb_send.at[j], lb_recv.at[j], dev(p, t, other(s, j, sub))) for j in range(1, sub)]
    grad_end(GATE)
    for c in late_b:
        c.wait_recv()
    total = l_sib[0]
    for j in range(1, sub):
        total = total + l_sib[j]
    l_tot[...] = total
    l_far[p] = total
    late_c = [send(l_tot, l_far.at[p], lc_send.at[k], lc_recv.at[k], dev(other(p, k, TEAM), t, s)) for k in range(1, TEAM)]
    grad_end(UP)

    x = tok_all[seat(t), :].astype(F32)
    d_normed = gathered(DNORM, norms)
    scale = lax.rsqrt(jnp.mean(x * x, axis=-1, keepdims=True) + EPSILON)
    dtok_ref[...] = (dmid_s[...] + norm_back(x, scale, gain_one, d_normed)).astype(BF16)
    store(dtok_ref, dtok_out)

    for c in late_c:
        c.wait_recv()
    total = l_far[0]
    for k in range(1, TEAM):
        total = total + l_far[k]
    table_s[...] = total[0:count, :].T[0:table_s.shape[0], :]
    store(table_s, table_out)
    parts = width // 128
    for i in range(2 * parts):
        gains_s[i // parts:i // parts + 1, (i % parts) * 128:(i % parts + 1) * 128] = total[count + i:count + i + 1, :]
    store(gains_s, gains_out)
    for c in third:
        c.wait_recv()
    store(small_ref, router_out)
    drain(len(pending))
    grad_end(ATTN)
    for c in stores:
        c.wait()


def finish_kernel(count, *refs):
    held, into, away = refs[2 * count:3 * count], refs[3 * count], refs[3 * count + 1]
    loads = [pltpu.make_async_copy(refs[i], held[i], into.at[i]) for i in range(count)]
    stores = [pltpu.make_async_copy(held[i], refs[count + i], away.at[i]) for i in range(count)]
    for c in loads:
        c.start()
    for load, keep in zip(loads, stores):
        load.wait()
        keep.start()
    for c in stores:
        c.wait()


def block(n, tokens, attn_weight, w_gate, w_up, w_down, norm_gains, bias_table, router,
          grad_out, segment, expert_ids, bucket_of):
    rows, width = tokens.shape
    shard = w_down.shape[0]
    sub = n // (TEAM * TEAM)
    head_count = bias_table.shape[1]
    heads = head_count // TEAM
    part = heads * (width // head_count)
    slots = bucket_of.shape[0]
    routed = router.shape[1]
    every = TEAM * rows
    dma = pltpu.SemaphoreType.DMA
    shape = jax.ShapeDtypeStruct
    buf = pltpu.VMEM
    depth = routed // (TEAM * sub)
    lines = -(-(bias_table.shape[0] + 2 * (width // 128)) // 8) * 8
    smem = pl.BlockSpec(memory_space=pltpu.SMEM)
    grad = shape((shard, width), F32)
    shapes = (shape(tokens.shape, BF16), shape(tokens.shape, BF16), grad, grad, grad, grad, shape(norm_gains.shape, F32),
              shape(bias_table.shape[::-1], F32), shape(router.shape[::-1], F32))
    outs = pl.pallas_call(
        functools.partial(block_kernel, n, head_count),
        out_shape=shapes,
        in_specs=[HBM] * 11 + [smem] * 2,
        out_specs=(HBM,) * len(shapes),
        scratch_shapes=[
            buf((1, rows), jnp.int32), buf((2, rows), jnp.int32), buf(norm_gains.shape, F32), buf((routed, width), F32),
            buf((1, slots), jnp.int32), buf((rows, width), BF16), buf((rows, width), BF16), buf((4, shard, width), F32),
            buf((routed, width), F32), buf(norm_gains.shape, F32), buf(bias_table.shape[::-1], F32), dma((11,)), dma((9,)),
            buf((4, width, width), BF16), buf((4, width, width), BF16), buf((4, sub - 1, TEAM, shard, width), BF16),
            buf((4, TEAM, shard, width), BF16), buf((4, TEAM, shard, width), BF16), buf((4, shard, width), BF16),
            buf((every, width), BF16), buf((every, width), BF16), buf((TEAM * LINES, rows), F32), buf((every, width), BF16),
            buf((every, part), BF16), buf((every, part), BF16), buf((every, part), BF16), buf((every, part), BF16),
            buf((heads, every, rows), F32), buf((heads, slots, 2 * slots), F32),
            buf((4, TEAM - 1, rows, width), BF16), buf((4, TEAM - 1, rows, width), BF16), buf((3, 2, rows // 2, width), BF16),
            buf((3, 2, rows // 2, width), F32), buf((4, rows, width), F32),
            buf((rows, width), F32), buf((every, width), BF16), buf((every, width), BF16), buf((rows, 128), F32),
            buf((rows, routed), F32), buf((routed, width), BF16), buf((routed, width), BF16),
            buf((every, 256), F32), buf((every, 256), F32), buf((every, width), BF16), buf((every, width), F32),
            buf((every, width), F32), buf((every, width), BF16), buf((every, width), BF16), buf((rows, width), F32),
            buf((every, width), BF16), buf((every, part), BF16), buf((every, part), BF16), buf((every, part), BF16),
            buf((heads, slots, 2 * slots), F32), buf((heads, slots, 2 * slots), F32),
            buf((routed, width), F32), buf((TEAM * sub - 1, depth, width), F32),
            buf((depth, width), F32), buf((TEAM, depth, width), F32),
            buf((lines, 128), F32), buf((TEAM - 1, lines, 128), F32), buf((lines, 128), F32),
            buf((sub, lines, 128), F32), buf((lines, 128), F32), buf((TEAM, lines, 128), F32),
            dma((9, 8)), dma((9, 8)), dma((4, TEAM)), dma((4, TEAM)), dma((4, TEAM, sub)), dma((4, TEAM, sub)),
            dma((4, TEAM, sub)), dma((4, TEAM, sub)), dma((4, TEAM)), dma((4, TEAM)), dma((4,)), dma((4,)),
            dma((TEAM * sub,)), dma((TEAM * sub,)), dma((TEAM,)), dma((TEAM,)), dma((TEAM * sub,)), dma((TEAM * sub,)),
            dma((TEAM,)), dma((TEAM,)), dma((sub,)), dma((sub,)), dma((TEAM,)), dma((TEAM,)),
        ],
        compiler_params=pltpu.CompilerParams(collective_id=0, has_side_effects=True, vmem_limit_bytes=56 * 2**20),
        name="block",
    )(attn_weight.T, w_gate.T, w_up.T, w_down, tokens, grad_out, segment.reshape(1, rows), expert_ids.T, norm_gains,
      router.T, bucket_of.reshape(1, slots), bias_table.T, bucket_of)
    result, dtok, g_attn, g_gate, g_up, g_down, gains, table, routes = pl.pallas_call(
        functools.partial(finish_kernel, len(shapes)),
        out_shape=shapes,
        in_specs=[HBM] * len(shapes),
        out_specs=(HBM,) * len(shapes),
        scratch_shapes=[buf(v.shape, v.dtype) for v in shapes] + [dma((len(shapes),)), dma((len(shapes),))],
        name="finish",
    )(*outs)
    return result, dtok, g_attn.T, g_gate.T, g_up.T, g_down, gains, table.T, routes.T


def solution(mesh):
    n = mesh.shape["fsdp"]
    row, col = P("fsdp", None), P(None, "fsdp")
    in_specs = (row, col, col, col, row, P(), P(), P(), row, P("fsdp"), row, P())
    out_specs = (row, row, col, col, col, row, P(), P(), P())

    def run(*args):
        shard, rows = args[4].shape[0] // n, args[0].shape[0] // n
        whole_tiles = shard % 16 == 0 and rows == 2 * args[11].shape[0] and args[7].shape[1] % (n // 2) == 0
        return jax.shard_map(
            functools.partial(block if whole_tiles else body, n),
            mesh=mesh, in_specs=in_specs, out_specs=out_specs, check_vma=False,
        )(*args)

    return run
```

```python
import functools
import math
import jax
import jax.numpy as jnp
from jax import lax
from jax.experimental import pallas as pl
from jax.experimental.pallas import tpu as pltpu
from jax.sharding import PartitionSpec as P

EPSILON = 1e-06
HIGHEST = lax.Precision.HIGHEST
MESH = pl.DeviceIdType.MESH
TEAM = 4
F32 = jnp.float32
BF16 = jnp.bfloat16
VMEM = pl.BlockSpec(memory_space=pltpu.VMEM)
ANY = pl.BlockSpec(memory_space=pl.ANY)
HBM = pl.BlockSpec(memory_space=pltpu.HBM)
CONTRACT_ROWS = (((0,), (0,)), ((), ()))
CONTRACT_COLS = (((1,), (1,)), ((), ()))


def place(n):
    sub = n // (TEAM * TEAM)
    me = lax.axis_index("fsdp")
    p = me // (TEAM * sub)
    t = lax.rem(me // sub, TEAM)
    s = lax.rem(me, sub)
    return sub, p, t, s, (lambda p, t, s: (p * (TEAM * sub) + t * sub + s,))


def greet(peers):
    barrier = pltpu.get_barrier_semaphore()
    for peer in peers:
        pl.semaphore_signal(barrier, inc=1, device_id=peer, device_id_type=MESH)
    pl.semaphore_wait(barrier, len(peers))


def remote(src, dst, send, recv, peer):
    return pltpu.make_async_remote_copy(
        src_ref=src, dst_ref=dst, send_sem=send, recv_sem=recv, device_id=peer, device_id_type=MESH
    )


def other(index, step, count):
    return lax.rem(index + step, count)


def spread_peers(sub, p, t, s, dev):
    peers = [dev(other(p, k, TEAM), t, s) for k in range(1, TEAM)]
    return peers + [dev(p, t, other(s, k, sub)) for k in range(1, sub)]


def team_peers(p, t, s, dev):
    return [dev(p, other(t, k, TEAM), s) for k in range(1, TEAM)]


def weights_start(n, w_ref, w_all, sems):
    sub, p, t, s, dev = place(n)
    p_send, p_recv, s_send, s_recv, own_sem = sems
    wide, near, local = [], [], []
    for i in range(w_ref.shape[0]):
        for k in range(1, TEAM):
            c = remote(w_ref.at[i], w_all.at[i, p, s], p_send.at[i, k], p_recv.at[i, k],
                       dev(other(p, k, TEAM), t, s))
            c.start()
            wide.append(c)
    for i in range(w_ref.shape[0]):
        for k in range(1, sub):
            c = remote(w_ref.at[i], w_all.at[i, p, s], s_send.at[i, 0, k], s_recv.at[i, 0, k],
                       dev(p, t, other(s, k, sub)))
            c.start()
            near.append(c)
        c = pltpu.make_async_copy(w_ref.at[i], w_all.at[i, p, s], own_sem.at[i])
        c.start()
        local.append(c)
    return wide, near, local


def weights_finish(n, w_all, sems, state):
    sub, p, t, s, dev = place(n)
    _, _, s_send, s_recv, _ = sems
    wide, near, local = state
    for i in range(w_all.shape[0]):
        for k in range(1, TEAM):
            wide[i * (TEAM - 1) + k - 1].wait_recv()
            q = other(p, TEAM - k, TEAM)
            for j in range(1, sub):
                c = remote(w_all.at[i, q, s], w_all.at[i, q, s], s_send.at[i, k, j], s_recv.at[i, k, j],
                           dev(p, t, other(s, j, sub)))
                c.start()
                near.append(c)
    for c in wide:
        c.wait_send()
    for c in near:
        c.wait()
    for c in local:
        c.wait()


def weights_sems(n, kinds):
    sub = n // (TEAM * TEAM)
    dma = pltpu.SemaphoreType.DMA
    return [dma((kinds, TEAM)), dma((kinds, TEAM)), dma((kinds, TEAM, sub)), dma((kinds, TEAM, sub)), dma((kinds,))]


def weights_shape(n, w):
    return jax.ShapeDtypeStruct((w.shape[0], TEAM, n // (TEAM * TEAM)) + w.shape[1:], w.dtype)


def gather_kernel(n, w_ref, tok_ref, dy_ref, meta_ref, w_all, tok_all, dy_all, meta_all,
                  t_send, t_recv, own_sem, *sems):
    sub, p, t, s, dev = place(n)
    greet(spread_peers(sub, p, t, s, dev) + team_peers(p, t, s, dev))
    state = weights_start(n, w_ref, w_all, sems)
    copies, local = [], []
    for i, (src, dst) in enumerate(((tok_ref, tok_all), (dy_ref, dy_all), (meta_ref, meta_all))):
        for k in range(1, TEAM):
            c = remote(src, dst.at[t], t_send.at[i, k], t_recv.at[i, k], dev(p, other(t, k, TEAM), s))
            c.start()
            copies.append(c)
        c = pltpu.make_async_copy(src, dst.at[t], own_sem.at[i])
        c.start()
        local.append(c)
    weights_finish(n, w_all, sems, state)
    for c in copies:
        c.wait()
    for c in local:
        c.wait()


def gather(n, w, tok, dy, meta):
    dma = pltpu.SemaphoreType.DMA
    shape = jax.ShapeDtypeStruct
    return pl.pallas_call(
        functools.partial(gather_kernel, n),
        out_shape=(
            weights_shape(n, w),
            shape((TEAM,) + tok.shape, BF16),
            shape((TEAM,) + dy.shape, BF16),
            shape((TEAM,) + meta.shape, jnp.int32),
        ),
        in_specs=[VMEM] * 4,
        out_specs=(ANY,) * 4,
        scratch_shapes=[dma((3, TEAM)), dma((3, TEAM)), dma((3,))] + weights_sems(n, w.shape[0]),
        compiler_params=pltpu.CompilerParams(collective_id=0, has_side_effects=True),
        name="gather_all",
    )(w, tok, dy, meta)


def middle_kernel(n, part_ref, x_ref, gain_ref, w_ref, y_ref, h_all, w_all, got, held,
                  a_send, a_recv, b_send, b_recv, own_sem, *sems):
    sub, p, t, s, dev = place(n)
    greet(spread_peers(sub, p, t, s, dev) + team_peers(p, t, s, dev))
    copies = []
    for k in range(1, TEAM):
        u = other(t, k, TEAM)
        c = remote(part_ref.at[u], got.at[k - 1], a_send.at[k], a_recv.at[k], dev(p, u, s))
        c.start()
        copies.append(c)
    state = weights_start(n, w_ref, w_all, sems)
    total = x_ref[...].astype(F32) + part_ref[t].astype(F32)
    for k in range(1, TEAM):
        copies[k - 1].wait_recv()
        total = total + got[k - 1].astype(F32)
    y_ref[...] = total
    scale = lax.rsqrt(jnp.mean(total * total, axis=-1, keepdims=True) + EPSILON)
    held[...] = (total * scale * gain_ref[1:2, :]).astype(BF16)
    local = pltpu.make_async_copy(held, h_all.at[t], own_sem)
    local.start()
    sends = []
    for k in range(1, TEAM):
        c = remote(held, h_all.at[t], b_send.at[k], b_recv.at[k], dev(p, other(t, k, TEAM), s))
        c.start()
        sends.append(c)
    weights_finish(n, w_all, sems, state)
    for c in copies:
        c.wait_send()
    for c in sends:
        c.wait()
    local.wait()


def middle_exchange(n, part, x, gains, w):
    dma = pltpu.SemaphoreType.DMA
    shape = jax.ShapeDtypeStruct
    return pl.pallas_call(
        functools.partial(middle_kernel, n),
        out_shape=(shape(x.shape, F32), shape((TEAM,) + x.shape, BF16), weights_shape(n, w)),
        in_specs=[VMEM] * 4,
        out_specs=(VMEM, ANY, ANY),
        scratch_shapes=[pltpu.VMEM((TEAM - 1,) + x.shape, BF16), pltpu.VMEM(x.shape, BF16),
                        dma((TEAM,)), dma((TEAM,)), dma((TEAM,)), dma((TEAM,)), dma] + weights_sems(n, w.shape[0]),
        compiler_params=pltpu.CompilerParams(collective_id=1, has_side_effects=True),
        name="middle_exchange",
    )(part, x, gains, w)


def reduce_kernel(n, m, h, gain_row, *refs):
    parts, rows, grad_ref = refs[:m], refs[m:m + h], refs[m + h]
    refs = refs[m + h + 1:]
    small = gain_row is not None
    if small:
        unit_ref, small_ref = refs[:2]
        refs = refs[2:]
    outs, rows_all, grad_out = refs[:m], refs[m:m + h], refs[m + h]
    if small:
        small_out = refs[m + h + 1]
        refs = refs[:m + h + 1] + refs[m + h + 2:]
    (got, sib, to_send, far, t_send, t_recv, h_send, h_recv, own_sem,
     s_send, s_recv, p_send, p_recv) = refs[m + h + 1:m + h + 14]
    rest = refs[m + h + 14:]
    sub, p, t, s, dev = place(n)
    greet(spread_peers(sub, p, t, s, dev) + team_peers(p, t, s, dev))
    kinds = grad_ref.shape[0]
    near, tokens, wide, shared, local = [], [], [], [], []
    for kind in range(kinds):
        for k in range(1, sub):
            v = other(s, k, sub)
            c = remote(grad_ref.at[kind, :, v], sib.at[kind, k - 1], s_send.at[kind, k], s_recv.at[kind, k],
                       dev(p, t, v))
            c.start()
            near.append(c)
    for i in range(h):
        for k in range(1, TEAM):
            c = remote(rows[i], rows_all[i].at[t], h_send.at[i, k], h_recv.at[i, k],
                       dev(p, other(t, k, TEAM), s))
            c.start()
            shared.append(c)
        c = pltpu.make_async_copy(rows[i], rows_all[i].at[t], own_sem.at[i])
        c.start()
        local.append(c)
    for i in range(m):
        for k in range(1, TEAM):
            u = other(t, k, TEAM)
            c = remote(parts[i].at[u], got.at[i, k - 1], t_send.at[i, k], t_recv.at[i, k], dev(p, u, s))
            c.start()
            tokens.append(c)
    for kind in range(kinds):
        for c in near[kind * (sub - 1):(kind + 1) * (sub - 1)]:
            c.wait_recv()
        for k in range(1, TEAM):
            q = other(p, k, TEAM)
            total = grad_ref[kind, q, s].astype(F32)
            for j in range(1, sub):
                total = total + sib[kind, j - 1, q].astype(F32)
            to_send[kind, k - 1] = total.astype(BF16)
            c = remote(to_send.at[kind, k - 1], far.at[kind, k - 1], p_send.at[kind, k], p_recv.at[kind, k],
                       dev(q, t, s))
            c.start()
            wide.append(c)
    for i in range(m):
        total = parts[i][t].astype(F32)
        for k in range(1, TEAM):
            tokens[i * (TEAM - 1) + k - 1].wait_recv()
            total = total + got[i, k - 1].astype(F32)
        outs[i][...] = total
    if small:
        buf = rest[0]
        piece, line = divmod(gain_row, small_ref.shape[1])
        gain = jnp.sum(outs[0][...] * unit_ref[...], axis=0, keepdims=True)
        buf[...] = small_ref[...]
        buf[piece, line:line + 1, :] = gain
        small_phases(n, buf, small_out, *rest[1:])
    for kind in range(kinds):
        for c in wide[kind * (TEAM - 1):(kind + 1) * (TEAM - 1)]:
            c.wait_recv()
        total = grad_ref[kind, p, s].astype(F32)
        for j in range(1, sub):
            total = total + sib[kind, j - 1, p].astype(F32)
        for k in range(1, TEAM):
            total = total + far[kind, k - 1].astype(F32)
        grad_out[kind] = total
    for c in near + tokens + wide:
        c.wait_send()
    for c in shared:
        c.wait()
    for c in local:
        c.wait()


def reduce_exchange(n, parts, rows, grads, ident, small=(), gain_row=None):
    sub = n // (TEAM * TEAM)
    m, h = len(parts), len(rows)
    dma = pltpu.SemaphoreType.DMA
    shape = jax.ShapeDtypeStruct
    block = parts[0].shape[1:] if m else (8, 128)
    kinds, tile = grads.shape[0], grads.shape[3:]
    outs = pl.pallas_call(
        functools.partial(reduce_kernel, n, m, h, gain_row),
        out_shape=(shape(block, F32),) * m
        + tuple(shape((TEAM,) + v.shape, v.dtype) for v in rows)
        + (shape((kinds,) + tile, F32),)
        + tuple(shape(v.shape, F32) for v in small[1:]),
        in_specs=[VMEM] * (m + h + 1 + len(small)),
        out_specs=(VMEM,) * m + (ANY,) * h + (VMEM,) * (1 + len(small[1:])),
        scratch_shapes=[
            pltpu.VMEM((max(m, 1), TEAM - 1) + block, BF16),
            pltpu.VMEM((kinds, sub - 1, TEAM) + tile, BF16),
            pltpu.VMEM((kinds, TEAM - 1) + tile, BF16),
            pltpu.VMEM((kinds, TEAM - 1) + tile, BF16),
            dma((max(m, 1), TEAM)), dma((max(m, 1), TEAM)),
            dma((max(h, 1), TEAM)), dma((max(h, 1), TEAM)), dma((max(h, 1),)),
            dma((kinds, sub)), dma((kinds, sub)), dma((kinds, TEAM)), dma((kinds, TEAM)),
        ] + (small_scratch(n, small[1].shape) if small else []),
        compiler_params=pltpu.CompilerParams(collective_id=ident, has_side_effects=True),
        name=f"reduce_{ident}",
    )(*parts, *rows, grads, *small)
    return (outs[:m], outs[m:m + h]) + tuple(outs[m + h:])


def small_phases(n, buf, out_ref, got, mine, sib, held, far,
                 a_send, a_recv, s_send, s_recv, b_send, b_recv, c_send, c_recv):
    sub, p, t, s, dev = place(n)
    first, near, second, third = [], [], [], []
    for k in range(1, TEAM):
        u = other(t, k, TEAM)
        c = remote(buf.at[u], got.at[k - 1], a_send.at[k], a_recv.at[k], dev(p, u, s))
        c.start()
        first.append(c)
    total = buf[t]
    for k in range(1, TEAM):
        first[k - 1].wait_recv()
        total = total + got[k - 1]
    mine[...] = total
    sib[s] = total
    for k in range(1, sub):
        c = remote(mine, sib.at[s], s_send.at[k], s_recv.at[k], dev(p, t, other(s, k, sub)))
        c.start()
        near.append(c)
    for c in near:
        c.wait_recv()
    total = sib[0]
    for k in range(1, sub):
        total = total + sib[k]
    held[...] = total
    far[p] = total
    for k in range(1, TEAM):
        c = remote(held, far.at[p], b_send.at[k], b_recv.at[k], dev(other(p, k, TEAM), t, s))
        c.start()
        second.append(c)
    for c in second:
        c.wait_recv()
    total = far[0]
    for k in range(1, TEAM):
        total = total + far[k]
    out_ref[t] = total
    for k in range(1, TEAM):
        c = remote(out_ref.at[t], out_ref.at[t], c_send.at[k], c_recv.at[k], dev(p, other(t, k, TEAM), s))
        c.start()
        third.append(c)
    for c in first + near + second:
        c.wait_send()
    for c in third:
        c.wait()


def small_scratch(n, shape):
    sub = n // (TEAM * TEAM)
    dma = pltpu.SemaphoreType.DMA
    tile = shape[1:]
    return [pltpu.VMEM(shape, F32), pltpu.VMEM((TEAM - 1,) + tile, F32), pltpu.VMEM(tile, F32),
            pltpu.VMEM((sub,) + tile, F32), pltpu.VMEM(tile, F32), pltpu.VMEM((TEAM,) + tile, F32),
            dma((TEAM,)), dma((TEAM,)), dma((sub,)), dma((sub,))] + [dma((TEAM,))] * 4


def gelu_tanh(inner):
    return jax.nn.gelu(inner, approximate=True)


def norm_back(inputs, scale, gain, upstream):
    weighted = gain * upstream
    return scale * weighted - inputs * scale * scale * scale * jnp.mean(
        weighted * inputs, axis=-1, keepdims=True
    )


def dot_t(a, b):
    return lax.dot_general(a, b, CONTRACT_COLS, preferred_element_type=F32)


def dot_r(a, b):
    return lax.dot_general(a, b, CONTRACT_ROWS, preferred_element_type=F32)


def dot(a, b):
    return jnp.dot(a, b, preferred_element_type=F32)


def body(n, tokens, attn_weight, w_gate, w_up, w_down, norm_gains, bias_table, router,
         grad_out, segment, expert_ids, bucket_of):
    rows, width = tokens.shape
    slots = bucket_of.shape[0]
    routed = router.shape[1]
    buckets, head_count = bias_table.shape
    head_width = width // head_count
    factor = head_width ** (-0.5)
    heads = head_count // TEAM
    part = heads * head_width
    sub, _, t, _, _ = place(n)
    all_rows = TEAM * rows
    spans = all_rows // slots

    early = jnp.stack([attn_weight.T, w_down])
    late = jnp.stack([w_gate.T, w_up.T])
    meta = jnp.concatenate([segment[None], expert_ids.T, jnp.zeros((5, rows), jnp.int32)], axis=0)
    w_all, tok_all, dy_all, meta_all = gather(n, early, tokens, grad_out, meta)
    w_all = w_all.reshape(2, -1, width)
    attn_t, down = w_all[0], w_all[1]
    qkv_t, out_t = attn_t[: 3 * part], attn_t[3 * part :]
    inputs = tok_all.reshape(all_rows, width).astype(F32)
    segments = meta_all[:, 0, :].reshape(all_rows)
    id_a = meta_all[:, 1, :].reshape(all_rows)
    id_b = meta_all[:, 2, :].reshape(all_rows)

    places = jnp.arange(slots)
    gap = places[:, None] - places[None, :]
    causal = gap >= 0
    gap_hit = (gap[:, :, None] == places[None, None, :]).astype(F32)
    bucket_hit = (bucket_of[:, None] == jnp.arange(buckets)[None, :]).astype(F32)
    table_mine = lax.dynamic_slice(bias_table, (0, heads * t), (buckets, heads))
    by_gap = jnp.dot(bucket_hit, table_mine, precision=HIGHEST)
    offsets = jnp.einsum("ijd,dh->hij", gap_hit, by_gap, precision=HIGHEST)

    scale_one = lax.rsqrt(jnp.mean(inputs * inputs, axis=-1, keepdims=True) + EPSILON)
    normed = (inputs * scale_one * norm_gains[0]).astype(BF16)
    triple = dot_t(normed, qkv_t).astype(BF16)
    heads_of = lambda v: v.reshape(spans, slots, heads, head_width)
    query = heads_of(triple[:, :part])
    keyset = heads_of(triple[:, part : 2 * part])
    valueset = heads_of(triple[:, 2 * part :])
    seg = segments.reshape(spans, slots)
    allowed = (seg[:, :, None] == seg[:, None, :]) & causal[None]
    raw = jnp.einsum("bihd,bjhd->bhij", query, keyset, preferred_element_type=F32)
    scores = jnp.where(allowed[:, None], raw * factor + offsets[None], -1e30)
    peak = jnp.max(scores, axis=-1, keepdims=True)
    lifted_scores = jnp.exp(scores - peak)
    weights = lifted_scores / jnp.sum(lifted_scores, axis=-1, keepdims=True)
    weights_low = weights.astype(BF16)
    mixed = jnp.einsum("bhij,bjhd->bihd", weights_low, valueset, preferred_element_type=F32)
    mixed = mixed.reshape(all_rows, part).astype(BF16)
    branch = dot(mixed, out_t).astype(BF16).reshape(TEAM, rows, width)
    middle, second_all, late_all = middle_exchange(n, branch, tokens, norm_gains, late)
    late_all = late_all.reshape(2, -1, width)
    gate_t, up_t = late_all[0], late_all[1]
    second_all = second_all.reshape(all_rows, width)

    second_wide = second_all.astype(F32)
    probs_all = jax.nn.softmax(jnp.dot(second_wide, router, precision=HIGHEST), axis=-1)
    lanes = jnp.arange(routed)[None, :]
    picked_all = jnp.where((id_a[:, None] == lanes) | (id_b[:, None] == lanes), 1.0, 0.0)
    total_all = jnp.sum(probs_all * picked_all, axis=-1)
    live_all = picked_all[:, 0] * jnp.where(segments >= 0, 1.0, 0.0)
    combine_all = probs_all[:, 0] * live_all / total_all
    gated = dot_t(second_all, gate_t)
    lifted = dot_t(second_all, up_t)
    activated, gelu_back = jax.vjp(gelu_tanh, gated)
    hidden = (activated * lifted).astype(BF16)
    out_part = dot(hidden, down).astype(BF16).reshape(TEAM, rows, width)
    d_expert = (combine_all[:, None] * dy_all.reshape(all_rows, width).astype(F32)).astype(BF16)
    d_hidden = dot_t(d_expert, down)
    d_gated = gelu_back(d_hidden * lifted)[0].astype(BF16)
    d_lifted = (d_hidden * activated).astype(BF16)
    back_part = (dot(d_gated, gate_t) + dot(d_lifted, up_t)).astype(BF16).reshape(TEAM, rows, width)
    grad_ffn = jnp.stack(
        [dot_r(d_gated, second_all).astype(BF16), dot_r(d_lifted, second_all).astype(BF16)]
    ).reshape(2, TEAM, sub, -1, width)
    (expert_out, d_second), _, g_ffn = reduce_exchange(n, (out_part, back_part), (), grad_ffn, 2)
    grad_down = dot_r(hidden, d_expert).astype(BF16).reshape(1, TEAM, sub, -1, width)

    mine = lambda v: lax.dynamic_slice_in_dim(v, t * rows, rows, 0)
    second, probs, picked = mine(second_wide), mine(probs_all), mine(picked_all)
    chosen_total, live, combine = mine(total_all), mine(live_all), mine(combine_all)
    upstream = grad_out.astype(F32)
    result = (middle + combine[:, None] * expert_out).astype(BF16)
    d_combine = jnp.sum(expert_out * upstream, axis=-1)
    first_hot = jnp.where(jnp.arange(routed) == 0, 1.0, 0.0)
    ratio = probs[:, 0] / (chosen_total * chosen_total)
    d_probs = (d_combine * live)[:, None] * (
        first_hot[None, :] / chosen_total[:, None] - ratio[:, None] * picked
    )
    d_logits = probs * (d_probs - jnp.sum(d_probs * probs, axis=-1, keepdims=True))
    grad_router_t = lax.dot_general(d_logits, second, CONTRACT_ROWS, precision=HIGHEST)
    d_second = d_second + jnp.dot(d_logits, router.T, precision=HIGHEST)
    scale_two = lax.rsqrt(jnp.mean(middle * middle, axis=-1, keepdims=True) + EPSILON)
    gain_two = jnp.sum(d_second * middle * scale_two, axis=0)
    d_middle = upstream + norm_back(middle, scale_two, norm_gains[1], d_second)
    _, (d_branch,), g_down = reduce_exchange(n, (), (d_middle.astype(BF16),), grad_down, 3)
    d_branch = d_branch.reshape(all_rows, width)

    grad_out_t = dot_r(mixed, d_branch)
    d_mixed = heads_of(dot_t(d_branch, out_t).astype(BF16))
    d_weights = jnp.einsum("bihd,bjhd->bhij", d_mixed, valueset, preferred_element_type=F32)
    d_values = jnp.einsum("bhij,bihd->bjhd", weights_low, d_mixed, preferred_element_type=F32)
    d_scores = weights * (d_weights - jnp.sum(weights * d_weights, axis=-1, keepdims=True))
    d_scores = d_scores.astype(BF16)
    d_query = jnp.einsum("bhij,bjhd->bihd", d_scores, keyset, preferred_element_type=F32) * factor
    d_keys = jnp.einsum("bhij,bihd->bjhd", d_scores, query, preferred_element_type=F32) * factor
    score_sum = jnp.sum(d_scores.astype(F32), axis=0)
    gap_sum = jnp.einsum("hij,ijd->dh", score_sum, gap_hit, precision=HIGHEST)
    table_part = lax.dot_general(bucket_hit, gap_sum, CONTRACT_ROWS, precision=HIGHEST)
    grad_table = lax.dynamic_update_slice(jnp.zeros(bias_table.shape, F32), table_part, (0, heads * t))
    flat = lambda v: v.reshape(all_rows, part).astype(BF16)
    d_triple = jnp.concatenate([flat(d_query), flat(d_keys), flat(d_values)], axis=1)
    grad_in_t = dot_r(d_triple, normed)
    grad_attn = jnp.concatenate([grad_in_t, grad_out_t], axis=0).astype(BF16)
    grad_attn = grad_attn.reshape(1, TEAM, sub, -1, width)
    d_normed_part = dot(d_triple, qkv_t).astype(BF16).reshape(TEAM, rows, width)
    own_inputs = tokens.astype(F32)
    own_scale = mine(scale_one)
    table_flat = grad_table.reshape(-1)
    lines = -(-table_flat.shape[0] // width)
    table_rows = jnp.pad(table_flat, (0, lines * width - table_flat.shape[0])).reshape(lines, width)
    small = jnp.concatenate([grad_router_t, jnp.zeros((1, width), F32), gain_two[None], table_rows], axis=0)
    depth = -(-small.shape[0] // (8 * TEAM)) * 8
    small = jnp.pad(small, ((0, depth * TEAM - small.shape[0]), (0, 0))).reshape(TEAM, depth, width)
    (d_normed,), _, g_attn, small = reduce_exchange(
        n, (d_normed_part,), (), grad_attn, 4, (own_inputs * own_scale, small), routed
    )
    small = small.reshape(TEAM * depth, width)
    input_grad = (d_middle + norm_back(own_inputs, own_scale, norm_gains[0], d_normed)).astype(BF16)
    grad_router = small[:routed].T
    grad_gains = small[routed : routed + 2]
    grad_table = small[routed + 2 : routed + 2 + lines].reshape(-1)[: table_flat.shape[0]].reshape(bias_table.shape)
    return (result, input_grad, g_attn[0].T, g_ffn[0].T, g_ffn[1].T, g_down[0],
            grad_gains, grad_table, grad_router)


LINES = 8
TOK, DY, META, BRANCH, SECOND, OUT, BACK, DBRANCH, DNORM = range(9)
ATTN, GATE, UP, DOWN = range(4)


def split_high(v):
    high = v.astype(BF16)
    return high, (v - high.astype(F32)).astype(BF16)


def eye(size, dtype):
    row = lax.broadcasted_iota(jnp.int32, (size, size), 0)
    col = lax.broadcasted_iota(jnp.int32, (size, size), 1)
    return jnp.where(row == col, 1.0, 0.0).astype(dtype)


def block_kernel(
    n, head_count,
    attn_in, gate_in, up_in, down_in, tok_in, dy_in, seg_in, ids_in, gains_in, router_in, buckets_in, table_ref, bucket_ref,
    result_out, dtok_out, attn_out, gate_out, up_out, down_out, gains_out, table_out, router_out,
    seg_ref, ids_ref, gains_ref, router_ref, buckets_ref, result_ref, dtok_ref, g_ref, small_ref, gains_s, table_s, in_sem, out_sem,
    w_all, g_part, sib, to_send, far, hop,
    tok_all, dy_all, meta_all, normed, q_all, k_all, v_all, mixed, probs_all, offs,
    row_send, row_got, passed, kept, own_part, middle_s, h_all, dexp_all, coef_s, eprobs_s, rhi, rlo,
    gs, us, hidden, ge_s, dgu_s, dg_s, du_s, dmid_s, db_all, dq_all, dk_all, dv_all, score_s, gap_s,
    sbuf, s_got, s_held, s_far, l_own, l_got, l_sum, l_sib, l_tot, l_far,
    t_send, t_recv, z_send, z_recv, ws_send, ws_recv, gs_send, gs_recv, gp_send, gp_recv, hp_send, hp_recv,
    sa_send, sa_recv, sc_send, sc_recv, sd_send, sd_recv,
    la_send, la_recv, lb_send, lb_recv, lc_send, lc_recv,
):
    sub, p, t, s, dev = place(n)
    rows, width = tok_in.shape
    shard = down_in.shape[0]
    heads = head_count // TEAM
    head_width = width // head_count
    part = heads * head_width
    factor = head_width ** (-0.5)
    slots = buckets_ref.shape[1]
    routed = router_ref.shape[0]
    chunk = 256

    barrier = pltpu.get_barrier_semaphore()
    ring = [(a, b) for a in range(TEAM) for b in range(sub)][1:]
    plane = [dev(p, other(t, a, TEAM), other(s, b, sub)) for a, b in ring]
    peers = plane + [dev(other(p, k, TEAM), t, s) for k in range(1, TEAM)]
    for peer in peers:
        pl.semaphore_signal(barrier, inc=1, device_id=peer, device_id_type=MESH)

    def mate(k):
        return other(t, k, TEAM)

    def seat(u):
        return pl.ds(pl.multiple_of(u * rows, rows), rows)

    def lot(q, v):
        return pl.ds(pl.multiple_of((q * sub + v) * shard, shard), shard)

    pending = []
    waited = [0]

    def drain(upto):
        for where, c in pending[waited[0]:upto]:
            if where is None:
                c.wait_send()
            else:
                pl.when(where)(c.wait_send)
        waited[0] = upto

    def send(src, dst, ssem, rsem, peer, where=None):
        c = remote(src, dst, ssem, rsem, peer)
        if where is None:
            c.start()
        else:
            pl.when(where)(c.start)
        pending.append((where, c))
        return c

    slot = {BRANCH: 0, OUT: 1, BACK: 2, DNORM: 3}
    beside = t + 1 - 2 * lax.rem(t, 2)
    across = other(t, 2, TEAM)
    corner = TEAM - 1 - t
    half = rows // 2

    def half_seat(u, i):
        return pl.ds(pl.multiple_of(u * rows + i * half, half), half)

    def team(kind, slot, src, dst, u):
        return send(src, dst, t_send.at[kind, slot], t_recv.at[kind, slot], dev(p, u, s))

    def spread(kind, whole):
        first, last = whole.at[half_seat(t, 0), :], whole.at[half_seat(t, 1), :]
        return {1: team(kind, 1, first, first, beside), 3: team(kind, 3, last, last, across),
                2: team(kind, 2, last, last, beside), 4: team(kind, 4, first, first, across)}

    def spread_on(kind, whole, copies):
        copies[1].wait_recv()
        block = whole.at[half_seat(beside, 0), :]
        copies[5] = team(kind, 5, block, block, across)
        copies[3].wait_recv()
        block = whole.at[half_seat(across, 1), :]
        copies[6] = team(kind, 6, block, block, beside)

    spread_order = ((beside, (2,)), (across, (4,)), (corner, (5, 6)))

    def fold(kind, u, value, copies):
        i = slot[kind]
        first, last = slice(0, half), slice(half, rows)
        if u is corner:
            row_send[i, 0] = value.astype(BF16)
            copies[1] = team(kind, 1, row_send.at[i, 0, first], passed.at[i, 0], beside)
            copies[2] = team(kind, 2, row_send.at[i, 0, last], passed.at[i, 1], across)
        elif u is beside:
            row_send[i, 1, first] = value[first].astype(BF16)
            copies[3] = team(kind, 3, row_send.at[i, 1, first], row_got.at[i, 0, first], beside)
            kept[i, 1] = value[last]
        elif u is across:
            row_send[i, 2, last] = value[last].astype(BF16)
            copies[5] = team(kind, 5, row_send.at[i, 2, last], row_got.at[i, 1, last], across)
            kept[i, 0] = value[first]
        else:
            own_part[i] = value

    def fold_on(kind, copies):
        i = slot[kind]
        copies[1].wait_recv()
        row_send[i, 2, 0:half] = (kept[i, 0] + passed[i, 0].astype(F32)).astype(BF16)
        copies[6] = team(kind, 6, row_send.at[i, 2, 0:half], row_got.at[i, 1, 0:half], across)
        copies[2].wait_recv()
        row_send[i, 1, half:rows] = (kept[i, 1] + passed[i, 1].astype(F32)).astype(BF16)
        copies[4] = team(kind, 4, row_send.at[i, 1, half:rows], row_got.at[i, 0, half:rows], beside)

    def folded(kind, copies):
        for k in (3, 5, 6, 4):
            copies[k].wait_recv()
        i = slot[kind]
        return own_part[i] + row_got[i, 0].astype(F32) + row_got[i, 1].astype(F32)

    fold_order = (corner, beside, across, t)

    def share(kind, src, whole):
        return [send(src, whole.at[seat(t)], t_send.at[kind, k], t_recv.at[kind, k], dev(p, mate(k), s))
                for k in range(1, TEAM)]

    weight_in = (attn_in, gate_in, up_in, down_in)
    loads = []
    for i, (src, dst) in enumerate((
        (seg_in, seg_ref), (ids_in, ids_ref), (tok_in, tok_all.at[seat(t)]), (attn_in, w_all.at[ATTN, lot(p, s), :]),
        (gains_in, gains_ref), (router_in, router_ref), (buckets_in, buckets_ref), (dy_in, dy_all.at[seat(t)]),
        (gate_in, w_all.at[GATE, lot(p, s), :]), (up_in, w_all.at[UP, lot(p, s), :]), (down_in, w_all.at[DOWN, lot(p, s), :]),
    )):
        loads.append(pltpu.make_async_copy(src, dst, in_sem.at[i]))
        loads[i].start()
    stores = []

    def store(src, dst):
        stores.append(pltpu.make_async_copy(src, dst, out_sem.at[len(stores)]))
        stores[-1].start()

    loads[0].wait()
    loads[1].wait()
    ids = ids_ref[...].astype(F32)
    line = lax.broadcasted_iota(jnp.int32, (LINES, rows), 0)
    meta_all[pl.ds(pl.multiple_of(t * LINES, LINES), LINES), :] = jnp.where(
        line == 0, seg_ref[...].astype(F32), jnp.where(line == 1, ids[0:1, :], jnp.where(line == 2, ids[1:2, :], 0.0))
    )
    pl.semaphore_wait(barrier, len(peers))

    wide = {}

    inner = (p == 1) | (p == 2)

    def weights_send(kind):
        mine = w_all.at[kind, lot(p, s), :]
        own = weight_in[kind]
        wide[kind] = {k: send(own, mine, z_send.at[kind, k], z_recv.at[kind, k], dev(other(p, k, TEAM), t, s), where)
                      for k, where in ((2, None), (1, p < TEAM - 1), (3, p > 0))}
        wide[kind, "near"] = [send(own, mine, ws_send.at[kind, 0, j], ws_recv.at[kind, 0, j], dev(p, t, other(s, j, sub)))
                              for j in range(1, sub)]

    def weights_arrive(kind, k):
        wide[kind][k].wait_recv()
        block = w_all.at[kind, lot(other(p, TEAM - k, TEAM), s), :]
        if k == 2:
            edge = p // 2
            send(block, block, z_send.at[kind, 0], z_recv.at[kind, 1 + 2 * edge], dev(3 * edge, t, s), inner)
        wide[kind, "near"] += [
            send(block, block, ws_send.at[kind, k, j], ws_recv.at[kind, k, j], dev(p, t, other(s, j, sub)))
            for j in range(1, sub)]

    def weights_forward(kind):
        weights_arrive(kind, 1)
        weights_arrive(kind, 3)

    def weights_wait(kind):
        for c in wide[kind, "near"]:
            c.wait_recv()

    mine_meta = meta_all.at[pl.ds(pl.multiple_of(t * LINES, LINES), LINES), :]
    metas = [send(mine_meta, mine_meta, t_send.at[META, k], t_recv.at[META, k], dev(p, mate(k), s)) for k in range(1, TEAM)]
    toks = share(TOK, tok_in, tok_all)
    weights_send(ATTN)
    weights_send(GATE)
    dys = share(DY, dy_in, dy_all)

    for c in loads[2:]:
        c.wait()
    rhi[...], rlo[...] = split_high(router_ref[...])

    place_r = lax.broadcasted_iota(jnp.int32, (slots, 2 * slots), 0)
    place_c = lax.rem(lax.broadcasted_iota(jnp.int32, (slots, 2 * slots), 1), slots)
    gap = place_r - place_c
    offs[...] = jnp.zeros(offs.shape, F32)

    def spread_bias(d, carry):
        hit = gap == d
        for h in range(heads):
            offs[h] = jnp.where(hit, table_ref[heads * t + h, bucket_ref[d]], offs[h])
        return carry

    lax.fori_loop(0, slots, spread_bias, 0)

    row_i = lax.broadcasted_iota(jnp.int32, (rows, rows), 0)
    col_i = lax.broadcasted_iota(jnp.int32, (rows, rows), 1)
    causal = (row_i >= col_i) & ((row_i // slots) == (col_i // slots))
    lane_head = lax.broadcasted_iota(jnp.int32, (rows, part), 1) // head_width
    gain_one, gain_two = gains_ref[0:1, :], gains_ref[1:2, :]
    zero_low = jnp.zeros((rows, part), BF16)

    def meta_of(u):
        lines = meta_all[pl.ds(pl.multiple_of(u * LINES, LINES), LINES), :]
        return lines, dot_t(eye(rows, F32), lines)

    def unit_of(u):
        x = tok_all[seat(u), :].astype(F32)
        return x * lax.rsqrt(jnp.mean(x * x, axis=-1, keepdims=True) + EPSILON)

    def attend(u):
        rows_u = seat(u)
        h1 = (unit_of(u) * gain_one).astype(BF16)
        normed[rows_u, :] = h1
        q = dot_t(h1, w_all[ATTN, 0:part, :]).astype(BF16)
        key = dot_t(h1, w_all[ATTN, part:2 * part, :]).astype(BF16)
        v = dot_t(h1, w_all[ATTN, 2 * part:3 * part, :]).astype(BF16)
        q_all[rows_u, :], k_all[rows_u, :], v_all[rows_u, :] = q, key, v
        lines, cols = meta_of(u)
        allowed = (cols[:, 0:1] == lines[0:1, :]) & causal
        mix = jnp.zeros((rows, part), F32)
        for h in range(heads):
            raw = dot_t(jnp.where(lane_head == h, q, zero_low), key)
            scores = jnp.where(allowed, raw * factor + jnp.concatenate([offs[h], offs[h]], axis=0), -1e30)
            lifted = jnp.exp(scores - jnp.max(scores, axis=-1, keepdims=True))
            weights = lifted / jnp.sum(lifted, axis=-1, keepdims=True)
            probs_all[h, rows_u, :] = weights
            mix = jnp.where(lane_head == h, dot(weights.astype(BF16), v), mix)
        low = mix.astype(BF16)
        mixed[rows_u, :] = low
        return dot(low, w_all[ATTN, 3 * part:4 * part, :])


    def scatter(kind, k, value, u):
        i = slot[kind]
        if k == 0:
            own_part[i] = value
            return []
        row_send[i, k - 1] = value.astype(BF16)
        return [send(row_send.at[i, k - 1], row_got.at[i, k - 1], t_send.at[kind, k], t_recv.at[kind, k],
                     dev(p, u, s))]

    def gathered(kind, copies):
        total = own_part[slot[kind]]
        for c in copies:
            c.wait_recv()
        for k in range(1, TEAM):
            total = total + row_got[slot[kind], k - 1].astype(F32)
        return total

    weights_arrive(ATTN, 2)
    weights_forward(ATTN)
    weights_send(UP)
    weights_wait(ATTN)
    for c in metas + toks:
        c.wait_recv()
    branch = {}
    for u in fold_order:
        fold(BRANCH, u, attend(u), branch)
    fold_on(BRANCH, branch)
    weights_arrive(GATE, 2)
    weights_send(DOWN)

    middle = tok_all[seat(t), :].astype(F32) + folded(BRANCH, branch)
    middle_s[...] = middle
    scale = lax.rsqrt(jnp.mean(middle * middle, axis=-1, keepdims=True) + EPSILON)
    h_all[seat(t), :] = (middle * scale * gain_two).astype(BF16)
    seconds = spread(SECOND, h_all)

    lane_expert = lax.broadcasted_iota(jnp.int32, (rows, routed), 1).astype(F32)

    def route(u):
        h2 = h_all[seat(u), :]
        logits = dot_t(h2, rhi[...]) + dot_t(h2, rlo[...])
        lifted = jnp.exp(logits - jnp.max(logits, axis=-1, keepdims=True))
        probs = lifted / jnp.sum(lifted, axis=-1, keepdims=True)
        _, cols = meta_of(u)
        picked = jnp.where((cols[:, 1:2] == lane_expert) | (cols[:, 2:3] == lane_expert), 1.0, 0.0)
        chosen = jnp.sum(probs * picked, axis=-1, keepdims=True)
        live = picked[:, 0:1] * jnp.where(cols[:, 0:1] >= 0.0, 1.0, 0.0)
        combine = probs[:, 0:1] * live / chosen
        dexp_all[seat(u), :] = (combine * dy_all[seat(u), :].astype(F32)).astype(BF16)
        return probs, picked, chosen, live, combine

    eprobs_s[...] = route(t)[0]
    spread_on(SECOND, h_all, seconds)
    weights_forward(GATE)
    weights_arrive(UP, 2)
    for c in dys:
        c.wait_recv()
    for u, parts in spread_order:
        for i in parts:
            seconds[i].wait_recv()
        route(u)

    weights_forward(UP)
    weights_wait(GATE)
    weights_wait(UP)
    k0 = (2.0 / math.pi) ** 0.5
    k1 = 0.044715
    step = 32
    for c in range(width // chunk):
        cols = slice(c * chunk, (c + 1) * chunk)
        gs[...] = dot_t(h_all[...], w_all[GATE, cols, :])
        us[...] = dot_t(h_all[...], w_all[UP, cols, :])

        def lift(r, carry):
            rr = pl.ds(pl.multiple_of(r * step, step), step)
            g, u = gs[rr, :], us[rr, :]
            square = g * g
            bend = jnp.tanh(k0 * g * (1.0 + k1 * square))
            half = 0.5 * (1.0 + bend)
            act = g * half
            slope = half + 0.5 * g * (1.0 - bend * bend) * (k0 * (1.0 + 3.0 * k1 * square))
            hidden[rr, cols] = (act * u).astype(BF16)
            ge_s[rr, cols] = act
            dgu_s[rr, cols] = slope * u
            return carry

        lax.fori_loop(0, TEAM * rows // step, lift, 0)

    near = {}

    def grad_near(kind, q):
        near[kind, q] = [
            send(g_part.at[kind, lot(q, other(s, j, sub)), :], sib.at[kind, j - 1, q], gs_send.at[kind, q, j],
                 gs_recv.at[kind, q, j], dev(p, t, other(s, j, sub)))
            for j in range(1, sub)]

    def grad_of(kind, q):
        total = g_part[kind, lot(q, s), :].astype(F32)
        for j in range(1, sub):
            total = total + sib[kind, j - 1, q].astype(F32)
        return total

    def to_owner(kind, q, where):
        send(to_send.at[kind, q], far.at[kind, p], gp_send.at[kind, q], gp_recv.at[kind, p], dev(q, t, s), where)

    def hop_of(kind, q):
        return remote(to_send.at[kind, q], hop.at[kind], hp_send.at[kind], hp_recv.at[kind], dev(2 - q // 2, t, s))

    def grad_push(kind, q):
        for c in near[kind, q]:
            c.wait_recv()

        @pl.when(p != q)
        def _():
            to_send[kind, q] = grad_of(kind, q).astype(BF16)

        if q in (0, 3) and kind != ATTN:
            next_to, end = (1, 3) if q == 0 else (2, 0)
            c = hop_of(kind, q)
            pl.when(p == end)(c.start)
            pending.append((p == end, c))
            to_owner(kind, q, p == next_to)
        else:
            to_owner(kind, q, p != q)

    def grad_relay(kind, q):
        through = 2 if q == 0 else 1

        @pl.when(p == through)
        def _():
            hop_of(kind, q).wait_recv()
            to_send[kind, q] = (grad_of(kind, q) + hop[kind].astype(F32)).astype(BF16)

        to_owner(kind, q, p == through)

    def grad_relays(kind):
        grad_relay(kind, 0)
        grad_relay(kind, 3)

    def grad_all_near(kind):
        for q in range(TEAM):
            grad_near(kind, q)

    def grad_wide(kind):
        for q in (0, 3, 1, 2):
            grad_push(kind, q)

    def grad_end(kind):
        g_ref[kind] = grad_of(kind, p)
        for q in range(TEAM):
            @pl.when((p != q) & (p + q != 3 if q in (0, 3) and kind != ATTN else p != q))
            def _():
                remote(to_send.at[kind, q], far.at[kind, q], gp_send.at[kind, q], gp_recv.at[kind, q], dev(q, t, s)).wait_recv()
                g_ref[kind] += far[kind, q].astype(F32)

        store(g_ref.at[kind], (attn_out, gate_out, up_out, down_out)[kind])

    weights_arrive(DOWN, 2)
    g_part[DOWN] = dot_r(hidden[...], dexp_all[...]).astype(BF16)
    grad_all_near(DOWN)
    grad_wide(DOWN)
    weights_forward(DOWN)
    weights_wait(DOWN)
    mark_down = len(pending)
    outs = {}
    for u in fold_order:
        fold(OUT, u, dot(hidden[seat(u), :], w_all[DOWN]), outs)
    for c in range(width // chunk):
        cols = slice(c * chunk, (c + 1) * chunk)
        gs[...] = dot_t(dexp_all[...], w_all[DOWN, cols, :])

        def lower(r, carry):
            rr = pl.ds(pl.multiple_of(r * step, step), step)
            da = gs[rr, :]
            dg_s[rr, cols] = (da * dgu_s[rr, cols]).astype(BF16)
            du_s[rr, cols] = (da * ge_s[rr, cols]).astype(BF16)
            return carry

        lax.fori_loop(0, TEAM * rows // step, lower, 0)
    backs = {}
    for u in fold_order:
        fold(BACK, u, dot(dg_s[seat(u), :], w_all[GATE]) + dot(du_s[seat(u), :], w_all[UP]), backs)
    g_part[GATE] = dot_r(dg_s[...], h_all[...]).astype(BF16)
    grad_all_near(GATE)
    fold_on(OUT, outs)
    g_part[UP] = dot_r(du_s[...], h_all[...]).astype(BF16)
    grad_all_near(UP)
    grad_wide(GATE)
    grad_wide(UP)
    grad_relays(DOWN)
    fold_on(BACK, backs)

    upstream = dy_all[seat(t), :].astype(F32)
    probs = eprobs_s[...]
    _, cols = meta_of(t)
    picked = jnp.where((cols[:, 1:2] == lane_expert) | (cols[:, 2:3] == lane_expert), 1.0, 0.0)
    chosen = jnp.sum(probs * picked, axis=-1, keepdims=True)
    live = picked[:, 0:1] * jnp.where(cols[:, 0:1] >= 0.0, 1.0, 0.0)
    combine = probs[:, 0:1] * live / chosen
    mark_out = len(pending)
    expert = folded(OUT, outs)
    result_ref[...] = (middle_s[...] + combine * expert).astype(BF16)
    store(result_ref, result_out)
    d_combine = jnp.sum(expert * upstream, axis=-1, keepdims=True)
    first_hot = jnp.where(lane_expert == 0.0, 1.0, 0.0)
    ratio = probs[:, 0:1] / (chosen * chosen)
    d_probs = (d_combine * live) * (first_hot / chosen - ratio * picked)
    d_logits = probs * (d_probs - jnp.sum(d_probs * probs, axis=-1, keepdims=True))
    l_hi, l_lo = split_high(d_logits)
    l_lowest = (d_logits - l_hi.astype(F32) - l_lo.astype(F32)).astype(BF16)
    d_route = dot(l_hi, rhi[...]) + dot(l_hi, rlo[...]) + dot(l_lo, rhi[...])
    depth = sbuf.shape[0] // (TEAM * sub)
    h2 = h_all[seat(t), :]
    sbuf[...] = dot_r(l_hi, h2) + dot_r(l_lo, h2) + dot_r(l_lowest, h2)

    def piece(a, b):
        return pl.ds(pl.multiple_of((other(t, a, TEAM) * sub + other(s, b, sub)) * depth, depth), depth)

    first = [send(sbuf.at[piece(a, b), :], s_got.at[i], sa_send.at[i], sa_recv.at[i], plane[i]) for i, (a, b) in enumerate(ring)]
    drain(mark_down)
    grad_relays(GATE)
    d_second = folded(BACK, backs) + d_route
    middle = middle_s[...]
    scale = lax.rsqrt(jnp.mean(middle * middle, axis=-1, keepdims=True) + EPSILON)
    d_middle = upstream + norm_back(middle, scale, gain_two, d_second)
    dmid_s[...] = d_middle
    db_all[seat(t), :] = d_middle.astype(BF16)
    dbs = spread(DBRANCH, db_all)
    gain_two_sum = jnp.sum(d_second * middle * scale, axis=0, keepdims=True)
    score_s[...] = jnp.zeros(score_s.shape, F32)

    def attend_back(u):
        rows_u = seat(u)
        d_mix = dot_t(db_all[rows_u, :], w_all[ATTN, 3 * part:4 * part, :]).astype(BF16)
        q, key, v = q_all[rows_u, :], k_all[rows_u, :], v_all[rows_u, :]
        dq = jnp.zeros((rows, part), F32)
        dk = jnp.zeros((rows, part), F32)
        dv = jnp.zeros((rows, part), F32)
        for h in range(heads):
            weights = probs_all[h, rows_u, :]
            d_w = dot_t(jnp.where(lane_head == h, d_mix, zero_low), v)
            ds = (weights * (d_w - jnp.sum(weights * d_w, axis=-1, keepdims=True))).astype(BF16)
            dv = jnp.where(lane_head == h, dot_r(weights.astype(BF16), d_mix), dv)
            dq = jnp.where(lane_head == h, dot(ds, key), dq)
            dk = jnp.where(lane_head == h, dot_r(ds, q), dk)
            wide_ds = ds.astype(F32)
            score_s[h] = score_s[h] + wide_ds[:slots] + wide_ds[slots:]
        dq_all[rows_u, :] = (dq * factor).astype(BF16)
        dk_all[rows_u, :] = (dk * factor).astype(BF16)
        dv_all[rows_u, :] = dv.astype(BF16)

    norms = []
    gain_sum = jnp.zeros((1, width), F32)

    def norm_rows(k, u):
        rows_u = seat(u)
        value = (dot(dq_all[rows_u, :], w_all[ATTN, 0:part, :]) + dot(dk_all[rows_u, :], w_all[ATTN, part:2 * part, :])
                 + dot(dv_all[rows_u, :], w_all[ATTN, 2 * part:3 * part, :]))
        norms.extend(scatter(DNORM, k, value, u))
        return jnp.sum(value * unit_of(u), axis=0, keepdims=True)

    attend_back(t)
    gain_sum = gain_sum + norm_rows(0, t)
    spread_on(DBRANCH, db_all, dbs)
    total = sbuf[piece(0, 0), :]
    for i, c in enumerate(first):
        c.wait_recv()
        total = total + s_got[i]
    s_held[...] = total
    s_far[p] = total
    second = [send(s_held, s_far.at[p], sc_send.at[k], sc_recv.at[k], dev(other(p, k, TEAM), t, s)) for k in range(1, TEAM)]
    grad_relays(UP)
    drain(mark_out)
    for slot_u, (u, parts) in enumerate(spread_order):
        for i in parts:
            dbs[i].wait_recv()
        attend_back(u)
        gain_sum = gain_sum + norm_rows(slot_u + 1, u)

    for q, left, right in ((3, mixed, db_all), (0, dq_all, normed), (2, dv_all, normed), (1, dk_all, normed)):
        g_part[ATTN, q * part:(q + 1) * part, :] = dot_r(left[...], right[...]).astype(BF16)
        grad_near(ATTN, q)
    for q in (3, 0, 2, 1):
        grad_push(ATTN, q)
    for c in second:
        c.wait_recv()
    total = s_far[0]
    for k in range(1, TEAM):
        total = total + s_far[k]
    small_ref[piece(0, 0), :] = total
    mine_small = small_ref.at[piece(0, 0), :]
    third = [send(mine_small, mine_small, sd_send.at[i], sd_recv.at[i], plane[i]) for i in range(len(plane))]
    def gather_gap(d, carry):
        hit = gap == d
        for h in range(heads):
            gap_s[h, pl.ds(d, 1), :] = jnp.sum(jnp.where(hit, score_s[h], 0.0), axis=0, keepdims=True)
        return carry

    lax.fori_loop(0, slots, gather_gap, 0)
    lane = lax.broadcasted_iota(jnp.int32, (slots, 128), 1)
    by_gap = jnp.zeros((slots, 128), F32)
    for h in range(heads):
        by_gap = jnp.where(lane == heads * t + h, jnp.sum(gap_s[h], axis=-1, keepdims=True), by_gap)
    count = table_ref.shape[1]
    bucket_hit = jnp.where(lax.broadcasted_iota(jnp.int32, (count, slots), 0) == buckets_ref[...], 1.0, 0.0)
    l_own[0:count, :] = jnp.dot(bucket_hit, by_gap, precision=HIGHEST, preferred_element_type=F32)
    for i in range(width // 128):
        l_own[count + i:count + i + 1, :] = gain_sum[:, i * 128:(i + 1) * 128]
        j = count + width // 128 + i
        l_own[j:j + 1, :] = gain_two_sum[:, i * 128:(i + 1) * 128]
    used = count + 2 * (width // 128)
    l_own[used:, :] = jnp.zeros((l_own.shape[0] - used, 128), F32)
    late_a = [send(l_own, l_got.at[k - 1], la_send.at[k], la_recv.at[k], dev(p, mate(k), s)) for k in range(1, TEAM)]

    grad_end(DOWN)
    for c in late_a:
        c.wait_recv()
    total = l_own[...]
    for k in range(1, TEAM):
        total = total + l_got[k - 1]
    l_sum[...] = total
    l_sib[s] = total
    late_b = [send(l_sum, l_sib.at[s], lb_send.at[j], lb_recv.at[j], dev(p, t, other(s, j, sub))) for j in range(1, sub)]
    grad_end(GATE)
    for c in late_b:
        c.wait_recv()
    total = l_sib[0]
    for j in range(1, sub):
        total = total + l_sib[j]
    l_tot[...] = total
    l_far[p] = total
    late_c = [send(l_tot, l_far.at[p], lc_send.at[k], lc_recv.at[k], dev(other(p, k, TEAM), t, s)) for k in range(1, TEAM)]
    grad_end(UP)

    x = tok_all[seat(t), :].astype(F32)
    d_normed = gathered(DNORM, norms)
    scale = lax.rsqrt(jnp.mean(x * x, axis=-1, keepdims=True) + EPSILON)
    dtok_ref[...] = (dmid_s[...] + norm_back(x, scale, gain_one, d_normed)).astype(BF16)
    store(dtok_ref, dtok_out)

    for c in late_c:
        c.wait_recv()
    total = l_far[0]
    for k in range(1, TEAM):
        total = total + l_far[k]
    table_s[...] = total[0:count, :].T[0:table_s.shape[0], :]
    store(table_s, table_out)
    parts = width // 128
    for i in range(2 * parts):
        gains_s[i // parts:i // parts + 1, (i % parts) * 128:(i % parts + 1) * 128] = total[count + i:count + i + 1, :]
    store(gains_s, gains_out)
    for c in third:
        c.wait_recv()
    store(small_ref, router_out)
    drain(len(pending))
    grad_end(ATTN)
    for c in stores:
        c.wait()


def finish_kernel(count, *refs):
    held, into, away = refs[2 * count:3 * count], refs[3 * count], refs[3 * count + 1]
    loads = [pltpu.make_async_copy(refs[i], held[i], into.at[i]) for i in range(count)]
    stores = [pltpu.make_async_copy(held[i], refs[count + i], away.at[i]) for i in range(count)]
    for c in loads:
        c.start()
    for load, keep in zip(loads, stores):
        load.wait()
        keep.start()
    for c in stores:
        c.wait()


def block(n, tokens, attn_weight, w_gate, w_up, w_down, norm_gains, bias_table, router,
          grad_out, segment, expert_ids, bucket_of):
    rows, width = tokens.shape
    shard = w_down.shape[0]
    sub = n // (TEAM * TEAM)
    head_count = bias_table.shape[1]
    heads = head_count // TEAM
    part = heads * (width // head_count)
    slots = bucket_of.shape[0]
    routed = router.shape[1]
    every = TEAM * rows
    dma = pltpu.SemaphoreType.DMA
    shape = jax.ShapeDtypeStruct
    buf = pltpu.VMEM
    depth = routed // (TEAM * sub)
    lines = -(-(bias_table.shape[0] + 2 * (width // 128)) // 8) * 8
    smem = pl.BlockSpec(memory_space=pltpu.SMEM)
    grad = shape((shard, width), F32)
    shapes = (shape(tokens.shape, BF16), shape(tokens.shape, BF16), grad, grad, grad, grad, shape(norm_gains.shape, F32),
              shape(bias_table.shape[::-1], F32), shape(router.shape[::-1], F32))
    outs = pl.pallas_call(
        functools.partial(block_kernel, n, head_count),
        out_shape=shapes,
        in_specs=[HBM] * 11 + [smem] * 2,
        out_specs=(HBM,) * len(shapes),
        scratch_shapes=[
            buf((1, rows), jnp.int32), buf((2, rows), jnp.int32), buf(norm_gains.shape, F32), buf((routed, width), F32),
            buf((1, slots), jnp.int32), buf((rows, width), BF16), buf((rows, width), BF16), buf((4, shard, width), F32),
            buf((routed, width), F32), buf(norm_gains.shape, F32), buf(bias_table.shape[::-1], F32), dma((11,)), dma((9,)),
            buf((4, width, width), BF16), buf((4, width, width), BF16), buf((4, sub - 1, TEAM, shard, width), BF16),
            buf((4, TEAM, shard, width), BF16), buf((4, TEAM, shard, width), BF16), buf((4, shard, width), BF16),
            buf((every, width), BF16), buf((every, width), BF16), buf((TEAM * LINES, rows), F32), buf((every, width), BF16),
            buf((every, part), BF16), buf((every, part), BF16), buf((every, part), BF16), buf((every, part), BF16),
            buf((heads, every, rows), F32), buf((heads, slots, 2 * slots), F32),
            buf((4, TEAM - 1, rows, width), BF16), buf((4, TEAM - 1, rows, width), BF16), buf((3, 2, rows // 2, width), BF16),
            buf((3, 2, rows // 2, width), F32), buf((4, rows, width), F32),
            buf((rows, width), F32), buf((every, width), BF16), buf((every, width), BF16), buf((rows, 128), F32),
            buf((rows, routed), F32), buf((routed, width), BF16), buf((routed, width), BF16),
            buf((every, 256), F32), buf((every, 256), F32), buf((every, width), BF16), buf((every, width), F32),
            buf((every, width), F32), buf((every, width), BF16), buf((every, width), BF16), buf((rows, width), F32),
            buf((every, width), BF16), buf((every, part), BF16), buf((every, part), BF16), buf((every, part), BF16),
            buf((heads, slots, 2 * slots), F32), buf((heads, slots, 2 * slots), F32),
            buf((routed, width), F32), buf((TEAM * sub - 1, depth, width), F32),
            buf((depth, width), F32), buf((TEAM, depth, width), F32),
            buf((lines, 128), F32), buf((TEAM - 1, lines, 128), F32), buf((lines, 128), F32),
            buf((sub, lines, 128), F32), buf((lines, 128), F32), buf((TEAM, lines, 128), F32),
            dma((9, 8)), dma((9, 8)), dma((4, TEAM)), dma((4, TEAM)), dma((4, TEAM, sub)), dma((4, TEAM, sub)),
            dma((4, TEAM, sub)), dma((4, TEAM, sub)), dma((4, TEAM)), dma((4, TEAM)), dma((4,)), dma((4,)),
            dma((TEAM * sub,)), dma((TEAM * sub,)), dma((TEAM,)), dma((TEAM,)), dma((TEAM * sub,)), dma((TEAM * sub,)),
            dma((TEAM,)), dma((TEAM,)), dma((sub,)), dma((sub,)), dma((TEAM,)), dma((TEAM,)),
        ],
        compiler_params=pltpu.CompilerParams(collective_id=0, has_side_effects=True, vmem_limit_bytes=56 * 2**20),
        name="block",
    )(attn_weight.T, w_gate.T, w_up.T, w_down, tokens, grad_out, segment.reshape(1, rows), expert_ids.T, norm_gains,
      router.T, bucket_of.reshape(1, slots), bias_table.T, bucket_of)
    result, dtok, g_attn, g_gate, g_up, g_down, gains, table, routes = pl.pallas_call(
        functools.partial(finish_kernel, len(shapes)),
        out_shape=shapes,
        in_specs=[HBM] * len(shapes),
        out_specs=(HBM,) * len(shapes),
        scratch_shapes=[buf(v.shape, v.dtype) for v in shapes] + [dma((len(shapes),)), dma((len(shapes),))],
        name="finish",
    )(*outs)
    return result, dtok, g_attn.T, g_gate.T, g_up.T, g_down, gains, table.T, routes.T


def solution(mesh):
    n = mesh.shape["fsdp"]
    row, col = P("fsdp", None), P(None, "fsdp")
    in_specs = (row, col, col, col, row, P(), P(), P(), row, P("fsdp"), row, P())
    out_specs = (row, row, col, col, col, row, P(), P(), P())

    def run(*args):
        shard, rows = args[4].shape[0] // n, args[0].shape[0] // n
        whole_tiles = shard % 16 == 0 and rows == 2 * args[11].shape[0] and args[7].shape[1] % (n // 2) == 0
        return jax.shard_map(
            functools.partial(block if whole_tiles else body, n),
            mesh=mesh, in_specs=in_specs, out_specs=out_specs, check_vma=False,
        )(*args)

    return run
```
